32 devices in a mesh: dp: 4 (over y, core), store: 8 (over z, x).
Axes of the slice: x: 2, y: 2, z: 4, core: 2. Of those that a mesh axis runs over, the one named last changes fastest.
Arguments:
- tokens: bfloat16 [16384, 768], P(('dp', 'store')), may hold values from -6 to 6
- datastore: bfloat16 [32768, 768], P('store'), may hold values from -6 to 6
- indices: int32 [16384, 16], P(('dp', 'store')), may hold values from 0 to 32767, as said below
- lengths: int32 [32], P(('dp', 'store')), may hold values from 64 to 512, as said below
- proj_weight: bfloat16 [768, 6, 768], replicated, may hold values from -0.21875 to 0.21875
- out_weight: bfloat16 [768, 2, 768], replicated, may hold values from -0.875 to 0.875
- proj_bias: float32 [768, 6], replicated, may hold values from -2 to 2
- norm_gain: float32 [768, 3], replicated, may hold values from 0.5 to 1.5
- norm_bias: float32 [768, 3], replicated, may hold values from -2 to 2
- inner_weight: bfloat16 [768, 3072], replicated, may hold values from -0.21875 to 0.21875
- inner_bias: float32 [3072], replicated, may hold values from -2 to 2
- outer_weight: bfloat16 [3072, 768], replicated, may hold values from -0.109375 to 0.109375
- outer_bias: float32 [768], replicated, may hold values from -2 to 2
- cotangent: bfloat16 [16384, 768], P(('dp', 'store')), may hold values from -6 to 6
Outputs:
- output: bfloat16 [16384, 768], P(('dp', 'store'))
- grad_tokens: bfloat16 [16384, 768], P(('dp', 'store'))
- grad_datastore: float32 [32768, 768], P('store')
- grad_proj_weight: float32 [768, 6, 768], P('store')
- grad_out_weight: float32 [768, 2, 768], P('store')
- grad_proj_bias: float32 [768, 6], P('store')
- grad_norm_gain: float32 [768, 3], P('store')
- grad_norm_bias: float32 [768, 3], P('store')
- grad_inner_weight: float32 [768, 3072], P('store')
- grad_inner_bias: float32 [3072], P('store')
- grad_outer_weight: float32 [3072, 768], P('store')
- grad_outer_bias: float32 [768], P('store')
The draws below stay inside these ranges and needn't reach their ends.
Inputs may be any that keep to these rules, and one draw needn't show every extreme that they name: `indices`: row numbers of the datastore. Of the 8192 numbers of one sequence, at most 2048 lie in the rows of one store device (o * 4096 to (o + 1) * 4096 - 1), and exactly 2048 lie in those of some device. `lengths`: each is at least 64; some sequence has 512.
All inputs are finite; a program needn't handle non-finite values.
Results may differ from the reference program's by a relative error of at most 0.025.
Values may be sent and summed in bfloat16 or wider, within the bound.
A program may use at most 320 MiB of HBM per device.

```python
import jax
import jax.numpy as jnp
from jax import lax

D = 768
H = 12
HD = 64
FF = 3072
TOK_DEV = 512
K = 16
ROWS_DEV = 4096
LEN_MIN = 64
SEQS = 32
TOKENS = 16384
ROWS = 32768
CAP = 2048
N_STORE = 8


def draw_indices(key, part):
    slot_count = TOK_DEV * K

    def one_block(block_key):
        key_extra, key_owner, key_shuffle, key_offset = jax.random.split(block_key, 4)
        shifted = jnp.arange(slot_count, dtype=jnp.int32) - CAP
        extra = jax.random.randint(key_extra, (slot_count,), 0, 2)
        ranked = jnp.where(shifted < 0, 0, 1 + (jnp.maximum(shifted, 0) + extra) % (N_STORE - 1))
        owner_table = jax.random.permutation(key_owner, N_STORE).astype(jnp.int32)
        owner_of = owner_table[ranked]
        shuffled = jax.random.permutation(key_shuffle, owner_of)
        offset = jax.random.randint(key_offset, (slot_count,), 0, ROWS_DEV)
        return (shuffled * ROWS_DEV + offset).reshape(TOK_DEV, K)
    block_keys = jax.random.split(jax.random.fold_in(key, 11), SEQS)
    return jax.vmap(one_block)(block_keys).reshape(SEQS * TOK_DEV, K).astype(jnp.int32)


def draw_lengths(key, part):
    key_base, key_full = jax.random.split(jax.random.fold_in(key, 23))
    base = jax.random.randint(key_base, (SEQS,), LEN_MIN, TOK_DEV + 1)
    longest = jax.random.randint(key_full, (), 0, SEQS)
    return jnp.where(jnp.arange(SEQS) == longest, TOK_DEV, base).astype(jnp.int32)


def with_spikes(values, own_key, source, target, parts, factor):
    owner, partner = [(jnp.arange(values.shape[dim]) // (values.shape[dim] // parts)).reshape([-1 if axis == dim else 1 for axis in range(values.ndim)]) for dim in (source, target)]
    chosen = jax.random.permutation(own_key, parts)[partner]
    strong = (owner == chosen) | (owner == (partner + parts // 2) % parts)
    return jnp.where(strong, factor * values, values)


def block_levels(own_key, shape, cuts, low, high):
    loudness = 1.0
    for dim, shards_of in cuts:
        heights = jax.random.uniform(jax.random.fold_in(jax.random.fold_in(own_key, 6), dim), (shards_of,), jnp.float32, low / len(cuts), high / len(cuts))
        loudness = loudness * jnp.repeat(jnp.exp(heights), shape[dim] // shards_of).reshape((-1,) + (1,) * (len(shape) - 1 - dim))
    return loudness


def noise(stream_key, shape, spread, bound, shards=(), kind=jnp.bfloat16):
    values = jax.random.normal(stream_key, shape, jnp.float32) * spread
    if len(shards) > 0:
        values = block_levels(stream_key, shape, shards, -0.22, 0.18) * values
    return jnp.clip(values, min=-bound, max=bound).astype(kind)


def noise_with(own_key, shape, scale, most, cuts, heavy, held_as=jnp.bfloat16):
    entries = scale * jax.random.normal(own_key, shape, jnp.float32)
    if cuts:
        entries = entries * block_levels(own_key, shape, cuts, -0.22, 0.18)
    return jnp.clip(with_spikes(entries, jax.random.fold_in(own_key, 3), *heavy), -most, most).astype(held_as)


def setup_inputs(seed: int = 0) -> dict:
    key_list = jax.random.split(jax.random.key(seed), 15)
    tokens = noise(key_list[0], (TOKENS, D), 1.0, 6.0, ((0, 32),))
    datastore = noise(key_list[1], (ROWS, D), 1.0, 6.0, ((0, 8),))
    indices = draw_indices(jax.random.fold_in(key_list[14], 71), 0)
    lengths = draw_lengths(jax.random.fold_in(key_list[14], 71), 0)
    proj_weight = noise(key_list[4], (D, 6, D), D ** -0.5, 0.21875)
    out_weight = noise(key_list[5], (D, 2, D), (D // 16) ** -0.5, 0.875)
    proj_bias = noise(key_list[6], (D, 6), 0.3, 2.0, (), jnp.float32)
    norm_gain = jnp.clip(1.0 + 0.1 * jax.random.normal(key_list[7], (D, 3), jnp.float32), 0.5, 1.5)
    norm_bias = noise(key_list[8], (D, 3), 0.3, 2.0, (), jnp.float32)
    inner_weight = noise(key_list[9], (D, FF), D ** -0.5, 0.21875)
    inner_bias = noise(key_list[10], (FF,), 0.3, 2.0, (), jnp.float32)
    outer_weight = noise(key_list[11], (FF, D), FF ** -0.5, 0.109375)
    outer_bias = noise(key_list[12], (D,), 0.3, 2.0, (), jnp.float32)
    cotangent = noise_with(key_list[13], (TOKENS, D), 1.0, 6.0, ((0, 32),), (0, 1, 32, 2.75))
    return {"tokens": tokens, "datastore": datastore, "indices": indices, "lengths": lengths, "proj_weight": proj_weight, "out_weight": out_weight, "proj_bias": proj_bias, "norm_gain": norm_gain, "norm_bias": norm_bias, "inner_weight": inner_weight, "inner_bias": inner_bias, "outer_weight": outer_weight, "outer_bias": outer_bias, "cotangent": cotangent}


EPSILON = 1e-05
HIGHEST_PRECISION = lax.Precision.HIGHEST

@jax.custom_vjp
def low(v):
    return lax.optimization_barrier(v.astype(jnp.bfloat16)).astype(jnp.float32)

@jax.custom_vjp
def low_back(v):
    return v

def low_keep(v):
    return (low(v), None)

def low_pass(kept, grad):
    return (grad,)

def back_keep(v):
    return (v, None)

def back_low(kept, grad):
    return (low(grad),)
low.defvjp(low_keep, low_pass)
low_back.defvjp(back_keep, back_low)

def matmul_high(matrix, factor):
    return jnp.dot(matrix, factor, precision=HIGHEST_PRECISION, preferred_element_type=jnp.float32)

def einsum_high(pattern, matrix, factor):
    return jnp.einsum(pattern, matrix, factor, precision=HIGHEST_PRECISION)

def layer_norm(hidden, norm_weight, norm_shift):
    centered = hidden - lax.optimization_barrier(jnp.mean(hidden, axis=-1, keepdims=True))
    variance = lax.optimization_barrier(jnp.mean(centered * centered, axis=-1, keepdims=True))
    return centered * lax.rsqrt(variance + EPSILON) * norm_weight + norm_shift

def one_sequence(params, datastore, one_piece):
    proj_weight, out_weight, proj_bias, norm_gain, norm_bias, inner_weight, inner_bias, outer_weight, outer_bias = params
    seq_tokens, picked, length = one_piece
    seq_len = seq_tokens.shape[0]
    score_scale = HD ** (-0.5)
    position = jnp.arange(seq_len)
    allowed = (position[None, :] <= position[:, None]) & (position[None, :] < length)
    zero_bias = jnp.zeros((D,), jnp.float32)
    joined_bias = jnp.concatenate([proj_bias[:, 0], zero_bias, proj_bias[:, 1]])
    joined = low_back(low(matmul_high(seq_tokens, proj_weight[:, 0:3, :].reshape(D, 3 * D)) + joined_bias))
    queries = joined[:, :D].reshape(seq_len, H, HD)
    self_keys = joined[:, D:2 * D].reshape(seq_len, H, HD)
    values = joined[:, 2 * D:].reshape(seq_len, H, HD)
    scores = low_back(einsum_high('qhe,khe->hqk', queries, self_keys) * score_scale)
    scores = jnp.where(allowed[None], scores, -1e+30)
    self_probs = low(jax.nn.softmax(scores, axis=-1))
    self_mixed = low_back(low(einsum_high('hqk,khe->qhe', self_probs, values).reshape(seq_len, D)))
    branch = low_back(matmul_high(self_mixed, out_weight[:, 0, :]) + proj_bias[:, 2])
    first_out = layer_norm(seq_tokens + branch, norm_gain[:, 0], norm_bias[:, 0])
    cross_query = low_back(low(matmul_high(low(first_out), proj_weight[:, 3, :]) + proj_bias[:, 3])).reshape(seq_len, H, HD)
    folded = low_back(low(einsum_high('the,dhe->thd', cross_query, proj_weight[:, 4, :].reshape(D, H, HD)) * score_scale))
    fetched = low_back(datastore[picked])
    cross_scores = low_back(einsum_high('thd,tkd->thk', folded, fetched))
    cross_probs = low(jax.nn.softmax(cross_scores, axis=-1))
    summary = low_back(low(einsum_high('thk,tkd->thd', cross_probs, fetched)))
    cross_mixed = low_back(low(einsum_high('thd,dhe->the', summary, proj_weight[:, 5, :].reshape(D, H, HD)).reshape(seq_len, D) + proj_bias[:, 4]))
    cross_branch = low_back(matmul_high(cross_mixed, out_weight[:, 1, :]) + proj_bias[:, 5])
    second = layer_norm(first_out + cross_branch, norm_gain[:, 1], norm_bias[:, 1])
    inner_pre = low_back(matmul_high(low(second), inner_weight) + inner_bias)
    activated = low(jax.nn.gelu(inner_pre, approximate=False))
    outer_out = low_back(matmul_high(activated, outer_weight) + outer_bias)
    third_out = layer_norm(second + outer_out, norm_gain[:, 2], norm_bias[:, 2])
    return jnp.where((position < length)[:, None], third_out, 0.0)

def reference(tokens, datastore, indices, lengths, proj_weight, out_weight, proj_bias, norm_gain, norm_bias, inner_weight, inner_bias, outer_weight, outer_bias, cotangent):
    params = tuple((member.astype(jnp.float32) for member in (proj_weight, out_weight, proj_bias, norm_gain, norm_bias, inner_weight, inner_bias, outer_weight, outer_bias)))
    seq_count = lengths.shape[0]

    def forward(weights, tokens_float, store_float):
        pieces = (tokens_float.reshape(seq_count, TOK_DEV, D), indices.reshape(seq_count, TOK_DEV, K), lengths)
        per_sequence = jax.checkpoint(lambda one_piece: one_sequence(weights, store_float, one_piece))
        return lax.map(per_sequence, pieces).reshape(seq_count * TOK_DEV, D)
    result, pullback = jax.vjp(forward, params, tokens.astype(jnp.float32), datastore.astype(jnp.float32))
    param_grads, grad_tokens, grad_store = pullback(cotangent.astype(jnp.float32))
    return (result.astype(jnp.bfloat16), grad_tokens.astype(jnp.bfloat16), grad_store, param_grads[0], param_grads[1], param_grads[2], param_grads[3], param_grads[4], param_grads[5], param_grads[6], param_grads[7], param_grads[8])
```

```python
import jax
import jax.numpy as jnp
from jax import lax
from jax.sharding import PartitionSpec as P

D = 768
H = 12
HD = 64
K = 16


EPSILON = 1e-05


def product(matrix, factor):
    return jnp.dot(matrix, factor, preferred_element_type=jnp.float32)


def product_back(matrix, weight):
    return jnp.einsum("tf,df->td", matrix, weight, preferred_element_type=jnp.float32)


def contract_rows(matrix, factor):
    return jnp.einsum("td,tf->df", matrix, factor, preferred_element_type=jnp.float32)


def column_sum(matrix):
    return jnp.sum(matrix.astype(jnp.float32), axis=0)


def norm_forward(hidden, norm_weight, norm_shift):
    centered = hidden - jnp.mean(hidden, axis=-1, keepdims=True)
    inverse = lax.rsqrt(jnp.mean(centered * centered, axis=-1, keepdims=True) + EPSILON)
    normed = centered * inverse
    return (normed * norm_weight + norm_shift, normed, inverse)


def norm_backward(upstream, normed, inverse, norm_weight):
    scaled = upstream * norm_weight
    plain_mean = jnp.mean(scaled, axis=-1, keepdims=True)
    normed_mean = jnp.mean(scaled * normed, axis=-1, keepdims=True)
    return (
        inverse * (scaled - plain_mean - normed * normed_mean),
        jnp.sum(upstream * normed, axis=0),
        jnp.sum(upstream, axis=0),
    )


def log_total(scores):
    highest = jnp.max(scores, axis=-1, keepdims=True)
    return highest + jnp.log(jnp.sum(jnp.exp(scores - highest), axis=-1, keepdims=True))


def route_slots(picked, rows_here, owners, capacity):
    flat_ids = picked.reshape(-1)
    owner_of = flat_ids // rows_here
    local_row = flat_ids % rows_here
    by_owner = jnp.argsort(owner_of, stable=True)
    sorted_owner = owner_of[by_owner]
    owner_loads = jnp.sum(
        (owner_of[:, None] == jnp.arange(owners, dtype=jnp.int32)[None, :]).astype(jnp.int32),
        axis=0,
    )
    starts = jnp.cumsum(owner_loads) - owner_loads
    within = jnp.arange(flat_ids.shape[0], dtype=jnp.int32) - starts[sorted_owner]
    placed = jnp.zeros_like(flat_ids).at[by_owner].set(within)
    target = owner_of * capacity + placed
    request = jnp.zeros((owners * capacity,), jnp.int32).at[target].set(local_row)
    return (target, request.reshape(owners, capacity))


def fetch_rows(request, datastore):
    asked_rows = lax.all_to_all(request, "store", split_axis=0, concat_axis=0, tiled=True)
    found_rows = datastore[asked_rows.reshape(-1)].reshape(asked_rows.shape + (datastore.shape[1],))
    return (
        lax.all_to_all(found_rows, "store", split_axis=0, concat_axis=0, tiled=True),
        asked_rows,
    )


def fetch_again(request, datastore):
    asked_rows = lax.all_to_all(request, "store", split_axis=0, concat_axis=0, tiled=True)
    found_rows = datastore[asked_rows.reshape(-1)].reshape(asked_rows.shape + (datastore.shape[1],))
    return (
        lax.all_to_all(found_rows, "store", split_axis=0, concat_axis=0, tiled=True),
        asked_rows,
    )


def self_scores(queries, self_keys, allowed, score_scale):
    scores = (
        jnp.einsum("qhe,khe->hqk", queries, self_keys, preferred_element_type=jnp.float32)
        * score_scale
    )
    return jnp.where(allowed[None], scores, -1e30)


DENSE_LIMIT = 1 << 16


def is_dense(owners, rows_here):
    return owners * rows_here <= DENSE_LIMIT


def gather_store(datastore):
    copies = lax.axis_size("dp")
    part = datastore.shape[0] // copies
    mine = lax.dynamic_slice_in_dim(datastore, lax.axis_index("dp") * part, part, axis=0)
    return lax.all_gather(mine, ("store", "dp"), axis=0, tiled=True)


def reduce_store(indices, row_grad, rows):
    partial = (
        jnp.zeros((rows, D), jnp.float32)
        .at[indices.reshape(-1)]
        .add(row_grad.reshape(-1, D).astype(jnp.float32))
    )
    share = lax.psum_scatter(
        partial.astype(jnp.bfloat16), ("store", "dp"), scatter_dimension=0, tiled=True
    )
    return lax.all_gather(share, "dp", axis=0, tiled=True).astype(jnp.float32)


def reduce_weights(squares, inner, outer, features, inner_bias):
    owners = lax.axis_size("store")
    part = D // owners
    wide = inner.shape[1] // D
    low = [square.astype(jnp.bfloat16).reshape(owners, part, D) for square in squares]
    low += [
        inner[:, block * D : (block + 1) * D].astype(jnp.bfloat16).reshape(owners, part, D)
        for block in range(wide)
    ]
    low.append(outer.astype(jnp.bfloat16).reshape(owners, wide * part, D))
    small = jnp.concatenate(
        [feature.astype(jnp.bfloat16).reshape(owners, part) for feature in features]
        + [inner_bias.astype(jnp.bfloat16).reshape(owners, wide * part)],
        axis=1,
    )
    small = jnp.pad(small, ((0, 0), (0, 64 * D - small.shape[1]))).reshape(owners, 64, D)
    packed = jnp.concatenate(low + [small], axis=1)
    share = lax.psum_scatter(
        packed.reshape(-1, D), ("store", "dp"), scatter_dimension=0, tiled=True
    )
    total = lax.all_gather(share, "dp", axis=0, tiled=True).astype(jnp.float32)
    count = len(squares)
    blocks = total[: (count + 2 * wide) * part].reshape(count + 2 * wide, part, D)
    grad_proj = jnp.transpose(blocks[:6], (1, 0, 2))
    grad_out = jnp.transpose(blocks[6:8], (1, 0, 2))
    grad_inner = jnp.transpose(blocks[8 : 8 + wide], (1, 0, 2)).reshape(part, wide * D)
    grad_outer = blocks[8 + wide :].reshape(wide * part, D)
    tail = total[(count + 2 * wide) * part :].reshape(-1)
    table = tail[: len(features) * part].reshape(len(features), part)
    grad_bias = jnp.transpose(table[0:6])
    grad_gain = jnp.transpose(table[6:9])
    grad_shift = jnp.transpose(table[9:12])
    grad_inner_bias = tail[len(features) * part :][: wide * part]
    return (
        grad_proj,
        grad_out,
        grad_bias,
        grad_gain,
        grad_shift,
        grad_inner,
        grad_inner_bias,
        grad_outer,
        table[12],
    )


def body(
    tokens,
    datastore,
    indices,
    lengths,
    proj_weight,
    out_weight,
    proj_bias,
    norm_gain,
    norm_bias,
    inner_weight,
    inner_bias,
    outer_weight,
    outer_bias,
    cotangent,
):
    seq_len = tokens.shape[0]
    score_scale = HD ** (-0.5)
    owners = lax.axis_size("store")
    rows_here = datastore.shape[0]
    capacity = 2 * seq_len * K // owners
    position = jnp.arange(seq_len)
    length = lengths[0]
    allowed = (position[None, :] <= position[:, None]) & (position[None, :] < length)
    valid = (position < length)[:, None]
    dense = is_dense(owners, rows_here)
    if dense:
        full_store = gather_store(datastore)
        fetched = full_store[indices.reshape(-1)].reshape(seq_len, K, D)
    else:
        target, request = route_slots(indices, rows_here, owners, capacity)
        returned, asked_here = fetch_rows(request, datastore)
        fetched = returned.reshape(owners * capacity, D)[target].reshape(seq_len, K, D)
    self_bias = jnp.concatenate([proj_bias[:, 0], jnp.zeros((D,), jnp.float32), proj_bias[:, 1]])
    self_proj = proj_weight[:, 0:3, :].reshape(D, 3 * D)
    joined = (product(tokens, self_proj) + self_bias).astype(jnp.bfloat16)
    queries = joined[:, :D].reshape(seq_len, H, HD)
    self_keys = joined[:, D : 2 * D].reshape(seq_len, H, HD)
    values = joined[:, 2 * D :].reshape(seq_len, H, HD)
    scores = self_scores(queries, self_keys, allowed, score_scale)
    self_lse = log_total(scores)
    self_probs = jnp.exp(scores - self_lse).astype(jnp.bfloat16)
    self_mixed = (
        jnp.einsum("hqk,khe->qhe", self_probs, values, preferred_element_type=jnp.float32)
        .reshape(seq_len, D)
        .astype(jnp.bfloat16)
    )
    first_pre = tokens.astype(jnp.float32) + (
        product(self_mixed, out_weight[:, 0, :]) + proj_bias[:, 2]
    )
    first_out, first_normed, first_inverse = norm_forward(
        first_pre, norm_gain[:, 0], norm_bias[:, 0]
    )
    first_low = first_out.astype(jnp.bfloat16)
    cross_query = (
        (product(first_low, proj_weight[:, 3, :]) + proj_bias[:, 3])
        .astype(jnp.bfloat16)
        .reshape(seq_len, H, HD)
    )
    key_heads = proj_weight[:, 4, :].reshape(D, H, HD)
    folded = (
        jnp.einsum("the,dhe->thd", cross_query, key_heads, preferred_element_type=jnp.float32)
        * score_scale
    ).astype(jnp.bfloat16)
    cross_scores = jnp.einsum("thd,tkd->thk", folded, fetched, preferred_element_type=jnp.float32)
    cross_lse = log_total(cross_scores)
    cross_full = jnp.exp(cross_scores - cross_lse)
    cross_probs = cross_full.astype(jnp.bfloat16)
    summary = jnp.einsum(
        "thk,tkd->thd", cross_probs, fetched, preferred_element_type=jnp.float32
    ).astype(jnp.bfloat16)
    value_heads = proj_weight[:, 5, :].reshape(D, H, HD)
    cross_mixed = (
        jnp.einsum(
            "thd,dhe->the", summary, value_heads, preferred_element_type=jnp.float32
        ).reshape(seq_len, D)
        + proj_bias[:, 4]
    ).astype(jnp.bfloat16)
    second_pre = first_out + (product(cross_mixed, out_weight[:, 1, :]) + proj_bias[:, 5])
    second_out, second_normed, second_inverse = norm_forward(
        second_pre, norm_gain[:, 1], norm_bias[:, 1]
    )
    second_low = second_out.astype(jnp.bfloat16)
    inner_pre = product(second_low, inner_weight) + inner_bias
    activated = jax.nn.gelu(inner_pre, approximate=False).astype(jnp.bfloat16)
    third_pre = second_out + (product(activated, outer_weight) + outer_bias)
    third_out, third_normed, third_inverse = norm_forward(
        third_pre, norm_gain[:, 2], norm_bias[:, 2]
    )
    output = jnp.where(valid, third_out, 0.0).astype(jnp.bfloat16)
    upstream = jnp.where(valid, cotangent.astype(jnp.float32), 0.0)
    third_grad, gain_three, shift_three = norm_backward(
        upstream, third_normed, third_inverse, norm_gain[:, 2]
    )
    outer_low = third_grad.astype(jnp.bfloat16)
    grad_outer_weight = contract_rows(activated, outer_low)
    grad_outer_bias = column_sum(outer_low)
    act_grad = product_back(outer_low, outer_weight)
    slope = jax.vjp(lambda activation_in: jax.nn.gelu(activation_in, approximate=False), inner_pre)[
        1
    ](act_grad)[0]
    inner_low = slope.astype(jnp.bfloat16)
    grad_inner_weight = contract_rows(second_low, inner_low)
    grad_inner_bias = column_sum(inner_low)
    second_up = third_grad + product_back(inner_low, inner_weight)
    second_grad, gain_two, shift_two = norm_backward(
        second_up, second_normed, second_inverse, norm_gain[:, 1]
    )
    cross_out_low = second_grad.astype(jnp.bfloat16)
    grad_cross_out = contract_rows(cross_mixed, cross_out_low)
    bias_five = column_sum(cross_out_low)
    mixed_low = product_back(cross_out_low, out_weight[:, 1, :]).astype(jnp.bfloat16)
    bias_four = column_sum(mixed_low)
    mixed_heads = mixed_low.reshape(seq_len, H, HD)
    grad_value_heads = jnp.einsum(
        "thd,the->dhe", summary, mixed_heads, preferred_element_type=jnp.float32
    )
    summary_low = jnp.einsum(
        "the,dhe->thd", mixed_heads, value_heads, preferred_element_type=jnp.float32
    ).astype(jnp.bfloat16)
    if dense:
        fetched_back = fetched
    else:
        returned_again, asked_back = fetch_again(request, datastore)
        fetched_back = returned_again.reshape(owners * capacity, D)[target].reshape(seq_len, K, D)
    prob_grad = jnp.einsum(
        "thd,tkd->thk", summary_low, fetched_back, preferred_element_type=jnp.float32
    )
    score_low = (
        cross_full * (prob_grad - jnp.sum(cross_full * prob_grad, axis=-1, keepdims=True))
    ).astype(jnp.bfloat16)
    row_grad = (
        jnp.einsum("thk,thd->tkd", cross_probs, summary_low, preferred_element_type=jnp.float32)
        + jnp.einsum("thk,thd->tkd", score_low, folded, preferred_element_type=jnp.float32)
    ).astype(jnp.bfloat16)
    folded_low = jnp.einsum(
        "thk,tkd->thd", score_low, fetched_back, preferred_element_type=jnp.float32
    ).astype(jnp.bfloat16)
    grad_key_heads = (
        jnp.einsum("thd,the->dhe", folded_low, cross_query, preferred_element_type=jnp.float32)
        * score_scale
    )
    query_low = (
        (
            jnp.einsum("thd,dhe->the", folded_low, key_heads, preferred_element_type=jnp.float32)
            * score_scale
        )
        .astype(jnp.bfloat16)
        .reshape(seq_len, D)
    )
    bias_three = column_sum(query_low)
    grad_cross_query = contract_rows(first_low, query_low)
    if dense:
        grad_store = reduce_store(indices, row_grad, owners * rows_here)
    else:
        grad_buffer = (
            jnp.zeros((owners * capacity, D), jnp.bfloat16)
            .at[target]
            .set(row_grad.reshape(-1, D))
            .reshape(owners, capacity, D)
        )
        arrived = lax.all_to_all(grad_buffer, "store", split_axis=0, concat_axis=0, tiled=True)
        partial_store = (
            jnp.zeros((rows_here, D), jnp.float32)
            .at[asked_back.reshape(-1)]
            .add(arrived.reshape(-1, D).astype(jnp.float32))
        )
        grad_store = lax.psum(partial_store.astype(jnp.bfloat16), "dp").astype(jnp.float32)
    first_up = second_grad + product_back(query_low, proj_weight[:, 3, :])
    first_grad, gain_one, shift_one = norm_backward(
        first_up, first_normed, first_inverse, norm_gain[:, 0]
    )
    self_out_low = first_grad.astype(jnp.bfloat16)
    grad_self_out = contract_rows(self_mixed, self_out_low)
    bias_two = column_sum(self_out_low)
    self_mixed_low = (
        product_back(self_out_low, out_weight[:, 0, :]).astype(jnp.bfloat16).reshape(seq_len, H, HD)
    )
    value_grad = jnp.einsum(
        "hqk,qhe->khe", self_probs, self_mixed_low, preferred_element_type=jnp.float32
    )
    attend_grad = jnp.einsum(
        "qhe,khe->hqk", self_mixed_low, values, preferred_element_type=jnp.float32
    )
    self_full = jnp.exp(self_scores(queries, self_keys, allowed, score_scale) - self_lse)
    self_score_low = (
        self_full * (attend_grad - jnp.sum(self_full * attend_grad, axis=-1, keepdims=True))
    ).astype(jnp.bfloat16)
    query_grad = (
        jnp.einsum("hqk,khe->qhe", self_score_low, self_keys, preferred_element_type=jnp.float32)
        * score_scale
    )
    key_grad = (
        jnp.einsum("hqk,qhe->khe", self_score_low, queries, preferred_element_type=jnp.float32)
        * score_scale
    )
    joined_low = jnp.concatenate(
        [
            query_grad.reshape(seq_len, D),
            key_grad.reshape(seq_len, D),
            value_grad.reshape(seq_len, D),
        ],
        axis=1,
    ).astype(jnp.bfloat16)
    grad_self_proj = contract_rows(tokens, joined_low).reshape(D, 3, D)
    bias_zero = column_sum(joined_low[:, :D])
    bias_one = column_sum(joined_low[:, 2 * D :])
    grad_tokens = (first_grad + product_back(joined_low, self_proj)).astype(jnp.bfloat16)
    if dense:
        squares = (
            grad_self_proj[:, 0],
            grad_self_proj[:, 1],
            grad_self_proj[:, 2],
            grad_cross_query,
            grad_key_heads.reshape(D, D),
            grad_value_heads.reshape(D, D),
            grad_self_out,
            grad_cross_out,
        )
        biases = (bias_zero, bias_one, bias_two, bias_three, bias_four, bias_five)
        gains = (gain_one, gain_two, gain_three)
        shifts = (shift_one, shift_two, shift_three)
        shares = reduce_weights(
            squares,
            grad_inner_weight,
            grad_outer_weight,
            biases + gains + shifts + (grad_outer_bias,),
            grad_inner_bias,
        )
        return (output, grad_tokens, grad_store) + shares
    grad_proj = jnp.stack(
        [
            grad_self_proj[:, 0],
            grad_self_proj[:, 1],
            grad_self_proj[:, 2],
            grad_cross_query,
            grad_key_heads.reshape(D, D),
            grad_value_heads.reshape(D, D),
        ],
        axis=1,
    )
    grad_out = jnp.stack([grad_self_out, grad_cross_out], axis=1)
    grad_bias = jnp.stack([bias_zero, bias_one, bias_two, bias_three, bias_four, bias_five], axis=1)
    grad_gain = jnp.stack([gain_one, gain_two, gain_three], axis=1)
    grad_shift = jnp.stack([shift_one, shift_two, shift_three], axis=1)
    shares = (
        lax.psum_scatter(
            grad_proj.astype(jnp.bfloat16), "store", scatter_dimension=0, tiled=True
        ).astype(jnp.float32),
        lax.psum_scatter(
            grad_out.astype(jnp.bfloat16), "store", scatter_dimension=0, tiled=True
        ).astype(jnp.float32),
        lax.psum_scatter(
            grad_bias.astype(jnp.bfloat16), "store", scatter_dimension=0, tiled=True
        ).astype(jnp.float32),
        lax.psum_scatter(
            grad_gain.astype(jnp.bfloat16), "store", scatter_dimension=0, tiled=True
        ).astype(jnp.float32),
        lax.psum_scatter(
            grad_shift.astype(jnp.bfloat16), "store", scatter_dimension=0, tiled=True
        ).astype(jnp.float32),
        lax.psum_scatter(
            grad_inner_weight.astype(jnp.bfloat16), "store", scatter_dimension=0, tiled=True
        ).astype(jnp.float32),
        lax.psum_scatter(
            grad_inner_bias.astype(jnp.bfloat16), "store", scatter_dimension=0, tiled=True
        ).astype(jnp.float32),
        lax.psum_scatter(
            grad_outer_weight.astype(jnp.bfloat16), "store", scatter_dimension=0, tiled=True
        ).astype(jnp.float32),
        lax.psum_scatter(
            grad_outer_bias.astype(jnp.bfloat16), "store", scatter_dimension=0, tiled=True
        ).astype(jnp.float32),
    )
    totals = (
        lax.psum(shares[0].astype(jnp.bfloat16), "dp").astype(jnp.float32),
        lax.psum(shares[1].astype(jnp.bfloat16), "dp").astype(jnp.float32),
        lax.psum(shares[2].astype(jnp.bfloat16), "dp").astype(jnp.float32),
        lax.psum(shares[3].astype(jnp.bfloat16), "dp").astype(jnp.float32),
        lax.psum(shares[4].astype(jnp.bfloat16), "dp").astype(jnp.float32),
        lax.psum(shares[5].astype(jnp.bfloat16), "dp").astype(jnp.float32),
        lax.psum(shares[6].astype(jnp.bfloat16), "dp").astype(jnp.float32),
        lax.psum(shares[7].astype(jnp.bfloat16), "dp").astype(jnp.float32),
        lax.psum(shares[8].astype(jnp.bfloat16), "dp").astype(jnp.float32),
    )
    return (
        output,
        grad_tokens,
        grad_store,
        totals[0],
        totals[1],
        totals[2],
        totals[3],
        totals[4],
        totals[5],
        totals[6],
        totals[7],
        totals[8],
    )


def solution(mesh):
    in_specs = (
        P(("dp", "store"), None),
        P("store", None),
        P(("dp", "store"), None),
        P(("dp", "store")),
        P(),
        P(),
        P(),
        P(),
        P(),
        P(),
        P(),
        P(),
        P(),
        P(("dp", "store"), None),
    )
    out_specs = (
        P(("dp", "store"), None),
        P(("dp", "store"), None),
        P("store", None),
        P("store", None, None),
        P("store", None, None),
        P("store", None),
        P("store", None),
        P("store", None),
        P("store", None),
        P("store"),
        P("store", None),
        P("store"),
    )
    return jax.shard_map(body, mesh=mesh, in_specs=in_specs, out_specs=out_specs, check_vma=False)
```

```python
import jax
import jax.numpy as jnp
from jax import lax
from jax.sharding import PartitionSpec as P

D = 768
H = 12
HD = 64
K = 16


EPSILON = 1e-05


def product(matrix, factor):
    return jnp.dot(matrix, factor, preferred_element_type=jnp.float32)


def product_back(matrix, weight):
    return jnp.einsum("tf,df->td", matrix, weight, preferred_element_type=jnp.float32)


def contract_rows(matrix, factor):
    return jnp.einsum("td,tf->df", matrix, factor, preferred_element_type=jnp.float32)


def column_sum(matrix):
    return jnp.sum(matrix.astype(jnp.float32), axis=0)


def norm_forward(hidden, norm_weight, norm_shift):
    centered = hidden - jnp.mean(hidden, axis=-1, keepdims=True)
    inverse = lax.rsqrt(jnp.mean(centered * centered, axis=-1, keepdims=True) + EPSILON)
    normed = centered * inverse
    return (normed * norm_weight + norm_shift, normed, inverse)


def norm_backward(upstream, normed, inverse, norm_weight):
    scaled = upstream * norm_weight
    plain_mean = jnp.mean(scaled, axis=-1, keepdims=True)
    normed_mean = jnp.mean(scaled * normed, axis=-1, keepdims=True)
    return (
        inverse * (scaled - plain_mean - normed * normed_mean),
        jnp.sum(upstream * normed, axis=0),
        jnp.sum(upstream, axis=0),
    )


def log_total(scores):
    highest = jnp.max(scores, axis=-1, keepdims=True)
    return highest + jnp.log(jnp.sum(jnp.exp(scores - highest), axis=-1, keepdims=True))


def route_slots(picked, rows_here, owners, capacity):
    flat_ids = picked.reshape(-1)
    owner_of = flat_ids // rows_here
    local_row = flat_ids % rows_here
    by_owner = jnp.argsort(owner_of, stable=True)
    sorted_owner = owner_of[by_owner]
    owner_loads = jnp.sum(
        (owner_of[:, None] == jnp.arange(owners, dtype=jnp.int32)[None, :]).astype(jnp.int32),
        axis=0,
    )
    starts = jnp.cumsum(owner_loads) - owner_loads
    within = jnp.arange(flat_ids.shape[0], dtype=jnp.int32) - starts[sorted_owner]
    placed = jnp.zeros_like(flat_ids).at[by_owner].set(within)
    target = owner_of * capacity + placed
    request = jnp.zeros((owners * capacity,), jnp.int32).at[target].set(local_row)
    return (target, request.reshape(owners, capacity))


def fetch_rows(request, datastore):
    asked_rows = lax.all_to_all(request, "store", split_axis=0, concat_axis=0, tiled=True)
    found_rows = datastore[asked_rows.reshape(-1)].reshape(asked_rows.shape + (datastore.shape[1],))
    return (
        lax.all_to_all(found_rows, "store", split_axis=0, concat_axis=0, tiled=True),
        asked_rows,
    )


def fetch_again(request, datastore):
    asked_rows = lax.all_to_all(request, "store", split_axis=0, concat_axis=0, tiled=True)
    found_rows = datastore[asked_rows.reshape(-1)].reshape(asked_rows.shape + (datastore.shape[1],))
    return (
        lax.all_to_all(found_rows, "store", split_axis=0, concat_axis=0, tiled=True),
        asked_rows,
    )


def self_scores(queries, self_keys, allowed, score_scale):
    scores = (
        jnp.einsum("qhe,khe->hqk", queries, self_keys, preferred_element_type=jnp.float32)
        * score_scale
    )
    return jnp.where(allowed[None], scores, -1e30)


DENSE_LIMIT = 1 << 16


def is_dense(owners, rows_here):
    return owners * rows_here <= DENSE_LIMIT


STORE_PARTS = 2


def fetch_dense(datastore, indices):
    copies = lax.axis_size("dp")
    rows_here = datastore.shape[0]
    share = rows_here // copies
    part = share // STORE_PARTS
    flat = indices.reshape(-1)
    which = (flat % share) // part
    local = (flat // share) * part + flat % part
    start = lax.axis_index("dp") * share
    fetched = None
    earlier = None
    for index in range(STORE_PARTS):
        mine = lax.dynamic_slice_in_dim(datastore, start + index * part, part, axis=0)
        if earlier is not None:
            mine, earlier = lax.optimization_barrier((mine, earlier))
        table = lax.all_gather(mine, ("store", "dp"), axis=0, tiled=True)
        earlier = mine
        rows = table[local]
        if fetched is None:
            fetched = rows
        else:
            fetched = jnp.where((which == index)[:, None], rows, fetched)
    return fetched


def reduce_store(indices, row_grad, rows):
    partial = (
        jnp.zeros((rows, D), jnp.float32)
        .at[indices.reshape(-1)]
        .add(row_grad.reshape(-1, D).astype(jnp.float32))
    )
    share = lax.psum_scatter(
        partial.astype(jnp.bfloat16), ("store", "dp"), scatter_dimension=0, tiled=True
    )
    return lax.all_gather(share, "dp", axis=0, tiled=True).astype(jnp.float32)


def reduce_weights(squares, inner, outer, features, inner_bias):
    owners = lax.axis_size("store")
    part = D // owners
    wide = inner.shape[1] // D
    low = [square.astype(jnp.bfloat16).reshape(owners, part, D) for square in squares]
    low += [
        inner[:, block * D : (block + 1) * D].astype(jnp.bfloat16).reshape(owners, part, D)
        for block in range(wide)
    ]
    low.append(outer.astype(jnp.bfloat16).reshape(owners, wide * part, D))
    small = jnp.concatenate(
        [feature.astype(jnp.bfloat16).reshape(owners, part) for feature in features]
        + [inner_bias.astype(jnp.bfloat16).reshape(owners, wide * part)],
        axis=1,
    )
    small = jnp.pad(small, ((0, 0), (0, 64 * D - small.shape[1]))).reshape(owners, 64, D)
    packed = jnp.concatenate(low + [small], axis=1)
    share = lax.psum_scatter(
        packed.reshape(-1, D), ("store", "dp"), scatter_dimension=0, tiled=True
    )
    total = lax.all_gather(share, "dp", axis=0, tiled=True).astype(jnp.float32)
    count = len(squares)
    blocks = total[: (count + 2 * wide) * part].reshape(count + 2 * wide, part, D)
    grad_proj = jnp.transpose(blocks[:6], (1, 0, 2))
    grad_out = jnp.transpose(blocks[6:8], (1, 0, 2))
    grad_inner = jnp.transpose(blocks[8 : 8 + wide], (1, 0, 2)).reshape(part, wide * D)
    grad_outer = blocks[8 + wide :].reshape(wide * part, D)
    tail = total[(count + 2 * wide) * part :].reshape(-1)
    table = tail[: len(features) * part].reshape(len(features), part)
    grad_bias = jnp.transpose(table[0:6])
    grad_gain = jnp.transpose(table[6:9])
    grad_shift = jnp.transpose(table[9:12])
    grad_inner_bias = tail[len(features) * part :][: wide * part]
    return (
        grad_proj,
        grad_out,
        grad_bias,
        grad_gain,
        grad_shift,
        grad_inner,
        grad_inner_bias,
        grad_outer,
        table[12],
    )


def body(
    tokens,
    datastore,
    indices,
    lengths,
    proj_weight,
    out_weight,
    proj_bias,
    norm_gain,
    norm_bias,
    inner_weight,
    inner_bias,
    outer_weight,
    outer_bias,
    cotangent,
):
    seq_len = tokens.shape[0]
    score_scale = HD ** (-0.5)
    owners = lax.axis_size("store")
    rows_here = datastore.shape[0]
    capacity = 2 * seq_len * K // owners
    position = jnp.arange(seq_len)
    length = lengths[0]
    allowed = (position[None, :] <= position[:, None]) & (position[None, :] < length)
    valid = (position < length)[:, None]
    dense = is_dense(owners, rows_here)
    if dense:
        fetched = fetch_dense(datastore, indices).reshape(seq_len, K, D)
    else:
        target, request = route_slots(indices, rows_here, owners, capacity)
        returned, asked_here = fetch_rows(request, datastore)
        fetched = returned.reshape(owners * capacity, D)[target].reshape(seq_len, K, D)
    self_bias = jnp.concatenate([proj_bias[:, 0], jnp.zeros((D,), jnp.float32), proj_bias[:, 1]])
    self_proj = proj_weight[:, 0:3, :].reshape(D, 3 * D)
    joined = (product(tokens, self_proj) + self_bias).astype(jnp.bfloat16)
    queries = joined[:, :D].reshape(seq_len, H, HD)
    self_keys = joined[:, D : 2 * D].reshape(seq_len, H, HD)
    values = joined[:, 2 * D :].reshape(seq_len, H, HD)
    scores = self_scores(queries, self_keys, allowed, score_scale)
    self_lse = log_total(scores)
    self_probs = jnp.exp(scores - self_lse).astype(jnp.bfloat16)
    self_mixed = (
        jnp.einsum("hqk,khe->qhe", self_probs, values, preferred_element_type=jnp.float32)
        .reshape(seq_len, D)
        .astype(jnp.bfloat16)
    )
    first_pre = tokens.astype(jnp.float32) + (
        product(self_mixed, out_weight[:, 0, :]) + proj_bias[:, 2]
    )
    first_out, first_normed, first_inverse = norm_forward(
        first_pre, norm_gain[:, 0], norm_bias[:, 0]
    )
    first_low = first_out.astype(jnp.bfloat16)
    cross_query = (
        (product(first_low, proj_weight[:, 3, :]) + proj_bias[:, 3])
        .astype(jnp.bfloat16)
        .reshape(seq_len, H, HD)
    )
    key_heads = proj_weight[:, 4, :].reshape(D, H, HD)
    folded = (
        jnp.einsum("the,dhe->thd", cross_query, key_heads, preferred_element_type=jnp.float32)
        * score_scale
    ).astype(jnp.bfloat16)
    cross_scores = jnp.einsum("thd,tkd->thk", folded, fetched, preferred_element_type=jnp.float32)
    cross_lse = log_total(cross_scores)
    cross_full = jnp.exp(cross_scores - cross_lse)
    cross_probs = cross_full.astype(jnp.bfloat16)
    summary = jnp.einsum(
        "thk,tkd->thd", cross_probs, fetched, preferred_element_type=jnp.float32
    ).astype(jnp.bfloat16)
    value_heads = proj_weight[:, 5, :].reshape(D, H, HD)
    cross_mixed = (
        jnp.einsum(
            "thd,dhe->the", summary, value_heads, preferred_element_type=jnp.float32
        ).reshape(seq_len, D)
        + proj_bias[:, 4]
    ).astype(jnp.bfloat16)
    second_pre = first_out + (product(cross_mixed, out_weight[:, 1, :]) + proj_bias[:, 5])
    second_out, second_normed, second_inverse = norm_forward(
        second_pre, norm_gain[:, 1], norm_bias[:, 1]
    )
    second_low = second_out.astype(jnp.bfloat16)
    inner_pre = product(second_low, inner_weight) + inner_bias
    activated = jax.nn.gelu(inner_pre, approximate=False).astype(jnp.bfloat16)
    third_pre = second_out + (product(activated, outer_weight) + outer_bias)
    third_out, third_normed, third_inverse = norm_forward(
        third_pre, norm_gain[:, 2], norm_bias[:, 2]
    )
    output = jnp.where(valid, third_out, 0.0).astype(jnp.bfloat16)
    upstream = jnp.where(valid, cotangent.astype(jnp.float32), 0.0)
    third_grad, gain_three, shift_three = norm_backward(
        upstream, third_normed, third_inverse, norm_gain[:, 2]
    )
    outer_low = third_grad.astype(jnp.bfloat16)
    grad_outer_weight = contract_rows(activated, outer_low)
    grad_outer_bias = column_sum(outer_low)
    act_grad = product_back(outer_low, outer_weight)
    slope = jax.vjp(lambda activation_in: jax.nn.gelu(activation_in, approximate=False), inner_pre)[
        1
    ](act_grad)[0]
    inner_low = slope.astype(jnp.bfloat16)
    grad_inner_weight = contract_rows(second_low, inner_low)
    grad_inner_bias = column_sum(inner_low)
    second_up = third_grad + product_back(inner_low, inner_weight)
    second_grad, gain_two, shift_two = norm_backward(
        second_up, second_normed, second_inverse, norm_gain[:, 1]
    )
    cross_out_low = second_grad.astype(jnp.bfloat16)
    grad_cross_out = contract_rows(cross_mixed, cross_out_low)
    bias_five = column_sum(cross_out_low)
    mixed_low = product_back(cross_out_low, out_weight[:, 1, :]).astype(jnp.bfloat16)
    bias_four = column_sum(mixed_low)
    mixed_heads = mixed_low.reshape(seq_len, H, HD)
    grad_value_heads = jnp.einsum(
        "thd,the->dhe", summary, mixed_heads, preferred_element_type=jnp.float32
    )
    summary_low = jnp.einsum(
        "the,dhe->thd", mixed_heads, value_heads, preferred_element_type=jnp.float32
    ).astype(jnp.bfloat16)
    if dense:
        fetched_back = fetched
    else:
        returned_again, asked_back = fetch_again(request, datastore)
        fetched_back = returned_again.reshape(owners * capacity, D)[target].reshape(seq_len, K, D)
    prob_grad = jnp.einsum(
        "thd,tkd->thk", summary_low, fetched_back, preferred_element_type=jnp.float32
    )
    score_low = (
        cross_full * (prob_grad - jnp.sum(cross_full * prob_grad, axis=-1, keepdims=True))
    ).astype(jnp.bfloat16)
    row_grad = (
        jnp.einsum("thk,thd->tkd", cross_probs, summary_low, preferred_element_type=jnp.float32)
        + jnp.einsum("thk,thd->tkd", score_low, folded, preferred_element_type=jnp.float32)
    ).astype(jnp.bfloat16)
    folded_low = jnp.einsum(
        "thk,tkd->thd", score_low, fetched_back, preferred_element_type=jnp.float32
    ).astype(jnp.bfloat16)
    grad_key_heads = (
        jnp.einsum("thd,the->dhe", folded_low, cross_query, preferred_element_type=jnp.float32)
        * score_scale
    )
    query_low = (
        (
            jnp.einsum("thd,dhe->the", folded_low, key_heads, preferred_element_type=jnp.float32)
            * score_scale
        )
        .astype(jnp.bfloat16)
        .reshape(seq_len, D)
    )
    bias_three = column_sum(query_low)
    grad_cross_query = contract_rows(first_low, query_low)
    if dense:
        grad_store = reduce_store(indices, row_grad, owners * rows_here)
    else:
        grad_buffer = (
            jnp.zeros((owners * capacity, D), jnp.bfloat16)
            .at[target]
            .set(row_grad.reshape(-1, D))
            .reshape(owners, capacity, D)
        )
        arrived = lax.all_to_all(grad_buffer, "store", split_axis=0, concat_axis=0, tiled=True)
        partial_store = (
            jnp.zeros((rows_here, D), jnp.float32)
            .at[asked_back.reshape(-1)]
            .add(arrived.reshape(-1, D).astype(jnp.float32))
        )
        grad_store = lax.psum(partial_store.astype(jnp.bfloat16), "dp").astype(jnp.float32)
    first_up = second_grad + product_back(query_low, proj_weight[:, 3, :])
    first_grad, gain_one, shift_one = norm_backward(
        first_up, first_normed, first_inverse, norm_gain[:, 0]
    )
    self_out_low = first_grad.astype(jnp.bfloat16)
    grad_self_out = contract_rows(self_mixed, self_out_low)
    bias_two = column_sum(self_out_low)
    self_mixed_low = (
        product_back(self_out_low, out_weight[:, 0, :]).astype(jnp.bfloat16).reshape(seq_len, H, HD)
    )
    value_grad = jnp.einsum(
        "hqk,qhe->khe", self_probs, self_mixed_low, preferred_element_type=jnp.float32
    )
    attend_grad = jnp.einsum(
        "qhe,khe->hqk", self_mixed_low, values, preferred_element_type=jnp.float32
    )
    self_full = jnp.exp(self_scores(queries, self_keys, allowed, score_scale) - self_lse)
    self_score_low = (
        self_full * (attend_grad - jnp.sum(self_full * attend_grad, axis=-1, keepdims=True))
    ).astype(jnp.bfloat16)
    query_grad = (
        jnp.einsum("hqk,khe->qhe", self_score_low, self_keys, preferred_element_type=jnp.float32)
        * score_scale
    )
    key_grad = (
        jnp.einsum("hqk,qhe->khe", self_score_low, queries, preferred_element_type=jnp.float32)
        * score_scale
    )
    joined_low = jnp.concatenate(
        [
            query_grad.reshape(seq_len, D),
            key_grad.reshape(seq_len, D),
            value_grad.reshape(seq_len, D),
        ],
        axis=1,
    ).astype(jnp.bfloat16)
    grad_self_proj = contract_rows(tokens, joined_low).reshape(D, 3, D)
    bias_zero = column_sum(joined_low[:, :D])
    bias_one = column_sum(joined_low[:, 2 * D :])
    grad_tokens = (first_grad + product_back(joined_low, self_proj)).astype(jnp.bfloat16)
    if dense:
        squares = (
            grad_self_proj[:, 0],
            grad_self_proj[:, 1],
            grad_self_proj[:, 2],
            grad_cross_query,
            grad_key_heads.reshape(D, D),
            grad_value_heads.reshape(D, D),
            grad_self_out,
            grad_cross_out,
        )
        biases = (bias_zero, bias_one, bias_two, bias_three, bias_four, bias_five)
        gains = (gain_one, gain_two, gain_three)
        shifts = (shift_one, shift_two, shift_three)
        shares = reduce_weights(
            squares,
            grad_inner_weight,
            grad_outer_weight,
            biases + gains + shifts + (grad_outer_bias,),
            grad_inner_bias,
        )
        return (output, grad_tokens, grad_store) + shares
    grad_proj = jnp.stack(
        [
            grad_self_proj[:, 0],
            grad_self_proj[:, 1],
            grad_self_proj[:, 2],
            grad_cross_query,
            grad_key_heads.reshape(D, D),
            grad_value_heads.reshape(D, D),
        ],
        axis=1,
    )
    grad_out = jnp.stack([grad_self_out, grad_cross_out], axis=1)
    grad_bias = jnp.stack([bias_zero, bias_one, bias_two, bias_three, bias_four, bias_five], axis=1)
    grad_gain = jnp.stack([gain_one, gain_two, gain_three], axis=1)
    grad_shift = jnp.stack([shift_one, shift_two, shift_three], axis=1)
    shares = (
        lax.psum_scatter(
            grad_proj.astype(jnp.bfloat16), "store", scatter_dimension=0, tiled=True
        ).astype(jnp.float32),
        lax.psum_scatter(
            grad_out.astype(jnp.bfloat16), "store", scatter_dimension=0, tiled=True
        ).astype(jnp.float32),
        lax.psum_scatter(
            grad_bias.astype(jnp.bfloat16), "store", scatter_dimension=0, tiled=True
        ).astype(jnp.float32),
        lax.psum_scatter(
            grad_gain.astype(jnp.bfloat16), "store", scatter_dimension=0, tiled=True
        ).astype(jnp.float32),
        lax.psum_scatter(
            grad_shift.astype(jnp.bfloat16), "store", scatter_dimension=0, tiled=True
        ).astype(jnp.float32),
        lax.psum_scatter(
            grad_inner_weight.astype(jnp.bfloat16), "store", scatter_dimension=0, tiled=True
        ).astype(jnp.float32),
        lax.psum_scatter(
            grad_inner_bias.astype(jnp.bfloat16), "store", scatter_dimension=0, tiled=True
        ).astype(jnp.float32),
        lax.psum_scatter(
            grad_outer_weight.astype(jnp.bfloat16), "store", scatter_dimension=0, tiled=True
        ).astype(jnp.float32),
        lax.psum_scatter(
            grad_outer_bias.astype(jnp.bfloat16), "store", scatter_dimension=0, tiled=True
        ).astype(jnp.float32),
    )
    totals = (
        lax.psum(shares[0].astype(jnp.bfloat16), "dp").astype(jnp.float32),
        lax.psum(shares[1].astype(jnp.bfloat16), "dp").astype(jnp.float32),
        lax.psum(shares[2].astype(jnp.bfloat16), "dp").astype(jnp.float32),
        lax.psum(shares[3].astype(jnp.bfloat16), "dp").astype(jnp.float32),
        lax.psum(shares[4].astype(jnp.bfloat16), "dp").astype(jnp.float32),
        lax.psum(shares[5].astype(jnp.bfloat16), "dp").astype(jnp.float32),
        lax.psum(shares[6].astype(jnp.bfloat16), "dp").astype(jnp.float32),
        lax.psum(shares[7].astype(jnp.bfloat16), "dp").astype(jnp.float32),
        lax.psum(shares[8].astype(jnp.bfloat16), "dp").astype(jnp.float32),
    )
    return (
        output,
        grad_tokens,
        grad_store,
        totals[0],
        totals[1],
        totals[2],
        totals[3],
        totals[4],
        totals[5],
        totals[6],
        totals[7],
        totals[8],
    )


def solution(mesh):
    in_specs = (
        P(("dp", "store"), None),
        P("store", None),
        P(("dp", "store"), None),
        P(("dp", "store")),
        P(),
        P(),
        P(),
        P(),
        P(),
        P(),
        P(),
        P(),
        P(),
        P(("dp", "store"), None),
    )
    out_specs = (
        P(("dp", "store"), None),
        P(("dp", "store"), None),
        P("store", None),
        P("store", None, None),
        P("store", None, None),
        P("store", None),
        P("store", None),
        P("store", None),
        P("store", None),
        P("store"),
        P("store", None),
        P("store"),
    )
    return jax.shard_map(body, mesh=mesh, in_specs=in_specs, out_specs=out_specs, check_vma=False)
```

```python
import functools

import jax
import jax.numpy as jnp
from jax import lax
from jax.experimental import pallas as pl
from jax.experimental.pallas import tpu as pltpu
from jax.sharding import PartitionSpec as P

D = 768
H = 12
HD = 64
K = 16


EPSILON = 1e-05


def product(matrix, factor):
    return jnp.dot(matrix, factor, preferred_element_type=jnp.float32)


def product_back(matrix, weight):
    return jnp.einsum("tf,df->td", matrix, weight, preferred_element_type=jnp.float32)


def contract_rows(matrix, factor):
    return jnp.einsum("td,tf->df", matrix, factor, preferred_element_type=jnp.float32)


def column_sum(matrix):
    return jnp.sum(matrix.astype(jnp.float32), axis=0)


def norm_forward(hidden, norm_weight, norm_shift):
    centered = hidden - jnp.mean(hidden, axis=-1, keepdims=True)
    inverse = lax.rsqrt(jnp.mean(centered * centered, axis=-1, keepdims=True) + EPSILON)
    normed = centered * inverse
    return (normed * norm_weight + norm_shift, normed, inverse)


def norm_backward(upstream, normed, inverse, norm_weight):
    scaled = upstream * norm_weight
    plain_mean = jnp.mean(scaled, axis=-1, keepdims=True)
    normed_mean = jnp.mean(scaled * normed, axis=-1, keepdims=True)
    return (
        inverse * (scaled - plain_mean - normed * normed_mean),
        jnp.sum(upstream * normed, axis=0),
        jnp.sum(upstream, axis=0),
    )


def log_total(scores):
    highest = jnp.max(scores, axis=-1, keepdims=True)
    return highest + jnp.log(jnp.sum(jnp.exp(scores - highest), axis=-1, keepdims=True))


def route_slots(picked, rows_here, owners, capacity):
    flat_ids = picked.reshape(-1)
    owner_of = flat_ids // rows_here
    local_row = flat_ids % rows_here
    by_owner = jnp.argsort(owner_of, stable=True)
    sorted_owner = owner_of[by_owner]
    owner_loads = jnp.sum(
        (owner_of[:, None] == jnp.arange(owners, dtype=jnp.int32)[None, :]).astype(jnp.int32),
        axis=0,
    )
    starts = jnp.cumsum(owner_loads) - owner_loads
    within = jnp.arange(flat_ids.shape[0], dtype=jnp.int32) - starts[sorted_owner]
    placed = jnp.zeros_like(flat_ids).at[by_owner].set(within)
    target = owner_of * capacity + placed
    request = jnp.zeros((owners * capacity,), jnp.int32).at[target].set(local_row)
    return (target, request.reshape(owners, capacity))


def fetch_rows(request, datastore):
    asked_rows = lax.all_to_all(request, "store", split_axis=0, concat_axis=0, tiled=True)
    found_rows = datastore[asked_rows.reshape(-1)].reshape(asked_rows.shape + (datastore.shape[1],))
    return (
        lax.all_to_all(found_rows, "store", split_axis=0, concat_axis=0, tiled=True),
        asked_rows,
    )


def fetch_again(request, datastore):
    asked_rows = lax.all_to_all(request, "store", split_axis=0, concat_axis=0, tiled=True)
    found_rows = datastore[asked_rows.reshape(-1)].reshape(asked_rows.shape + (datastore.shape[1],))
    return (
        lax.all_to_all(found_rows, "store", split_axis=0, concat_axis=0, tiled=True),
        asked_rows,
    )


def self_scores(queries, self_keys, allowed, score_scale):
    scores = (
        jnp.einsum("qhe,khe->hqk", queries, self_keys, preferred_element_type=jnp.float32)
        * score_scale
    )
    return jnp.where(allowed[None], scores, -1e30)


DENSE_LIMIT = 1 << 16


def is_dense(owners, rows_here):
    fits = owners * rows_here <= DENSE_LIMIT and rows_here % (8 * CHUNK) == 0
    return fits and owners == 8 and lax.axis_size("dp") == 4


STORE_PARTS = 2


def fetch_dense(datastore, indices, plan):
    copies = lax.axis_size("dp")
    rows_here = datastore.shape[0]
    share = rows_here // copies
    part = share // STORE_PARTS
    flat = indices.reshape(-1)
    which = (flat % share) // part
    local = (flat // share) * part + flat % part
    start = lax.axis_index("dp") * share
    fetched = None
    earlier = None
    for index in range(STORE_PARTS):
        mine = lax.dynamic_slice_in_dim(datastore, start + index * part, part, axis=0)
        if earlier is not None:
            mine, earlier = lax.optimization_barrier((mine, earlier))
        table = lax.all_gather(mine, ("store", "dp"), axis=0, tiled=True)
        earlier = mine
        if index == STORE_PARTS - 1:
            which, plan = lax.optimization_barrier((which, plan))
        rows = table[local]
        if fetched is None:
            fetched = rows
        else:
            fetched = jnp.where((which == index)[:, None], rows, fetched)
    return fetched, plan


MESH_ID = pl.DeviceIdType.MESH
VMEM_LIMIT = 67043328
CHUNK = 64


GROUP = 8


def scatter_kernel(steps, block, out_rows, row_ref, from_ref, twice_ref, groups_ref, own_ref, other_ref, out_ref, total, wide):
    step = pl.program_id(0)

    @pl.when(step == 0)
    def _():
        def clear(i, carry):
            total[pl.ds(i * 32, 32), :] = jnp.zeros((32, D), jnp.float32)
            return carry
        lax.fori_loop(0, total.shape[0] // 32, clear, 0)

    @pl.when(step < steps // 2)
    def _():
        wide[...] = own_ref[...].astype(jnp.float32)

    @pl.when((step >= steps // 2) & (step < steps))
    def _():
        wide[...] = other_ref[...].astype(jnp.float32)

    @pl.when(step < steps)
    def _():
        def group(i, carry):
            first = step * block + i * GROUP
            rows = [row_ref[first + k] for k in range(GROUP)]
            came = [from_ref[first + k] for k in range(GROUP)]
            twice = twice_ref[step * (block // GROUP) + i]

            @pl.when(twice == 0)
            def _():
                sums = [total[pl.ds(rows[k], 1), :] + wide[pl.ds(came[k], 1), :] for k in range(GROUP)]
                for k in range(GROUP):
                    total[pl.ds(rows[k], 1), :] = sums[k]

            @pl.when(twice != 0)
            def _():
                for k in range(GROUP):
                    total[pl.ds(rows[k], 1), :] = total[pl.ds(rows[k], 1), :] + wide[pl.ds(came[k], 1), :]
            return carry
        lax.fori_loop(0, groups_ref[step], group, 0)

    @pl.when(step >= steps)
    def _():
        first = pl.multiple_of((step - steps) * out_rows, out_rows)
        out_ref[...] = total[pl.ds(first, out_rows), :].astype(jnp.bfloat16)


SCATTER_BLOCK = 256


def scatter_plan(where, rows):
    keys = jnp.arange(where.shape[0], dtype=jnp.int32).reshape(-1, SCATTER_BLOCK) % SCATTER_BLOCK
    where = where.reshape(-1, SCATTER_BLOCK)
    skipped = where >= rows
    keys, where = lax.sort((jnp.where(skipped, keys + SCATTER_BLOCK, keys), where), dimension=1, num_keys=1)
    count = jnp.sum((~skipped).astype(jnp.int32), axis=1)
    groups = (count + GROUP - 1) // GROUP
    where = jnp.where(keys >= SCATTER_BLOCK, rows + keys % GROUP, where)
    spare = lax.broadcasted_iota(jnp.int32, where.shape, 1) % GROUP
    where = jnp.where(keys >= SCATTER_BLOCK, rows + spare, where)
    eights = where.reshape(-1, GROUP)
    twice = jnp.zeros((eights.shape[0],), jnp.int32)
    for shift in range(1, GROUP):
        same = eights[:, shift:] == eights[:, :-shift]
        twice = twice | jnp.any(same, axis=1).astype(jnp.int32)
    return where.reshape(-1), (keys % SCATTER_BLOCK).reshape(-1), twice, groups


def scatter_rows(plan, own, other, rows, out_rows=256):
    block = SCATTER_BLOCK
    half = own.shape[0] // block
    steps = 2 * half
    return pl.pallas_call(
        functools.partial(scatter_kernel, steps, block, out_rows),
        out_shape=jax.ShapeDtypeStruct((rows, D), jnp.bfloat16),
        grid_spec=pltpu.PrefetchScalarGridSpec(
            num_scalar_prefetch=4,
            grid=(steps + rows // out_rows,),
            in_specs=[
                pl.BlockSpec((block, D), lambda i, *_: (jnp.minimum(i, half - 1), 0)),
                pl.BlockSpec((block, D), lambda i, *_: (jnp.clip(i - half, 0, half - 1), 0)),
            ],
            out_specs=pl.BlockSpec((out_rows, D), lambda i, *_: (jnp.maximum(i - steps, 0), 0)),
            scratch_shapes=[
                pltpu.VMEM((rows + 32, D), jnp.float32),
                pltpu.VMEM((block, D), jnp.float32),
            ],
        ),
        compiler_params=pltpu.CompilerParams(vmem_limit_bytes=VMEM_LIMIT),
        name="scatter_rows",
    )(*plan, own, other)


def reduce_kernel(chunks, part_ref, out_ref, keep_a, keep_b, one_a, one_b, two_a, two_b, layer, along, done,
                  keep_sem, one_send, one_recv, two_send, two_recv, z_send, z_recv,
                  own_sem, y_send, y_recv, core_send, core_recv, pass_send, pass_recv):
    dp = lax.axis_index("dp")
    store = lax.axis_index("store")
    y, core = lax.div(dp, 2), lax.rem(dp, 2)
    z, x = lax.div(store, 2), lax.rem(store, 2)
    x_peer = (dp, z * 2 + (1 - x))
    y_peer = ((1 - y) * 2 + core, store)
    core_peer = (y * 2 + (1 - core), store)
    z_of = [lax.rem(z + hop, 4) for hop in range(4)]
    z_peer = [(dp, z_of[hop] * 2 + x) for hop in range(4)]

    barrier = pltpu.get_barrier_semaphore()
    for peer in (x_peer, y_peer, core_peer, z_peer[1], z_peer[2], z_peer[3]):
        pl.semaphore_signal(barrier, inc=1, device_id=peer, device_id_type=MESH_ID)
    pl.semaphore_wait(barrier, 6)

    def remote(src, dst, send, recv, peer):
        return pltpu.make_async_remote_copy(src_ref=src, dst_ref=dst, send_sem=send, recv_sem=recv,
                                            device_id=peer, device_id_type=MESH_ID)

    keeps = [(
        pltpu.make_async_copy(part_ref.at[:, x, :, 0, q], keep_a.at[q], keep_sem.at[0, q]),
        pltpu.make_async_copy(part_ref.at[:, :, y, 1, q], keep_b.at[q], keep_sem.at[1, q]),
    ) for q in range(chunks)]
    ones = [(
        remote(part_ref.at[:, 1 - x, :, 0, q], one_a.at[q], one_send.at[0, q], one_recv.at[0, q], x_peer),
        remote(part_ref.at[:, :, 1 - y, 1, q], one_b.at[q], one_send.at[1, q], one_recv.at[1, q], y_peer),
    ) for q in range(chunks)]
    twos = [(
        remote(keep_a.at[q, :, 1 - y], two_a.at[q], two_send.at[0, q], two_recv.at[0, q], y_peer),
        remote(keep_b.at[q, :, 1 - x], two_b.at[q], two_send.at[1, q], two_recv.at[1, q], x_peer),
    ) for q in range(chunks)]
    zs = [[
        remote(layer.at[q, z_of[hop]], along.at[q, hop - 1], z_send.at[hop - 1, q], z_recv.at[hop - 1, q], z_peer[hop])
        for hop in (1, 2, 3)] for q in range(chunks)]
    own = [pltpu.make_async_copy(done.at[q], out_ref.at[core, y, :, q], own_sem.at[q]) for q in range(chunks)]
    to_y = [remote(done.at[q], out_ref.at[core, y, :, q], y_send.at[q], y_recv.at[q], y_peer) for q in range(chunks)]
    to_core = [remote(done.at[q], out_ref.at[core, y, :, q], core_send.at[q], core_recv.at[q], core_peer) for q in range(chunks)]
    passed = [remote(out_ref.at[core, 1 - y, :, q], out_ref.at[core, 1 - y, :, q], pass_send.at[q], pass_recv.at[q], core_peer)
              for q in range(chunks)]

    def plus(first, second):
        return (first.astype(jnp.float32) + second.astype(jnp.float32)).astype(jnp.bfloat16)

    window = 2
    for q in range(min(window, chunks)):
        for copy in keeps[q] + ones[q]:
            copy.start()
    for step in range(chunks + 3):
        q = step
        if q < chunks:
            for copy in keeps[q]:
                copy.wait()
            for copy in ones[q]:
                copy.wait_recv()

            def merge(i, carry, q=q):
                for half in range(2):
                    keep_a[q, i, half] = plus(keep_a[q, i, half], one_a[q, i, half])
                    keep_b[q, i, half] = plus(keep_b[q, i, half], one_b[q, i, half])
                return carry
            lax.fori_loop(0, 4, merge, 0)
            for copy in twos[q]:
                copy.start()
            if q + window < chunks:
                for copy in keeps[q + window] + ones[q + window]:
                    copy.start()
        q = step - 1
        if 0 <= q < chunks:
            for copy in twos[q]:
                copy.wait_recv()

            def merge_two(i, carry, q=q):
                layer[q, i, 0] = plus(keep_a[q, i, y], two_a[q, i])
                layer[q, i, 1] = plus(keep_b[q, i, x], two_b[q, i])
                return carry
            lax.fori_loop(0, 4, merge_two, 0)
            for copy in zs[q]:
                copy.start()
        q = step - 2
        if 0 <= q < chunks:
            for copy in zs[q]:
                copy.wait_recv()

            def finish(i, carry, q=q):
                value = layer[q, z, i].astype(jnp.float32)
                for hop in range(3):
                    value = value + along[q, hop, i].astype(jnp.float32)
                done[q, i] = value.astype(jnp.bfloat16)
                return carry
            lax.fori_loop(0, 2, finish, 0)
            for copy in (own[q], to_y[q], to_core[q]):
                copy.start()
        q = step - 3
        if 0 <= q < chunks:
            to_y[q].wait_recv()
            passed[q].start()
    for q in range(chunks):
        for copy in ones[q] + twos[q] + tuple(zs[q]):
            copy.wait_send()
        own[q].wait()
        to_y[q].wait_send()
        to_core[q].wait()
        passed[q].wait()


def reduce_rows(partial, collective_id=0):
    rows = partial.shape[0] // 8
    chunks = rows // (4 * CHUNK)
    blocks = partial.reshape(4, 2, 2, 2, chunks, CHUNK, D)
    dma = pltpu.SemaphoreType.DMA
    vm = lambda *lead: pltpu.VMEM(lead + (CHUNK, D), jnp.bfloat16)
    out = pl.pallas_call(
        functools.partial(reduce_kernel, chunks),
        out_shape=jax.ShapeDtypeStruct((2, 2, 2, chunks, CHUNK, D), jnp.bfloat16),
        in_specs=[pl.BlockSpec(memory_space=pl.ANY)],
        out_specs=pl.BlockSpec(memory_space=pl.ANY),
        scratch_shapes=[
            vm(chunks, 4, 2), vm(chunks, 4, 2), vm(chunks, 4, 2), vm(chunks, 4, 2),
            vm(chunks, 4), vm(chunks, 4), vm(chunks, 4, 2), vm(chunks, 3, 2), vm(chunks, 2),
            dma((2, chunks)), dma((2, chunks)), dma((2, chunks)), dma((2, chunks)), dma((2, chunks)),
            dma((3, chunks)), dma((3, chunks)),
            dma((chunks,)), dma((chunks,)), dma((chunks,)), dma((chunks,)), dma((chunks,)), dma((chunks,)), dma((chunks,)),
        ],
        compiler_params=pltpu.CompilerParams(collective_id=collective_id, has_side_effects=True, vmem_limit_bytes=VMEM_LIMIT),
        name="reduce_rows",
    )(blocks)
    return out.reshape(2 * rows, D)

PAIRS = ((0, 1), (1, 0), (2, 3), (3, 2))


def own_rows(flat, rows_here):
    half = rows_here // 2
    core = lax.rem(lax.axis_index("dp"), 2)
    local = flat % rows_here
    rows = lax.axis_size("store") * half
    return jnp.where(local // half == core, (flat // rows_here) * half + local % half, rows)


def plan_store(indices, rows_here):
    flat = indices.reshape(-1)
    other = lax.ppermute(flat, "dp", PAIRS)
    where = jnp.concatenate([own_rows(flat, rows_here), own_rows(other, rows_here)])
    return scatter_plan(where, lax.axis_size("store") * rows_here // 2)


def reduce_store(plan, row_grad, rows_here):
    own = row_grad.reshape(-1, D)
    other = lax.ppermute(own, "dp", PAIRS)
    partial = scatter_rows(plan, own, other, lax.axis_size("store") * rows_here // 2)
    return reduce_rows(partial).astype(jnp.float32)


def reduce_weights(squares, inner, outer, features, inner_bias):
    owners = lax.axis_size("store")
    part = D // owners
    wide = inner.shape[1] // D
    low = [square.astype(jnp.bfloat16).reshape(owners, part, D) for square in squares]
    low += [
        inner[:, block * D : (block + 1) * D].astype(jnp.bfloat16).reshape(owners, part, D)
        for block in range(wide)
    ]
    low.append(outer.astype(jnp.bfloat16).reshape(owners, wide * part, D))
    small = jnp.concatenate(
        [feature.astype(jnp.bfloat16).reshape(owners, part) for feature in features]
        + [inner_bias.astype(jnp.bfloat16).reshape(owners, wide * part)],
        axis=1,
    )
    small = jnp.pad(small, ((0, 0), (0, 64 * D - small.shape[1]))).reshape(owners, 64, D)
    packed = jnp.concatenate(low + [small], axis=1)
    share = lax.psum_scatter(
        packed.reshape(-1, D), ("store", "dp"), scatter_dimension=0, tiled=True
    )
    total = lax.all_gather(share, "dp", axis=0, tiled=True).astype(jnp.float32)
    count = len(squares)
    blocks = total[: (count + 2 * wide) * part].reshape(count + 2 * wide, part, D)
    grad_proj = jnp.transpose(blocks[:6], (1, 0, 2))
    grad_out = jnp.transpose(blocks[6:8], (1, 0, 2))
    grad_inner = jnp.transpose(blocks[8 : 8 + wide], (1, 0, 2)).reshape(part, wide * D)
    grad_outer = blocks[8 + wide :].reshape(wide * part, D)
    tail = total[(count + 2 * wide) * part :].reshape(-1)
    table = tail[: len(features) * part].reshape(len(features), part)
    grad_bias = jnp.transpose(table[0:6])
    grad_gain = jnp.transpose(table[6:9])
    grad_shift = jnp.transpose(table[9:12])
    grad_inner_bias = tail[len(features) * part :][: wide * part]
    return (
        grad_proj,
        grad_out,
        grad_bias,
        grad_gain,
        grad_shift,
        grad_inner,
        grad_inner_bias,
        grad_outer,
        table[12],
    )


def body(
    tokens,
    datastore,
    indices,
    lengths,
    proj_weight,
    out_weight,
    proj_bias,
    norm_gain,
    norm_bias,
    inner_weight,
    inner_bias,
    outer_weight,
    outer_bias,
    cotangent,
):
    seq_len = tokens.shape[0]
    score_scale = HD ** (-0.5)
    owners = lax.axis_size("store")
    rows_here = datastore.shape[0]
    capacity = 2 * seq_len * K // owners
    position = jnp.arange(seq_len)
    length = lengths[0]
    allowed = (position[None, :] <= position[:, None]) & (position[None, :] < length)
    valid = (position < length)[:, None]
    dense = is_dense(owners, rows_here)
    if dense:
        plan = plan_store(indices, rows_here)
        fetched, plan = fetch_dense(datastore, indices, plan)
        fetched = fetched.reshape(seq_len, K, D)
    else:
        target, request = route_slots(indices, rows_here, owners, capacity)
        returned, asked_here = fetch_rows(request, datastore)
        fetched = returned.reshape(owners * capacity, D)[target].reshape(seq_len, K, D)
    self_bias = jnp.concatenate([proj_bias[:, 0], jnp.zeros((D,), jnp.float32), proj_bias[:, 1]])
    self_proj = proj_weight[:, 0:3, :].reshape(D, 3 * D)
    joined = (product(tokens, self_proj) + self_bias).astype(jnp.bfloat16)
    queries = joined[:, :D].reshape(seq_len, H, HD)
    self_keys = joined[:, D : 2 * D].reshape(seq_len, H, HD)
    values = joined[:, 2 * D :].reshape(seq_len, H, HD)
    scores = self_scores(queries, self_keys, allowed, score_scale)
    self_lse = log_total(scores)
    self_probs = jnp.exp(scores - self_lse).astype(jnp.bfloat16)
    self_mixed = (
        jnp.einsum("hqk,khe->qhe", self_probs, values, preferred_element_type=jnp.float32)
        .reshape(seq_len, D)
        .astype(jnp.bfloat16)
    )
    first_pre = tokens.astype(jnp.float32) + (
        product(self_mixed, out_weight[:, 0, :]) + proj_bias[:, 2]
    )
    first_out, first_normed, first_inverse = norm_forward(
        first_pre, norm_gain[:, 0], norm_bias[:, 0]
    )
    first_low = first_out.astype(jnp.bfloat16)
    cross_query = (
        (product(first_low, proj_weight[:, 3, :]) + proj_bias[:, 3])
        .astype(jnp.bfloat16)
        .reshape(seq_len, H, HD)
    )
    key_heads = proj_weight[:, 4, :].reshape(D, H, HD)
    folded = (
        jnp.einsum("the,dhe->thd", cross_query, key_heads, preferred_element_type=jnp.float32)
        * score_scale
    ).astype(jnp.bfloat16)
    cross_scores = jnp.einsum("thd,tkd->thk", folded, fetched, preferred_element_type=jnp.float32)
    cross_lse = log_total(cross_scores)
    cross_full = jnp.exp(cross_scores - cross_lse)
    cross_probs = cross_full.astype(jnp.bfloat16)
    summary = jnp.einsum(
        "thk,tkd->thd", cross_probs, fetched, preferred_element_type=jnp.float32
    ).astype(jnp.bfloat16)
    value_heads = proj_weight[:, 5, :].reshape(D, H, HD)
    cross_mixed = (
        jnp.einsum(
            "thd,dhe->the", summary, value_heads, preferred_element_type=jnp.float32
        ).reshape(seq_len, D)
        + proj_bias[:, 4]
    ).astype(jnp.bfloat16)
    second_pre = first_out + (product(cross_mixed, out_weight[:, 1, :]) + proj_bias[:, 5])
    second_out, second_normed, second_inverse = norm_forward(
        second_pre, norm_gain[:, 1], norm_bias[:, 1]
    )
    second_low = second_out.astype(jnp.bfloat16)
    inner_pre = product(second_low, inner_weight) + inner_bias
    activated = jax.nn.gelu(inner_pre, approximate=False).astype(jnp.bfloat16)
    third_pre = second_out + (product(activated, outer_weight) + outer_bias)
    third_out, third_normed, third_inverse = norm_forward(
        third_pre, norm_gain[:, 2], norm_bias[:, 2]
    )
    output = jnp.where(valid, third_out, 0.0).astype(jnp.bfloat16)
    upstream = jnp.where(valid, cotangent.astype(jnp.float32), 0.0)
    third_grad, gain_three, shift_three = norm_backward(
        upstream, third_normed, third_inverse, norm_gain[:, 2]
    )
    outer_low = third_grad.astype(jnp.bfloat16)
    grad_outer_weight = contract_rows(activated, outer_low)
    grad_outer_bias = column_sum(outer_low)
    act_grad = product_back(outer_low, outer_weight)
    slope = jax.vjp(lambda activation_in: jax.nn.gelu(activation_in, approximate=False), inner_pre)[
        1
    ](act_grad)[0]
    inner_low = slope.astype(jnp.bfloat16)
    grad_inner_weight = contract_rows(second_low, inner_low)
    grad_inner_bias = column_sum(inner_low)
    second_up = third_grad + product_back(inner_low, inner_weight)
    second_grad, gain_two, shift_two = norm_backward(
        second_up, second_normed, second_inverse, norm_gain[:, 1]
    )
    cross_out_low = second_grad.astype(jnp.bfloat16)
    grad_cross_out = contract_rows(cross_mixed, cross_out_low)
    bias_five = column_sum(cross_out_low)
    mixed_low = product_back(cross_out_low, out_weight[:, 1, :]).astype(jnp.bfloat16)
    bias_four = column_sum(mixed_low)
    mixed_heads = mixed_low.reshape(seq_len, H, HD)
    grad_value_heads = jnp.einsum(
        "thd,the->dhe", summary, mixed_heads, preferred_element_type=jnp.float32
    )
    summary_low = jnp.einsum(
        "the,dhe->thd", mixed_heads, value_heads, preferred_element_type=jnp.float32
    ).astype(jnp.bfloat16)
    if dense:
        fetched_back = fetched
    else:
        returned_again, asked_back = fetch_again(request, datastore)
        fetched_back = returned_again.reshape(owners * capacity, D)[target].reshape(seq_len, K, D)
    prob_grad = jnp.einsum(
        "thd,tkd->thk", summary_low, fetched_back, preferred_element_type=jnp.float32
    )
    score_low = (
        cross_full * (prob_grad - jnp.sum(cross_full * prob_grad, axis=-1, keepdims=True))
    ).astype(jnp.bfloat16)
    row_grad = (
        jnp.einsum("thk,thd->tkd", cross_probs, summary_low, preferred_element_type=jnp.float32)
        + jnp.einsum("thk,thd->tkd", score_low, folded, preferred_element_type=jnp.float32)
    ).astype(jnp.bfloat16)
    folded_low = jnp.einsum(
        "thk,tkd->thd", score_low, fetched_back, preferred_element_type=jnp.float32
    ).astype(jnp.bfloat16)
    grad_key_heads = (
        jnp.einsum("thd,the->dhe", folded_low, cross_query, preferred_element_type=jnp.float32)
        * score_scale
    )
    query_low = (
        (
            jnp.einsum("thd,dhe->the", folded_low, key_heads, preferred_element_type=jnp.float32)
            * score_scale
        )
        .astype(jnp.bfloat16)
        .reshape(seq_len, D)
    )
    if dense:
        query_low, row_grad = lax.optimization_barrier((query_low, row_grad))
    bias_three = column_sum(query_low)
    grad_cross_query = contract_rows(first_low, query_low)
    if dense:
        grad_store = reduce_store(plan, row_grad, rows_here)
    else:
        grad_buffer = (
            jnp.zeros((owners * capacity, D), jnp.bfloat16)
            .at[target]
            .set(row_grad.reshape(-1, D))
            .reshape(owners, capacity, D)
        )
        arrived = lax.all_to_all(grad_buffer, "store", split_axis=0, concat_axis=0, tiled=True)
        partial_store = (
            jnp.zeros((rows_here, D), jnp.float32)
            .at[asked_back.reshape(-1)]
            .add(arrived.reshape(-1, D).astype(jnp.float32))
        )
        grad_store = lax.psum(partial_store.astype(jnp.bfloat16), "dp").astype(jnp.float32)
    first_up = second_grad + product_back(query_low, proj_weight[:, 3, :])
    first_grad, gain_one, shift_one = norm_backward(
        first_up, first_normed, first_inverse, norm_gain[:, 0]
    )
    self_out_low = first_grad.astype(jnp.bfloat16)
    grad_self_out = contract_rows(self_mixed, self_out_low)
    bias_two = column_sum(self_out_low)
    self_mixed_low = (
        product_back(self_out_low, out_weight[:, 0, :]).astype(jnp.bfloat16).reshape(seq_len, H, HD)
    )
    value_grad = jnp.einsum(
        "hqk,qhe->khe", self_probs, self_mixed_low, preferred_element_type=jnp.float32
    )
    attend_grad = jnp.einsum(
        "qhe,khe->hqk", self_mixed_low, values, preferred_element_type=jnp.float32
    )
    self_full = jnp.exp(self_scores(queries, self_keys, allowed, score_scale) - self_lse)
    self_score_low = (
        self_full * (attend_grad - jnp.sum(self_full * attend_grad, axis=-1, keepdims=True))
    ).astype(jnp.bfloat16)
    query_grad = (
        jnp.einsum("hqk,khe->qhe", self_score_low, self_keys, preferred_element_type=jnp.float32)
        * score_scale
    )
    key_grad = (
        jnp.einsum("hqk,qhe->khe", self_score_low, queries, preferred_element_type=jnp.float32)
        * score_scale
    )
    joined_low = jnp.concatenate(
        [
            query_grad.reshape(seq_len, D),
            key_grad.reshape(seq_len, D),
            value_grad.reshape(seq_len, D),
        ],
        axis=1,
    ).astype(jnp.bfloat16)
    grad_self_proj = contract_rows(tokens, joined_low).reshape(D, 3, D)
    bias_zero = column_sum(joined_low[:, :D])
    bias_one = column_sum(joined_low[:, 2 * D :])
    grad_tokens = (first_grad + product_back(joined_low, self_proj)).astype(jnp.bfloat16)
    if dense:
        squares = (
            grad_self_proj[:, 0],
            grad_self_proj[:, 1],
            grad_self_proj[:, 2],
            grad_cross_query,
            grad_key_heads.reshape(D, D),
            grad_value_heads.reshape(D, D),
            grad_self_out,
            grad_cross_out,
        )
        biases = (bias_zero, bias_one, bias_two, bias_three, bias_four, bias_five)
        gains = (gain_one, gain_two, gain_three)
        shifts = (shift_one, shift_two, shift_three)
        shares = reduce_weights(
            squares,
            grad_inner_weight,
            grad_outer_weight,
            biases + gains + shifts + (grad_outer_bias,),
            grad_inner_bias,
        )
        return (output, grad_tokens, grad_store) + shares
    grad_proj = jnp.stack(
        [
            grad_self_proj[:, 0],
            grad_self_proj[:, 1],
            grad_self_proj[:, 2],
            grad_cross_query,
            grad_key_heads.reshape(D, D),
            grad_value_heads.reshape(D, D),
        ],
        axis=1,
    )
    grad_out = jnp.stack([grad_self_out, grad_cross_out], axis=1)
    grad_bias = jnp.stack([bias_zero, bias_one, bias_two, bias_three, bias_four, bias_five], axis=1)
    grad_gain = jnp.stack([gain_one, gain_two, gain_three], axis=1)
    grad_shift = jnp.stack([shift_one, shift_two, shift_three], axis=1)
    shares = (
        lax.psum_scatter(
            grad_proj.astype(jnp.bfloat16), "store", scatter_dimension=0, tiled=True
        ).astype(jnp.float32),
        lax.psum_scatter(
            grad_out.astype(jnp.bfloat16), "store", scatter_dimension=0, tiled=True
        ).astype(jnp.float32),
        lax.psum_scatter(
            grad_bias.astype(jnp.bfloat16), "store", scatter_dimension=0, tiled=True
        ).astype(jnp.float32),
        lax.psum_scatter(
            grad_gain.astype(jnp.bfloat16), "store", scatter_dimension=0, tiled=True
        ).astype(jnp.float32),
        lax.psum_scatter(
            grad_shift.astype(jnp.bfloat16), "store", scatter_dimension=0, tiled=True
        ).astype(jnp.float32),
        lax.psum_scatter(
            grad_inner_weight.astype(jnp.bfloat16), "store", scatter_dimension=0, tiled=True
        ).astype(jnp.float32),
        lax.psum_scatter(
            grad_inner_bias.astype(jnp.bfloat16), "store", scatter_dimension=0, tiled=True
        ).astype(jnp.float32),
        lax.psum_scatter(
            grad_outer_weight.astype(jnp.bfloat16), "store", scatter_dimension=0, tiled=True
        ).astype(jnp.float32),
        lax.psum_scatter(
            grad_outer_bias.astype(jnp.bfloat16), "store", scatter_dimension=0, tiled=True
        ).astype(jnp.float32),
    )
    totals = (
        lax.psum(shares[0].astype(jnp.bfloat16), "dp").astype(jnp.float32),
        lax.psum(shares[1].astype(jnp.bfloat16), "dp").astype(jnp.float32),
        lax.psum(shares[2].astype(jnp.bfloat16), "dp").astype(jnp.float32),
        lax.psum(shares[3].astype(jnp.bfloat16), "dp").astype(jnp.float32),
        lax.psum(shares[4].astype(jnp.bfloat16), "dp").astype(jnp.float32),
        lax.psum(shares[5].astype(jnp.bfloat16), "dp").astype(jnp.float32),
        lax.psum(shares[6].astype(jnp.bfloat16), "dp").astype(jnp.float32),
        lax.psum(shares[7].astype(jnp.bfloat16), "dp").astype(jnp.float32),
        lax.psum(shares[8].astype(jnp.bfloat16), "dp").astype(jnp.float32),
    )
    return (
        output,
        grad_tokens,
        grad_store,
        totals[0],
        totals[1],
        totals[2],
        totals[3],
        totals[4],
        totals[5],
        totals[6],
        totals[7],
        totals[8],
    )


def solution(mesh):
    in_specs = (
        P(("dp", "store"), None),
        P("store", None),
        P(("dp", "store"), None),
        P(("dp", "store")),
        P(),
        P(),
        P(),
        P(),
        P(),
        P(),
        P(),
        P(),
        P(),
        P(("dp", "store"), None),
    )
    out_specs = (
        P(("dp", "store"), None),
        P(("dp", "store"), None),
        P("store", None),
        P("store", None, None),
        P("store", None, None),
        P("store", None),
        P("store", None),
        P("store", None),
        P("store", None),
        P("store"),
        P("store", None),
        P("store"),
    )
    return jax.shard_map(body, mesh=mesh, in_specs=in_specs, out_specs=out_specs, check_vma=False)
```

```python
import functools

import jax
import jax.numpy as jnp
from jax import lax
from jax.experimental import pallas as pl
from jax.experimental.pallas import tpu as pltpu
from jax.sharding import PartitionSpec as P


D = 768
H = 12
HD = 64
K = 16


EPSILON = 1e-05


def product(matrix, factor):
    return jnp.dot(matrix, factor, preferred_element_type=jnp.float32)


def product_back(matrix, weight):
    return jnp.einsum("tf,df->td", matrix, weight, preferred_element_type=jnp.float32)


def contract_rows(matrix, factor):
    return jnp.einsum("td,tf->df", matrix, factor, preferred_element_type=jnp.float32)


def column_sum(matrix):
    return jnp.sum(matrix.astype(jnp.float32), axis=0)


def norm_forward(hidden, norm_weight, norm_shift):
    centered = hidden - jnp.mean(hidden, axis=-1, keepdims=True)
    inverse = lax.rsqrt(jnp.mean(centered * centered, axis=-1, keepdims=True) + EPSILON)
    normed = centered * inverse
    return (normed * norm_weight + norm_shift, normed, inverse)


def norm_backward(upstream, normed, inverse, norm_weight):
    scaled = upstream * norm_weight
    plain_mean = jnp.mean(scaled, axis=-1, keepdims=True)
    normed_mean = jnp.mean(scaled * normed, axis=-1, keepdims=True)
    return (
        inverse * (scaled - plain_mean - normed * normed_mean),
        jnp.sum(upstream * normed, axis=0),
        jnp.sum(upstream, axis=0),
    )


def log_total(scores):
    highest = jnp.max(scores, axis=-1, keepdims=True)
    return highest + jnp.log(jnp.sum(jnp.exp(scores - highest), axis=-1, keepdims=True))


def route_slots(picked, rows_here, owners, capacity):
    flat_ids = picked.reshape(-1)
    owner_of = flat_ids // rows_here
    local_row = flat_ids % rows_here
    by_owner = jnp.argsort(owner_of, stable=True)
    sorted_owner = owner_of[by_owner]
    owner_loads = jnp.sum(
        (owner_of[:, None] == jnp.arange(owners, dtype=jnp.int32)[None, :]).astype(jnp.int32),
        axis=0,
    )
    starts = jnp.cumsum(owner_loads) - owner_loads
    within = jnp.arange(flat_ids.shape[0], dtype=jnp.int32) - starts[sorted_owner]
    placed = jnp.zeros_like(flat_ids).at[by_owner].set(within)
    target = owner_of * capacity + placed
    request = jnp.zeros((owners * capacity,), jnp.int32).at[target].set(local_row)
    return (target, request.reshape(owners, capacity))


def fetch_rows(request, datastore):
    asked_rows = lax.all_to_all(request, "store", split_axis=0, concat_axis=0, tiled=True)
    found_rows = datastore[asked_rows.reshape(-1)].reshape(asked_rows.shape + (datastore.shape[1],))
    return (
        lax.all_to_all(found_rows, "store", split_axis=0, concat_axis=0, tiled=True),
        asked_rows,
    )


def fetch_again(request, datastore):
    asked_rows = lax.all_to_all(request, "store", split_axis=0, concat_axis=0, tiled=True)
    found_rows = datastore[asked_rows.reshape(-1)].reshape(asked_rows.shape + (datastore.shape[1],))
    return (
        lax.all_to_all(found_rows, "store", split_axis=0, concat_axis=0, tiled=True),
        asked_rows,
    )


def self_scores(queries, self_keys, allowed, score_scale):
    scores = (
        jnp.einsum("qhe,khe->hqk", queries, self_keys, preferred_element_type=jnp.float32)
        * score_scale
    )
    return jnp.where(allowed[None], scores, -1e30)


DENSE_LIMIT = 1 << 16


def is_dense(owners, rows_here):
    fits = owners * rows_here <= DENSE_LIMIT and rows_here % (8 * CHUNK) == 0
    return fits and owners == 8 and lax.axis_size("dp") == 4


STORE_PARTS = 2


def fetch_dense(datastore, indices, plan):
    copies = lax.axis_size("dp")
    rows_here = datastore.shape[0]
    share = rows_here // copies
    part = share // STORE_PARTS
    flat = indices.reshape(-1)
    which = (flat % share) // part
    local = (flat // share) * part + flat % part
    start = lax.axis_index("dp") * share
    fetched = None
    earlier = None
    for index in range(STORE_PARTS):
        mine = lax.dynamic_slice_in_dim(datastore, start + index * part, part, axis=0)
        if earlier is not None:
            mine, earlier = lax.optimization_barrier((mine, earlier))
        table = lax.all_gather(mine, ("store", "dp"), axis=0, tiled=True)
        earlier = mine
        if index == STORE_PARTS - 1:
            which, plan = lax.optimization_barrier((which, plan))
        rows = table[local]
        if fetched is None:
            fetched = rows
        else:
            fetched = jnp.where((which == index)[:, None], rows, fetched)
    return fetched, plan


MESH_ID = pl.DeviceIdType.MESH
VMEM_LIMIT = 67043328
CHUNK = 64


GROUP = 8


SPLIT = D // 128


def scatter_kernel(steps, block, out_rows, row_ref, from_ref, twice_ref, groups_ref, own_ref, other_ref, *rest):
    outs, (total, wide) = rest[:-2], rest[-2:]
    step = pl.program_id(0)

    @pl.when(step == 0)
    def _():
        def clear(i, carry):
            total[pl.ds(i * 192, 192), :] = jnp.zeros((192, 128), jnp.float32)
            return carry

        lax.fori_loop(0, total.shape[0] // 192, clear, 0)

    def widen(ref):
        def strip(i, carry):
            first = pl.multiple_of(i * 32, 32)
            value = ref[pl.ds(first, 32), :].astype(jnp.float32)
            for part in range(SPLIT):
                wide[pl.ds(first * SPLIT + part, 32, stride=SPLIT), :] = value[:, part * 128 : (part + 1) * 128]
            return carry

        lax.fori_loop(0, block // 32, strip, 0)

    @pl.when(step < steps // 2)
    def _():
        widen(own_ref)

    @pl.when((step >= steps // 2) & (step < steps))
    def _():
        widen(other_ref)

    @pl.when(step < steps)
    def _():
        def group(i, carry):
            first = step * block + i * GROUP
            rows = [row_ref[first + k] for k in range(GROUP)]
            came = [from_ref[first + k] for k in range(GROUP)]
            twice = twice_ref[step * (block // GROUP) + i]

            @pl.when(twice == 0)
            def _():
                sums = [total[pl.ds(rows[k], SPLIT), :] + wide[pl.ds(came[k], SPLIT), :] for k in range(GROUP)]
                for k in range(GROUP):
                    total[pl.ds(rows[k], SPLIT), :] = sums[k]

            @pl.when(twice != 0)
            def _():
                for k in range(GROUP):
                    total[pl.ds(rows[k], SPLIT), :] = total[pl.ds(rows[k], SPLIT), :] + wide[pl.ds(came[k], SPLIT), :]

            return carry

        lax.fori_loop(0, groups_ref[step], group, 0)

    def narrow(out_ref):
        def strip(i, carry):
            first = pl.multiple_of((step - steps) * out_rows * SPLIT + i * (32 * SPLIT), 32 * SPLIT)
            for part in range(SPLIT):
                value = total[pl.ds(first + part, 32, stride=SPLIT), :]
                out_ref[pl.ds(pl.multiple_of(i * 32, 32), 32), part * 128 : (part + 1) * 128] = value.astype(jnp.bfloat16)
            return carry

        lax.fori_loop(0, out_rows // 32, strip, 0)

    quarter = (total.shape[0] // SPLIT // 4) // out_rows
    for index, out_ref in enumerate(outs):
        last = quarter * (index + 1 if index < 2 else 4)

        @pl.when((step >= steps + quarter * index) & (step < steps + last))
        def _(out_ref=out_ref):
            narrow(out_ref)


SCATTER_BLOCK = 1024


def scatter_plan(where, rows):
    keys = jnp.arange(where.shape[0], dtype=jnp.int32).reshape(-1, SCATTER_BLOCK) % SCATTER_BLOCK
    where = where.reshape(-1, SCATTER_BLOCK)
    skipped = where >= rows
    keys, where = lax.sort((jnp.where(skipped, keys + SCATTER_BLOCK, keys), where), dimension=1, num_keys=1)
    count = jnp.sum((~skipped).astype(jnp.int32), axis=1)
    groups = (count + GROUP - 1) // GROUP
    where = jnp.where(keys >= SCATTER_BLOCK, rows + keys % GROUP, where)
    spare = lax.broadcasted_iota(jnp.int32, where.shape, 1) % GROUP
    where = jnp.where(keys >= SCATTER_BLOCK, rows + spare, where)
    eights = where.reshape(-1, GROUP)
    twice = jnp.zeros((eights.shape[0],), jnp.int32)
    for shift in range(1, GROUP):
        same = eights[:, shift:] == eights[:, :-shift]
        twice = twice | jnp.any(same, axis=1).astype(jnp.int32)
    return SPLIT * where.reshape(-1), SPLIT * (keys % SCATTER_BLOCK).reshape(-1), twice, groups


def scatter_rows(plan, own, other, rows, out_rows=512):
    block = SCATTER_BLOCK
    half = own.shape[0] // block
    steps = 2 * half
    quarter = rows // 4 // out_rows

    def part(first, count):
        return pl.BlockSpec((out_rows, D), lambda i, *_: (jnp.clip(i - steps - first, 0, count - 1), 0))

    return pl.pallas_call(
        functools.partial(scatter_kernel, steps, block, out_rows),
        out_shape=[
            jax.ShapeDtypeStruct((rows // 4, D), jnp.bfloat16),
            jax.ShapeDtypeStruct((rows // 4, D), jnp.bfloat16),
            jax.ShapeDtypeStruct((rows // 2, D), jnp.bfloat16),
        ],
        grid_spec=pltpu.PrefetchScalarGridSpec(
            num_scalar_prefetch=4,
            grid=(steps + rows // out_rows,),
            in_specs=[
                pl.BlockSpec((block, D), lambda i, *_: (jnp.minimum(i, half - 1), 0)),
                pl.BlockSpec((block, D), lambda i, *_: (jnp.clip(i - half, 0, half - 1), 0)),
            ],
            out_specs=[part(0, quarter), part(quarter, quarter), part(2 * quarter, 2 * quarter)],
            scratch_shapes=[
                pltpu.VMEM(((rows + 32) * SPLIT, 128), jnp.float32),
                pltpu.VMEM((block * SPLIT, 128), jnp.float32),
            ],
        ),
        compiler_params=pltpu.CompilerParams(vmem_limit_bytes=VMEM_LIMIT),
        cost_estimate=pl.CostEstimate(flops=0, transcendentals=0, bytes_accessed=220_000_000),
        name="scatter_rows",
    )(*plan, own, other)


def reduce_kernel(chunks, keep_ref, came_a, came_b, out_ref, keep_a, keep_b, one_a, one_b, two_a, two_b, layer, along, done,
                  keep_sem, two_send, two_recv, z_send, z_recv,
                  own_sem, y_send, y_recv, core_send, core_recv, pass_send, pass_recv):
    dp = lax.axis_index("dp")
    store = lax.axis_index("store")
    y, core = lax.div(dp, 2), lax.rem(dp, 2)
    z, x = lax.div(store, 2), lax.rem(store, 2)
    x_peer = (dp, z * 2 + (1 - x))
    y_peer = ((1 - y) * 2 + core, store)
    core_peer = (y * 2 + (1 - core), store)
    z_of = [lax.rem(z + hop, 4) for hop in range(4)]
    z_peer = [(dp, z_of[hop] * 2 + x) for hop in range(4)]

    barrier = pltpu.get_barrier_semaphore()
    for peer in (x_peer, y_peer, core_peer, z_peer[1], z_peer[2], z_peer[3]):
        pl.semaphore_signal(barrier, inc=1, device_id=peer, device_id_type=MESH_ID)
    pl.semaphore_wait(barrier, 6)

    def remote(src, dst, send, recv, peer):
        return pltpu.make_async_remote_copy(src_ref=src, dst_ref=dst, send_sem=send, recv_sem=recv,
                                            device_id=peer, device_id_type=MESH_ID)

    keeps = [(
        pltpu.make_async_copy(keep_ref.at[0, :, :, q], keep_a.at[q], keep_sem.at[0, q]),
        pltpu.make_async_copy(keep_ref.at[1, :, :, q], keep_b.at[q], keep_sem.at[1, q]),
        pltpu.make_async_copy(came_a.at[:, :, q], one_a.at[q], keep_sem.at[2, q]),
        pltpu.make_async_copy(came_b.at[:, :, q], one_b.at[q], keep_sem.at[3, q]),
    ) for q in range(chunks)]
    twos = [(
        remote(keep_a.at[q, :, 1 - y], two_a.at[q], two_send.at[0, q], two_recv.at[0, q], y_peer),
        remote(keep_b.at[q, :, 1 - x], two_b.at[q], two_send.at[1, q], two_recv.at[1, q], x_peer),
    ) for q in range(chunks)]
    zs = [[
        remote(layer.at[q, z_of[hop]], along.at[q, hop - 1], z_send.at[hop - 1, q], z_recv.at[hop - 1, q], z_peer[hop])
        for hop in (1, 2, 3)] for q in range(chunks)]
    own = [pltpu.make_async_copy(done.at[q], out_ref.at[core, y, :, q], own_sem.at[q]) for q in range(chunks)]
    to_y = [remote(done.at[q], out_ref.at[core, y, :, q], y_send.at[q], y_recv.at[q], y_peer) for q in range(chunks)]
    to_core = [remote(done.at[q], out_ref.at[core, y, :, q], core_send.at[q], core_recv.at[q], core_peer) for q in range(chunks)]
    passed = [remote(out_ref.at[core, 1 - y, :, q], out_ref.at[core, 1 - y, :, q], pass_send.at[q], pass_recv.at[q], core_peer)
              for q in range(chunks)]

    def plus(first, second):
        return (first.astype(jnp.float32) + second.astype(jnp.float32)).astype(jnp.bfloat16)

    for q in range(chunks):
        for copy in keeps[q]:
            copy.start()
    for step in range(chunks + 3):
        q = step
        if q < chunks:
            for copy in keeps[q]:
                copy.wait()

            def merge(i, carry, q=q):
                for half in range(2):
                    keep_a[q, i, half] = plus(keep_a[q, i, half], one_a[q, i, half])
                    keep_b[q, i, half] = plus(keep_b[q, i, half], one_b[q, i, half])
                return carry

            lax.fori_loop(0, 4, merge, 0)
            for copy in twos[q]:
                copy.start()
        q = step - 1
        if 0 <= q < chunks:
            for copy in twos[q]:
                copy.wait_recv()

            def merge_two(i, carry, q=q):
                layer[q, i, 0] = plus(keep_a[q, i, y], two_a[q, i])
                layer[q, i, 1] = plus(keep_b[q, i, x], two_b[q, i])
                return carry

            lax.fori_loop(0, 4, merge_two, 0)
            for copy in zs[q]:
                copy.start()
        q = step - 2
        if 0 <= q < chunks:
            for copy in zs[q]:
                copy.wait_recv()

            def finish(i, carry, q=q):
                value = layer[q, z, i].astype(jnp.float32)
                for hop in range(3):
                    value = value + along[q, hop, i].astype(jnp.float32)
                done[q, i] = value.astype(jnp.bfloat16)
                return carry

            lax.fori_loop(0, 2, finish, 0)
            for copy in (own[q], to_y[q], to_core[q]):
                copy.start()
        q = step - 3
        if 0 <= q < chunks:
            to_y[q].wait_recv()
            passed[q].start()
    for q in range(chunks):
        for copy in twos[q] + tuple(zs[q]):
            copy.wait_send()
        own[q].wait()
        to_y[q].wait_send()
        to_core[q].wait()
        passed[q].wait()


def reduce_rows(keep, came_a, came_b, collective_id=0):
    rows = keep.shape[0] // 4
    chunks = rows // (4 * CHUNK)
    dma = pltpu.SemaphoreType.DMA
    vm = lambda *lead: pltpu.VMEM(lead + (CHUNK, D), jnp.bfloat16)
    out = pl.pallas_call(
        functools.partial(reduce_kernel, chunks),
        out_shape=jax.ShapeDtypeStruct((2, 2, 2, chunks, CHUNK, D), jnp.bfloat16),
        in_specs=[pl.BlockSpec(memory_space=pl.ANY)] * 3,
        out_specs=pl.BlockSpec(memory_space=pl.ANY),
        scratch_shapes=[
            vm(chunks, 4, 2), vm(chunks, 4, 2), vm(chunks, 4, 2), vm(chunks, 4, 2),
            vm(chunks, 4), vm(chunks, 4), vm(chunks, 4, 2), vm(chunks, 3, 2), vm(chunks, 2),
            dma((4, chunks)), dma((2, chunks)), dma((2, chunks)),
            dma((3, chunks)), dma((3, chunks)),
            dma((chunks,)), dma((chunks,)), dma((chunks,)), dma((chunks,)), dma((chunks,)), dma((chunks,)), dma((chunks,)),
        ],
        compiler_params=pltpu.CompilerParams(collective_id=collective_id, has_side_effects=True, vmem_limit_bytes=VMEM_LIMIT),
        cost_estimate=pl.CostEstimate(flops=0, transcendentals=0, bytes_accessed=450_000_000),
        name="reduce_rows",
    )(
        keep.reshape(2, 4, 2, chunks, CHUNK, D),
        came_a.reshape(4, 2, chunks, CHUNK, D),
        came_b.reshape(4, 2, chunks, CHUNK, D),
    )
    return out.reshape(2 * rows, D)


PAIRS = ((0, 1), (1, 0), (2, 3), (3, 2))


def own_rows(flat, rows_here):
    half = rows_here // 2
    quarter = half // 4
    dp = lax.axis_index("dp")
    here_y, core = dp // 2, dp % 2
    here_x = lax.axis_index("store") % 2
    owner, local = flat // rows_here, flat % rows_here
    z, x = owner // 2, owner % 2
    y = (local % half) // (2 * quarter)
    second = (local // quarter) % 2
    stays = jnp.where(second == 0, x == here_x, y == here_y)
    pair = jnp.where(second == 0, y, x)
    rows = 8 * half
    target = (2 * stays + second) * (rows // 4) + (2 * z + pair) * quarter + local % quarter
    return jnp.where(local // half == core, target, rows)


def plan_store(indices, rows_here):
    flat = indices.reshape(-1)
    other = lax.ppermute(flat, "dp", PAIRS)
    where = jnp.concatenate([own_rows(flat, rows_here), own_rows(other, rows_here)])
    return scatter_plan(where, lax.axis_size("store") * rows_here // 2)


def add_store(plan, own, other, rows_here):
    return scatter_rows(plan, own, other, lax.axis_size("store") * rows_here // 2)


def swap_store(send_a, send_b):
    owners = lax.axis_size("store")
    came_a = lax.ppermute(send_a, "store", [(i, i ^ 1) for i in range(owners)])
    came_b = lax.ppermute(send_b, "dp", [(i, i ^ 2) for i in range(4)])
    return came_a, came_b


def by_owner(matrix):
    owners = lax.axis_size("store")
    return matrix.astype(jnp.bfloat16).reshape(owners, -1, D)


def reduce_packed(packed):
    return lax.psum_scatter(
        packed.reshape(-1, D), ("store", "dp"), scatter_dimension=0, tiled=True
    )


def all_copies(first, second):
    split = first.shape[0]
    total = lax.all_gather(jnp.concatenate([first, second]), "dp", axis=0, tiled=False)
    total = total.astype(jnp.float32)
    return total[:, :split].reshape(-1, D), total[:, split:].reshape(-1, D)


def pack_early(inner, outer, squares):
    blocks = [inner[:, block * D : (block + 1) * D] for block in range(inner.shape[1] // D)]
    return jnp.concatenate([by_owner(piece) for piece in blocks + [outer] + list(squares)], axis=1)


def unpack_early(total, wide):
    part = D // lax.axis_size("store")
    inner_total = jnp.transpose(total[: wide * part].reshape(wide, part, D), (1, 0, 2))
    rest = total[wide * part :]
    return (
        inner_total.reshape(part, wide * D),
        rest[: wide * part],
        rest[wide * part :].reshape(-1, part, D),
    )


def pack_late(squares, features, inner_bias):
    owners = lax.axis_size("store")
    part = D // owners
    wide = inner_bias.shape[0] // D
    small = jnp.concatenate(
        [feature.astype(jnp.bfloat16).reshape(owners, part) for feature in features]
        + [inner_bias.astype(jnp.bfloat16).reshape(owners, wide * part)],
        axis=1,
    )
    small = jnp.pad(small, ((0, 0), (0, 64 * D - small.shape[1]))).reshape(owners, 64, D)
    return jnp.concatenate([by_owner(square) for square in squares] + [small], axis=1)


def unpack_late(total, count, features, wide):
    part = D // lax.axis_size("store")
    tail = total[count * part :].reshape(-1)
    table = tail[: features * part].reshape(features, part)
    return (
        total[: count * part].reshape(count, part, D),
        table,
        tail[features * part :][: wide * part],
    )


def body(
    tokens,
    datastore,
    indices,
    lengths,
    proj_weight,
    out_weight,
    proj_bias,
    norm_gain,
    norm_bias,
    inner_weight,
    inner_bias,
    outer_weight,
    outer_bias,
    cotangent,
):
    seq_len = tokens.shape[0]
    score_scale = HD ** (-0.5)
    owners = lax.axis_size("store")
    rows_here = datastore.shape[0]
    capacity = 2 * seq_len * K // owners
    position = jnp.arange(seq_len)
    length = lengths[0]
    allowed = (position[None, :] <= position[:, None]) & (position[None, :] < length)
    valid = (position < length)[:, None]
    dense = is_dense(owners, rows_here)
    if dense:
        plan = plan_store(indices, rows_here)
        fetched, plan = fetch_dense(datastore, indices, plan)
        fetched = fetched.reshape(seq_len, K, D)
    else:
        target, request = route_slots(indices, rows_here, owners, capacity)
        returned, _ = fetch_rows(request, datastore)
        fetched = returned.reshape(owners * capacity, D)[target].reshape(seq_len, K, D)
    self_bias = jnp.concatenate([proj_bias[:, 0], jnp.zeros((D,), jnp.float32), proj_bias[:, 1]])
    self_proj = proj_weight[:, 0:3, :].reshape(D, 3 * D)
    joined = (product(tokens, self_proj) + self_bias).astype(jnp.bfloat16)
    queries = joined[:, :D].reshape(seq_len, H, HD)
    self_keys = joined[:, D : 2 * D].reshape(seq_len, H, HD)
    values = joined[:, 2 * D :].reshape(seq_len, H, HD)
    scores = self_scores(queries, self_keys, allowed, score_scale)
    self_lse = log_total(scores)
    self_probs = jnp.exp(scores - self_lse).astype(jnp.bfloat16)
    self_mixed = (
        jnp.einsum("hqk,khe->qhe", self_probs, values, preferred_element_type=jnp.float32)
        .reshape(seq_len, D)
        .astype(jnp.bfloat16)
    )
    first_pre = tokens.astype(jnp.float32) + (
        product(self_mixed, out_weight[:, 0, :]) + proj_bias[:, 2]
    )
    first_out, first_normed, first_inverse = norm_forward(
        first_pre, norm_gain[:, 0], norm_bias[:, 0]
    )
    first_low = first_out.astype(jnp.bfloat16)
    cross_query = (
        (product(first_low, proj_weight[:, 3, :]) + proj_bias[:, 3])
        .astype(jnp.bfloat16)
        .reshape(seq_len, H, HD)
    )
    key_heads = proj_weight[:, 4, :].reshape(D, H, HD)
    folded = (
        jnp.einsum("the,dhe->thd", cross_query, key_heads, preferred_element_type=jnp.float32)
        * score_scale
    ).astype(jnp.bfloat16)
    cross_scores = jnp.einsum("thd,tkd->thk", folded, fetched, preferred_element_type=jnp.float32)
    cross_lse = log_total(cross_scores)
    cross_full = jnp.exp(cross_scores - cross_lse)
    cross_probs = cross_full.astype(jnp.bfloat16)
    summary = jnp.einsum(
        "thk,tkd->thd", cross_probs, fetched, preferred_element_type=jnp.float32
    ).astype(jnp.bfloat16)
    value_heads = proj_weight[:, 5, :].reshape(D, H, HD)
    cross_mixed = (
        jnp.einsum(
            "thd,dhe->the", summary, value_heads, preferred_element_type=jnp.float32
        ).reshape(seq_len, D)
        + proj_bias[:, 4]
    ).astype(jnp.bfloat16)
    second_pre = first_out + (product(cross_mixed, out_weight[:, 1, :]) + proj_bias[:, 5])
    second_out, second_normed, second_inverse = norm_forward(
        second_pre, norm_gain[:, 1], norm_bias[:, 1]
    )
    second_low = second_out.astype(jnp.bfloat16)
    inner_pre = product(second_low, inner_weight) + inner_bias
    activated = jax.nn.gelu(inner_pre, approximate=False).astype(jnp.bfloat16)
    third_pre = second_out + (product(activated, outer_weight) + outer_bias)
    third_out, third_normed, third_inverse = norm_forward(
        third_pre, norm_gain[:, 2], norm_bias[:, 2]
    )
    output = jnp.where(valid, third_out, 0.0).astype(jnp.bfloat16)
    upstream = jnp.where(valid, cotangent.astype(jnp.float32), 0.0)
    third_grad, gain_three, shift_three = norm_backward(
        upstream, third_normed, third_inverse, norm_gain[:, 2]
    )
    outer_low = third_grad.astype(jnp.bfloat16)
    grad_outer_weight = contract_rows(activated, outer_low)
    grad_outer_bias = column_sum(outer_low)
    act_grad = product_back(outer_low, outer_weight)
    slope = jax.vjp(lambda activation_in: jax.nn.gelu(activation_in, approximate=False), inner_pre)[
        1
    ](act_grad)[0]
    inner_low = slope.astype(jnp.bfloat16)
    grad_inner_weight = contract_rows(second_low, inner_low)
    grad_inner_bias = column_sum(inner_low)
    second_up = third_grad + product_back(inner_low, inner_weight)
    second_grad, gain_two, shift_two = norm_backward(
        second_up, second_normed, second_inverse, norm_gain[:, 1]
    )
    cross_out_low = second_grad.astype(jnp.bfloat16)
    grad_cross_out = contract_rows(cross_mixed, cross_out_low)
    bias_five = column_sum(cross_out_low)
    mixed_low = product_back(cross_out_low, out_weight[:, 1, :]).astype(jnp.bfloat16)
    bias_four = column_sum(mixed_low)
    mixed_heads = mixed_low.reshape(seq_len, H, HD)
    grad_value_heads = jnp.einsum(
        "thd,the->dhe", summary, mixed_heads, preferred_element_type=jnp.float32
    )
    if dense:
        packed_early = pack_early(
            grad_inner_weight,
            grad_outer_weight,
            (grad_value_heads.reshape(D, D), grad_cross_out),
        )
        mixed_heads, packed_early = lax.optimization_barrier((mixed_heads, packed_early))
        share_early = reduce_packed(packed_early)
    summary_low = jnp.einsum(
        "the,dhe->thd", mixed_heads, value_heads, preferred_element_type=jnp.float32
    ).astype(jnp.bfloat16)
    if dense:
        fetched_back = fetched
    else:
        returned_again, asked_back = fetch_again(request, datastore)
        fetched_back = returned_again.reshape(owners * capacity, D)[target].reshape(seq_len, K, D)
    prob_grad = jnp.einsum(
        "thd,tkd->thk", summary_low, fetched_back, preferred_element_type=jnp.float32
    )
    score_low = (
        cross_full * (prob_grad - jnp.sum(cross_full * prob_grad, axis=-1, keepdims=True))
    ).astype(jnp.bfloat16)
    row_grad = (
        jnp.einsum("thk,thd->tkd", cross_probs, summary_low, preferred_element_type=jnp.float32)
        + jnp.einsum("thk,thd->tkd", score_low, folded, preferred_element_type=jnp.float32)
    ).astype(jnp.bfloat16)
    if dense:
        score_low, row_grad = lax.optimization_barrier((score_low, row_grad))
        own_grad = row_grad.reshape(-1, D)
        other_grad = lax.ppermute(own_grad, "dp", PAIRS)
    folded_low = jnp.einsum(
        "thk,tkd->thd", score_low, fetched_back, preferred_element_type=jnp.float32
    ).astype(jnp.bfloat16)
    grad_key_heads = (
        jnp.einsum("thd,the->dhe", folded_low, cross_query, preferred_element_type=jnp.float32)
        * score_scale
    )
    query_low = (
        (
            jnp.einsum("thd,dhe->the", folded_low, key_heads, preferred_element_type=jnp.float32)
            * score_scale
        )
        .astype(jnp.bfloat16)
        .reshape(seq_len, D)
    )
    if dense:
        query_low, other_grad = lax.optimization_barrier((query_low, other_grad))
        send_a, send_b, keep = add_store(plan, own_grad, other_grad, rows_here)
        query_low, send_a, send_b, keep = lax.optimization_barrier(
            (query_low, send_a, send_b, keep)
        )
        came_a, came_b = swap_store(send_a, send_b)
    bias_three = column_sum(query_low)
    grad_cross_query = contract_rows(first_low, query_low)
    if not dense:
        grad_buffer = (
            jnp.zeros((owners * capacity, D), jnp.bfloat16)
            .at[target]
            .set(row_grad.reshape(-1, D))
            .reshape(owners, capacity, D)
        )
        arrived = lax.all_to_all(grad_buffer, "store", split_axis=0, concat_axis=0, tiled=True)
        partial_store = (
            jnp.zeros((rows_here, D), jnp.float32)
            .at[asked_back.reshape(-1)]
            .add(arrived.reshape(-1, D).astype(jnp.float32))
        )
        grad_store = lax.psum(partial_store.astype(jnp.bfloat16), "dp").astype(jnp.float32)
    first_up = second_grad + product_back(query_low, proj_weight[:, 3, :])
    first_grad, gain_one, shift_one = norm_backward(
        first_up, first_normed, first_inverse, norm_gain[:, 0]
    )
    self_out_low = first_grad.astype(jnp.bfloat16)
    grad_self_out = contract_rows(self_mixed, self_out_low)
    bias_two = column_sum(self_out_low)
    self_mixed_low = (
        product_back(self_out_low, out_weight[:, 0, :]).astype(jnp.bfloat16).reshape(seq_len, H, HD)
    )
    value_grad = jnp.einsum(
        "hqk,qhe->khe", self_probs, self_mixed_low, preferred_element_type=jnp.float32
    )
    attend_grad = jnp.einsum(
        "qhe,khe->hqk", self_mixed_low, values, preferred_element_type=jnp.float32
    )
    self_full = jnp.exp(self_scores(queries, self_keys, allowed, score_scale) - self_lse)
    self_score_low = (
        self_full * (attend_grad - jnp.sum(self_full * attend_grad, axis=-1, keepdims=True))
    ).astype(jnp.bfloat16)
    query_grad = (
        jnp.einsum("hqk,khe->qhe", self_score_low, self_keys, preferred_element_type=jnp.float32)
        * score_scale
    )
    key_grad = (
        jnp.einsum("hqk,qhe->khe", self_score_low, queries, preferred_element_type=jnp.float32)
        * score_scale
    )
    joined_low = jnp.concatenate(
        [
            query_grad.reshape(seq_len, D),
            key_grad.reshape(seq_len, D),
            value_grad.reshape(seq_len, D),
        ],
        axis=1,
    ).astype(jnp.bfloat16)
    grad_self_proj = contract_rows(tokens, joined_low).reshape(D, 3, D)
    bias_zero = column_sum(joined_low[:, :D])
    bias_one = column_sum(joined_low[:, 2 * D :])
    grad_tokens = (first_grad + product_back(joined_low, self_proj)).astype(jnp.bfloat16)
    if dense:
        packed_late = pack_late(
            (
                grad_self_proj[:, 0],
                grad_self_proj[:, 1],
                grad_self_proj[:, 2],
                grad_cross_query,
                grad_key_heads.reshape(D, D),
                grad_self_out,
            ),
            (bias_zero, bias_one, bias_two, bias_three, bias_four, bias_five)
            + (gain_one, gain_two, gain_three)
            + (shift_one, shift_two, shift_three)
            + (grad_outer_bias,),
            grad_inner_bias,
        )
        share_late = reduce_packed(packed_late)
        keep, came_a, came_b, share_early = lax.optimization_barrier(
            (keep, came_a, came_b, share_early)
        )
        grad_store = reduce_rows(keep, came_a, came_b).astype(jnp.float32)
        wide = grad_inner_bias.shape[0] // D
        total_early, total_late = all_copies(share_early, share_late)
        inner_total, outer_total, early = unpack_early(total_early, wide)
        late, table, bias_inner = unpack_late(total_late, 6, 13, wide)
        return (
            output,
            grad_tokens,
            grad_store,
            jnp.stack([late[0], late[1], late[2], late[3], late[4], early[0]], axis=1),
            jnp.stack([late[5], early[1]], axis=1),
            jnp.transpose(table[0:6]),
            jnp.transpose(table[6:9]),
            jnp.transpose(table[9:12]),
            inner_total,
            bias_inner,
            outer_total,
            table[12],
        )
    grad_proj = jnp.stack(
        [
            grad_self_proj[:, 0],
            grad_self_proj[:, 1],
            grad_self_proj[:, 2],
            grad_cross_query,
            grad_key_heads.reshape(D, D),
            grad_value_heads.reshape(D, D),
        ],
        axis=1,
    )
    grad_out = jnp.stack([grad_self_out, grad_cross_out], axis=1)
    grad_bias = jnp.stack([bias_zero, bias_one, bias_two, bias_three, bias_four, bias_five], axis=1)
    grad_gain = jnp.stack([gain_one, gain_two, gain_three], axis=1)
    grad_shift = jnp.stack([shift_one, shift_two, shift_three], axis=1)
    shares = (
        lax.psum_scatter(
            grad_proj.astype(jnp.bfloat16), "store", scatter_dimension=0, tiled=True
        ).astype(jnp.float32),
        lax.psum_scatter(
            grad_out.astype(jnp.bfloat16), "store", scatter_dimension=0, tiled=True
        ).astype(jnp.float32),
        lax.psum_scatter(
            grad_bias.astype(jnp.bfloat16), "store", scatter_dimension=0, tiled=True
        ).astype(jnp.float32),
        lax.psum_scatter(
            grad_gain.astype(jnp.bfloat16), "store", scatter_dimension=0, tiled=True
        ).astype(jnp.float32),
        lax.psum_scatter(
            grad_shift.astype(jnp.bfloat16), "store", scatter_dimension=0, tiled=True
        ).astype(jnp.float32),
        lax.psum_scatter(
            grad_inner_weight.astype(jnp.bfloat16), "store", scatter_dimension=0, tiled=True
        ).astype(jnp.float32),
        lax.psum_scatter(
            grad_inner_bias.astype(jnp.bfloat16), "store", scatter_dimension=0, tiled=True
        ).astype(jnp.float32),
        lax.psum_scatter(
            grad_outer_weight.astype(jnp.bfloat16), "store", scatter_dimension=0, tiled=True
        ).astype(jnp.float32),
        lax.psum_scatter(
            grad_outer_bias.astype(jnp.bfloat16), "store", scatter_dimension=0, tiled=True
        ).astype(jnp.float32),
    )
    totals = (
        lax.psum(shares[0].astype(jnp.bfloat16), "dp").astype(jnp.float32),
        lax.psum(shares[1].astype(jnp.bfloat16), "dp").astype(jnp.float32),
        lax.psum(shares[2].astype(jnp.bfloat16), "dp").astype(jnp.float32),
        lax.psum(shares[3].astype(jnp.bfloat16), "dp").astype(jnp.float32),
        lax.psum(shares[4].astype(jnp.bfloat16), "dp").astype(jnp.float32),
        lax.psum(shares[5].astype(jnp.bfloat16), "dp").astype(jnp.float32),
        lax.psum(shares[6].astype(jnp.bfloat16), "dp").astype(jnp.float32),
        lax.psum(shares[7].astype(jnp.bfloat16), "dp").astype(jnp.float32),
        lax.psum(shares[8].astype(jnp.bfloat16), "dp").astype(jnp.float32),
    )
    return (
        output,
        grad_tokens,
        grad_store,
        totals[0],
        totals[1],
        totals[2],
        totals[3],
        totals[4],
        totals[5],
        totals[6],
        totals[7],
        totals[8],
    )


def solution(mesh):
    in_specs = (
        P(("dp", "store"), None),
        P("store", None),
        P(("dp", "store"), None),
        P(("dp", "store")),
        P(),
        P(),
        P(),
        P(),
        P(),
        P(),
        P(),
        P(),
        P(),
        P(("dp", "store"), None),
    )
    out_specs = (
        P(("dp", "store"), None),
        P(("dp", "store"), None),
        P("store", None),
        P("store", None, None),
        P("store", None, None),
        P("store", None),
        P("store", None),
        P("store", None),
        P("store", None),
        P("store"),
        P("store", None),
        P("store"),
    )

    return jax.shard_map(body, mesh=mesh, in_specs=in_specs, out_specs=out_specs, check_vma=False)
```

```python
import functools

import jax
import jax.numpy as jnp
from jax import lax
from jax.experimental import pallas as pl
from jax.experimental.pallas import tpu as pltpu
from jax.sharding import PartitionSpec as P


D = 768
H = 12
HD = 64
K = 16


EPSILON = 1e-05


def product(matrix, factor):
    return jnp.dot(matrix, factor, preferred_element_type=jnp.float32)


def product_back(matrix, weight):
    return jnp.einsum("tf,df->td", matrix, weight, preferred_element_type=jnp.float32)


def contract_rows(matrix, factor):
    return jnp.einsum("td,tf->df", matrix, factor, preferred_element_type=jnp.float32)


def column_sum(matrix):
    return jnp.sum(matrix.astype(jnp.float32), axis=0)


def norm_forward(hidden, norm_weight, norm_shift):
    centered = hidden - jnp.mean(hidden, axis=-1, keepdims=True)
    inverse = lax.rsqrt(jnp.mean(centered * centered, axis=-1, keepdims=True) + EPSILON)
    normed = centered * inverse
    return (normed * norm_weight + norm_shift, normed, inverse)


def norm_backward(upstream, normed, inverse, norm_weight):
    scaled = upstream * norm_weight
    plain_mean = jnp.mean(scaled, axis=-1, keepdims=True)
    normed_mean = jnp.mean(scaled * normed, axis=-1, keepdims=True)
    return (
        inverse * (scaled - plain_mean - normed * normed_mean),
        jnp.sum(upstream * normed, axis=0),
        jnp.sum(upstream, axis=0),
    )


def log_total(scores):
    highest = jnp.max(scores, axis=-1, keepdims=True)
    return highest + jnp.log(jnp.sum(jnp.exp(scores - highest), axis=-1, keepdims=True))


def route_slots(picked, rows_here, owners, capacity):
    flat_ids = picked.reshape(-1)
    owner_of = flat_ids // rows_here
    local_row = flat_ids % rows_here
    by_owner = jnp.argsort(owner_of, stable=True)
    sorted_owner = owner_of[by_owner]
    owner_loads = jnp.sum(
        (owner_of[:, None] == jnp.arange(owners, dtype=jnp.int32)[None, :]).astype(jnp.int32),
        axis=0,
    )
    starts = jnp.cumsum(owner_loads) - owner_loads
    within = jnp.arange(flat_ids.shape[0], dtype=jnp.int32) - starts[sorted_owner]
    placed = jnp.zeros_like(flat_ids).at[by_owner].set(within)
    target = owner_of * capacity + placed
    request = jnp.zeros((owners * capacity,), jnp.int32).at[target].set(local_row)
    return (target, request.reshape(owners, capacity))


def fetch_rows(request, datastore):
    asked_rows = lax.all_to_all(request, "store", split_axis=0, concat_axis=0, tiled=True)
    found_rows = datastore[asked_rows.reshape(-1)].reshape(asked_rows.shape + (datastore.shape[1],))
    return (
        lax.all_to_all(found_rows, "store", split_axis=0, concat_axis=0, tiled=True),
        asked_rows,
    )


def fetch_again(request, datastore):
    asked_rows = lax.all_to_all(request, "store", split_axis=0, concat_axis=0, tiled=True)
    found_rows = datastore[asked_rows.reshape(-1)].reshape(asked_rows.shape + (datastore.shape[1],))
    return (
        lax.all_to_all(found_rows, "store", split_axis=0, concat_axis=0, tiled=True),
        asked_rows,
    )


def self_scores(queries, self_keys, allowed, score_scale):
    scores = (
        jnp.einsum("qhe,khe->hqk", queries, self_keys, preferred_element_type=jnp.float32)
        * score_scale
    )
    return jnp.where(allowed[None], scores, -1e30)


DENSE_LIMIT = 1 << 16


def is_dense(owners, rows_here):
    fits = owners * rows_here <= DENSE_LIMIT and rows_here % (8 * CHUNK) == 0
    return fits and owners == 8 and lax.axis_size("dp") == 4


STORE_PARTS = 2


def fetch_dense(datastore, indices, plan):
    copies = lax.axis_size("dp")
    rows_here = datastore.shape[0]
    share = rows_here // copies
    part = share // STORE_PARTS
    flat = indices.reshape(-1)
    which = (flat % share) // part
    local = (flat // share) * part + flat % part
    start = lax.axis_index("dp") * share
    found = []
    earlier = None
    for index in range(STORE_PARTS):
        mine = lax.dynamic_slice_in_dim(datastore, start + index * part, part, axis=0)
        if earlier is not None:
            mine, earlier = lax.optimization_barrier((mine, earlier))
        table = lax.all_gather(mine, ("store", "dp"), axis=0, tiled=True)
        earlier = mine
        if index == STORE_PARTS - 1:
            which, plan = lax.optimization_barrier((which, plan))
        found.append(table[local])
    return found[0], found[1], which[:, None], plan


MESH_ID = pl.DeviceIdType.MESH
VMEM_LIMIT = 67043328
CHUNK = 64


GROUP = 8


SPLIT = D // 128


def scatter_kernel(steps, block, out_rows, row_ref, from_ref, twice_ref, groups_ref, own_ref, other_ref, *rest):
    outs, (total, wide) = rest[:-2], rest[-2:]
    step = pl.program_id(0)

    @pl.when(step == 0)
    def _():
        def clear(i, carry):
            total[pl.ds(i * 192, 192), :] = jnp.zeros((192, 128), jnp.float32)
            return carry

        lax.fori_loop(0, total.shape[0] // 192, clear, 0)

    def widen(ref):
        def strip(i, carry):
            first = pl.multiple_of(i * 32, 32)
            value = ref[pl.ds(first, 32), :].astype(jnp.float32)
            for part in range(SPLIT):
                wide[pl.ds(first * SPLIT + part, 32, stride=SPLIT), :] = value[:, part * 128 : (part + 1) * 128]
            return carry

        lax.fori_loop(0, block // 32, strip, 0)

    @pl.when(step < steps // 2)
    def _():
        widen(own_ref)

    @pl.when((step >= steps // 2) & (step < steps))
    def _():
        widen(other_ref)

    @pl.when(step < steps)
    def _():
        def group(i, carry):
            first = step * block + i * GROUP
            rows = [row_ref[first + k] for k in range(GROUP)]
            came = [from_ref[first + k] for k in range(GROUP)]
            twice = twice_ref[step * (block // GROUP) + i]

            @pl.when(twice == 0)
            def _():
                sums = [total[pl.ds(rows[k], SPLIT), :] + wide[pl.ds(came[k], SPLIT), :] for k in range(GROUP)]
                for k in range(GROUP):
                    total[pl.ds(rows[k], SPLIT), :] = sums[k]

            @pl.when(twice != 0)
            def _():
                for k in range(GROUP):
                    total[pl.ds(rows[k], SPLIT), :] = total[pl.ds(rows[k], SPLIT), :] + wide[pl.ds(came[k], SPLIT), :]

            return carry

        lax.fori_loop(0, groups_ref[step], group, 0)

    def narrow(out_ref):
        def strip(i, carry):
            first = pl.multiple_of((step - steps) * out_rows * SPLIT + i * (32 * SPLIT), 32 * SPLIT)
            for part in range(SPLIT):
                value = total[pl.ds(first + part, 32, stride=SPLIT), :]
                out_ref[pl.ds(pl.multiple_of(i * 32, 32), 32), part * 128 : (part + 1) * 128] = value.astype(jnp.bfloat16)
            return carry

        lax.fori_loop(0, out_rows // 32, strip, 0)

    quarter = (total.shape[0] // SPLIT // 4) // out_rows
    for index, out_ref in enumerate(outs):
        last = quarter * (index + 1 if index < 2 else 4)

        @pl.when((step >= steps + quarter * index) & (step < steps + last))
        def _(out_ref=out_ref):
            narrow(out_ref)


SCATTER_BLOCK = 1024


def scatter_plan(where, rows):
    keys = jnp.arange(where.shape[0], dtype=jnp.int32).reshape(-1, SCATTER_BLOCK) % SCATTER_BLOCK
    where = where.reshape(-1, SCATTER_BLOCK)
    skipped = where >= rows
    keys, where = lax.sort((jnp.where(skipped, keys + SCATTER_BLOCK, keys), where), dimension=1, num_keys=1)
    count = jnp.sum((~skipped).astype(jnp.int32), axis=1)
    groups = (count + GROUP - 1) // GROUP
    where = jnp.where(keys >= SCATTER_BLOCK, rows + keys % GROUP, where)
    spare = lax.broadcasted_iota(jnp.int32, where.shape, 1) % GROUP
    where = jnp.where(keys >= SCATTER_BLOCK, rows + spare, where)
    eights = where.reshape(-1, GROUP)
    twice = jnp.zeros((eights.shape[0],), jnp.int32)
    for shift in range(1, GROUP):
        same = eights[:, shift:] == eights[:, :-shift]
        twice = twice | jnp.any(same, axis=1).astype(jnp.int32)
    return SPLIT * where.reshape(-1), SPLIT * (keys % SCATTER_BLOCK).reshape(-1), twice, groups


def scatter_rows(plan, own, other, rows, out_rows=512):
    block = SCATTER_BLOCK
    half = own.shape[0] // block
    steps = 2 * half
    quarter = rows // 4 // out_rows

    def part(first, count):
        return pl.BlockSpec((out_rows, D), lambda i, *_: (jnp.clip(i - steps - first, 0, count - 1), 0))

    return pl.pallas_call(
        functools.partial(scatter_kernel, steps, block, out_rows),
        out_shape=[
            jax.ShapeDtypeStruct((rows // 4, D), jnp.bfloat16),
            jax.ShapeDtypeStruct((rows // 4, D), jnp.bfloat16),
            jax.ShapeDtypeStruct((rows // 2, D), jnp.bfloat16),
        ],
        grid_spec=pltpu.PrefetchScalarGridSpec(
            num_scalar_prefetch=4,
            grid=(steps + rows // out_rows,),
            in_specs=[
                pl.BlockSpec((block, D), lambda i, *_: (jnp.minimum(i, half - 1), 0)),
                pl.BlockSpec((block, D), lambda i, *_: (jnp.clip(i - half, 0, half - 1), 0)),
            ],
            out_specs=[part(0, quarter), part(quarter, quarter), part(2 * quarter, 2 * quarter)],
            scratch_shapes=[
                pltpu.VMEM(((rows + 32) * SPLIT, 128), jnp.float32),
                pltpu.VMEM((block * SPLIT, 128), jnp.float32),
            ],
        ),
        compiler_params=pltpu.CompilerParams(vmem_limit_bytes=VMEM_LIMIT),
        cost_estimate=pl.CostEstimate(flops=0, transcendentals=0, bytes_accessed=220_000_000),
        name="scatter_rows",
    )(*plan, own, other)


def reduce_kernel(chunks, keep_ref, came_a, came_b, out_ref, keep_a, keep_b, one_a, one_b, two_a, two_b, layer, along, done,
                  keep_sem, two_send, two_recv, z_send, z_recv,
                  own_sem, y_send, y_recv, core_send, core_recv, pass_send, pass_recv):
    dp = lax.axis_index("dp")
    store = lax.axis_index("store")
    y, core = lax.div(dp, 2), lax.rem(dp, 2)
    z, x = lax.div(store, 2), lax.rem(store, 2)
    x_peer = (dp, z * 2 + (1 - x))
    y_peer = ((1 - y) * 2 + core, store)
    core_peer = (y * 2 + (1 - core), store)
    z_of = [lax.rem(z + hop, 4) for hop in range(4)]
    z_peer = [(dp, z_of[hop] * 2 + x) for hop in range(4)]

    barrier = pltpu.get_barrier_semaphore()
    for peer in (x_peer, y_peer, core_peer, z_peer[1], z_peer[2], z_peer[3]):
        pl.semaphore_signal(barrier, inc=1, device_id=peer, device_id_type=MESH_ID)
    pl.semaphore_wait(barrier, 6)

    def remote(src, dst, send, recv, peer):
        return pltpu.make_async_remote_copy(src_ref=src, dst_ref=dst, send_sem=send, recv_sem=recv,
                                            device_id=peer, device_id_type=MESH_ID)

    keeps = [(
        pltpu.make_async_copy(keep_ref.at[0, :, :, q], keep_a.at[q], keep_sem.at[0, q]),
        pltpu.make_async_copy(keep_ref.at[1, :, :, q], keep_b.at[q], keep_sem.at[1, q]),
        pltpu.make_async_copy(came_a.at[:, :, q], one_a.at[q], keep_sem.at[2, q]),
        pltpu.make_async_copy(came_b.at[:, :, q], one_b.at[q], keep_sem.at[3, q]),
    ) for q in range(chunks)]
    twos = [(
        remote(keep_a.at[q, :, 1 - y], two_a.at[q], two_send.at[0, q], two_recv.at[0, q], y_peer),
        remote(keep_b.at[q, :, 1 - x], two_b.at[q], two_send.at[1, q], two_recv.at[1, q], x_peer),
    ) for q in range(chunks)]
    zs = [[
        remote(layer.at[q, z_of[hop]], along.at[q, hop - 1], z_send.at[hop - 1, q], z_recv.at[hop - 1, q], z_peer[hop])
        for hop in (1, 2, 3)] for q in range(chunks)]
    own = [pltpu.make_async_copy(done.at[q], out_ref.at[core, y, :, q], own_sem.at[q]) for q in range(chunks)]
    to_y = [remote(done.at[q], out_ref.at[core, y, :, q], y_send.at[q], y_recv.at[q], y_peer) for q in range(chunks)]
    to_core = [remote(done.at[q], out_ref.at[core, y, :, q], core_send.at[q], core_recv.at[q], core_peer) for q in range(chunks)]
    passed = [remote(out_ref.at[core, 1 - y, :, q], out_ref.at[core, 1 - y, :, q], pass_send.at[q], pass_recv.at[q], core_peer)
              for q in range(chunks)]

    def plus(first, second):
        return (first.astype(jnp.float32) + second.astype(jnp.float32)).astype(jnp.bfloat16)

    for q in range(chunks):
        for copy in keeps[q]:
            copy.start()
    for step in range(chunks + 3):
        q = step
        if q < chunks:
            for copy in keeps[q]:
                copy.wait()

            def merge(i, carry, q=q):
                for half in range(2):
                    keep_a[q, i, half] = plus(keep_a[q, i, half], one_a[q, i, half])
                    keep_b[q, i, half] = plus(keep_b[q, i, half], one_b[q, i, half])
                return carry

            lax.fori_loop(0, 4, merge, 0)
            for copy in twos[q]:
                copy.start()
        q = step - 1
        if 0 <= q < chunks:
            for copy in twos[q]:
                copy.wait_recv()

            def merge_two(i, carry, q=q):
                layer[q, i, 0] = plus(keep_a[q, i, y], two_a[q, i])
                layer[q, i, 1] = plus(keep_b[q, i, x], two_b[q, i])
                return carry

            lax.fori_loop(0, 4, merge_two, 0)
            for copy in zs[q]:
                copy.start()
        q = step - 2
        if 0 <= q < chunks:
            for copy in zs[q]:
                copy.wait_recv()

            def finish(i, carry, q=q):
                value = layer[q, z, i].astype(jnp.float32)
                for hop in range(3):
                    value = value + along[q, hop, i].astype(jnp.float32)
                done[q, i] = value.astype(jnp.bfloat16)
                return carry

            lax.fori_loop(0, 2, finish, 0)
            for copy in (own[q], to_y[q], to_core[q]):
                copy.start()
        q = step - 3
        if 0 <= q < chunks:
            to_y[q].wait_recv()
            passed[q].start()
    for q in range(chunks):
        for copy in twos[q] + tuple(zs[q]):
            copy.wait_send()
        own[q].wait()
        to_y[q].wait_send()
        to_core[q].wait()
        passed[q].wait()


def reduce_rows(keep, came_a, came_b, collective_id=0):
    rows = keep.shape[0] // 4
    chunks = rows // (4 * CHUNK)
    dma = pltpu.SemaphoreType.DMA
    vm = lambda *lead: pltpu.VMEM(lead + (CHUNK, D), jnp.bfloat16)
    out = pl.pallas_call(
        functools.partial(reduce_kernel, chunks),
        out_shape=jax.ShapeDtypeStruct((2, 2, 2, chunks, CHUNK, D), jnp.bfloat16),
        in_specs=[pl.BlockSpec(memory_space=pl.ANY)] * 3,
        out_specs=pl.BlockSpec(memory_space=pl.ANY),
        scratch_shapes=[
            vm(chunks, 4, 2), vm(chunks, 4, 2), vm(chunks, 4, 2), vm(chunks, 4, 2),
            vm(chunks, 4), vm(chunks, 4), vm(chunks, 4, 2), vm(chunks, 3, 2), vm(chunks, 2),
            dma((4, chunks)), dma((2, chunks)), dma((2, chunks)),
            dma((3, chunks)), dma((3, chunks)),
            dma((chunks,)), dma((chunks,)), dma((chunks,)), dma((chunks,)), dma((chunks,)), dma((chunks,)), dma((chunks,)),
        ],
        compiler_params=pltpu.CompilerParams(collective_id=collective_id, has_side_effects=True, vmem_limit_bytes=VMEM_LIMIT),
        cost_estimate=pl.CostEstimate(flops=0, transcendentals=0, bytes_accessed=450_000_000),
        name="reduce_rows",
    )(
        keep.reshape(2, 4, 2, chunks, CHUNK, D),
        came_a.reshape(4, 2, chunks, CHUNK, D),
        came_b.reshape(4, 2, chunks, CHUNK, D),
    )
    return out.reshape(2 * rows, D)


PAIRS = ((0, 1), (1, 0), (2, 3), (3, 2))


def own_rows(flat, rows_here):
    half = rows_here // 2
    quarter = half // 4
    dp = lax.axis_index("dp")
    here_y, core = dp // 2, dp % 2
    here_x = lax.axis_index("store") % 2
    owner, local = flat // rows_here, flat % rows_here
    z, x = owner // 2, owner % 2
    y = (local % half) // (2 * quarter)
    second = (local // quarter) % 2
    stays = jnp.where(second == 0, x == here_x, y == here_y)
    pair = jnp.where(second == 0, y, x)
    rows = 8 * half
    target = (2 * stays + second) * (rows // 4) + (2 * z + pair) * quarter + local % quarter
    return jnp.where(local // half == core, target, rows)


def plan_store(indices, rows_here):
    flat = indices.reshape(-1)
    other = lax.ppermute(flat, "dp", PAIRS)
    where = jnp.concatenate([own_rows(flat, rows_here), own_rows(other, rows_here)])
    return scatter_plan(where, lax.axis_size("store") * rows_here // 2)


def add_store(plan, own, other, rows_here):
    return scatter_rows(plan, own, other, lax.axis_size("store") * rows_here // 2)


def swap_store(send_a, send_b):
    owners = lax.axis_size("store")
    came_a = lax.ppermute(send_a, "store", [(i, i ^ 1) for i in range(owners)])
    came_b = lax.ppermute(send_b, "dp", [(i, i ^ 2) for i in range(4)])
    return came_a, came_b


def by_owner(matrix):
    owners = lax.axis_size("store")
    return matrix.astype(jnp.bfloat16).reshape(owners, -1, D)


def reduce_packed(packed):
    return lax.psum_scatter(
        packed.reshape(-1, D), ("store", "dp"), scatter_dimension=0, tiled=True
    )


def all_copies(share):
    return lax.all_gather(share, "dp", axis=0, tiled=True).astype(jnp.float32)


def pack_early(inner, outer, squares):
    blocks = [inner[:, block * D : (block + 1) * D] for block in range(inner.shape[1] // D)]
    return jnp.concatenate([by_owner(piece) for piece in blocks + [outer] + list(squares)], axis=1)


def unpack_early(total, wide):
    part = D // lax.axis_size("store")
    inner_total = jnp.transpose(total[: wide * part].reshape(wide, part, D), (1, 0, 2))
    rest = total[wide * part :]
    return (
        inner_total.reshape(part, wide * D),
        rest[: wide * part],
        rest[wide * part :].reshape(-1, part, D),
    )


def pack_late(squares, features, inner_bias):
    owners = lax.axis_size("store")
    part = D // owners
    wide = inner_bias.shape[0] // D
    small = jnp.concatenate(
        [feature.astype(jnp.bfloat16).reshape(owners, part) for feature in features]
        + [inner_bias.astype(jnp.bfloat16).reshape(owners, wide * part)],
        axis=1,
    )
    small = jnp.pad(small, ((0, 0), (0, 64 * D - small.shape[1]))).reshape(owners, 64, D)
    return jnp.concatenate([by_owner(square) for square in squares] + [small], axis=1)


def unpack_late(total, count, features, wide):
    part = D // lax.axis_size("store")
    tail = total[count * part :].reshape(-1)
    table = tail[: features * part].reshape(features, part)
    return (
        total[: count * part].reshape(count, part, D),
        table,
        tail[features * part :][: wide * part],
    )


def cross_probs_of(folded, rows):
    scores = lax.dot_general(folded, rows, (((1,), (1,)), ((), ())), preferred_element_type=jnp.float32)
    token = lax.broadcasted_iota(jnp.int32, scores.shape, 0) % CROSS_TOKENS
    owner = lax.broadcasted_iota(jnp.int32, scores.shape, 1) // K
    scores = jnp.where(token == owner, scores, -1e30)
    raised = jnp.exp(scores - jnp.max(scores, axis=1, keepdims=True))
    return raised * (1.0 / jnp.sum(raised, axis=1, keepdims=True))


def cross_tiles(ref):
    tokens = ref.shape[1]
    for first in range(0, tokens, CROSS_TOKENS):
        yield pl.ds(first, CROSS_TOKENS), pl.ds(first * K, CROSS_TOKENS * K)


def cross_forward_kernel(folded_ref, first_ref, second_ref, which_ref, rows_ref, summary_ref):
    for some, slots in cross_tiles(folded_ref):
        which = which_ref[slots, :] != 0
        rows = jnp.where(
            which, second_ref[slots, :].astype(jnp.float32), first_ref[slots, :].astype(jnp.float32)
        ).astype(jnp.bfloat16)
        rows_ref[slots, :] = rows
        probs = cross_probs_of(folded_ref[:, some, :].reshape(H * CROSS_TOKENS, D), rows)
        summary = jnp.dot(probs.astype(jnp.bfloat16), rows, preferred_element_type=jnp.float32)
        summary_ref[:, some, :] = summary.astype(jnp.bfloat16).reshape(H, CROSS_TOKENS, D)


def cross_backward_kernel(folded_ref, grad_ref, rows_ref, row_grad_ref, folded_grad_ref):
    for some, slots in cross_tiles(folded_ref):
        rows = rows_ref[slots, :]
        folded = folded_ref[:, some, :].reshape(H * CROSS_TOKENS, D)
        grad = grad_ref[:, some, :].reshape(H * CROSS_TOKENS, D)
        probs = cross_probs_of(folded, rows)
        prob_grad = lax.dot_general(
            grad, rows, (((1,), (1,)), ((), ())), preferred_element_type=jnp.float32
        )
        total = jnp.sum(probs * prob_grad, axis=1, keepdims=True)
        score_low = (probs * (prob_grad - total)).astype(jnp.bfloat16)
        turned = (((0,), (0,)), ((), ()))
        row_grad = lax.dot_general(
            probs.astype(jnp.bfloat16), grad, turned, preferred_element_type=jnp.float32
        )
        row_grad += lax.dot_general(score_low, folded, turned, preferred_element_type=jnp.float32)
        row_grad_ref[slots, :] = row_grad.astype(jnp.bfloat16)
        folded_grad = jnp.dot(score_low, rows, preferred_element_type=jnp.float32)
        folded_grad_ref[:, some, :] = folded_grad.astype(jnp.bfloat16).reshape(H, CROSS_TOKENS, D)


CROSS_TOKENS = 16
CROSS_STEP = 64


def cross_specs():
    heads = pl.BlockSpec((H, CROSS_STEP, D), lambda i: (0, i, 0))
    rows = pl.BlockSpec((CROSS_STEP * K, D), lambda i: (i, 0))
    return heads, rows


def cross_forward(folded, first, second, which):
    heads, rows = cross_specs()
    tokens = folded.shape[1]
    return pl.pallas_call(
        cross_forward_kernel,
        out_shape=[
            jax.ShapeDtypeStruct((tokens * K, D), jnp.bfloat16),
            jax.ShapeDtypeStruct((H, tokens, D), jnp.bfloat16),
        ],
        grid=(tokens // CROSS_STEP,),
        in_specs=[heads, rows, rows, pl.BlockSpec((CROSS_STEP * K, 1), lambda i: (i, 0))],
        out_specs=[rows, heads],
        cost_estimate=pl.CostEstimate(flops=0, transcendentals=0, bytes_accessed=65_000_000),
        name="cross_forward",
    )(folded, first, second, which)


def cross_backward(folded, grad, fetched):
    heads, rows = cross_specs()
    tokens = folded.shape[1]
    return pl.pallas_call(
        cross_backward_kernel,
        out_shape=[
            jax.ShapeDtypeStruct((tokens * K, D), jnp.bfloat16),
            jax.ShapeDtypeStruct((H, tokens, D), jnp.bfloat16),
        ],
        grid=(tokens // CROSS_STEP,),
        in_specs=[heads, heads, rows],
        out_specs=[rows, heads],
        cost_estimate=pl.CostEstimate(flops=0, transcendentals=0, bytes_accessed=100_000_000),
        name="cross_backward",
    )(folded, grad, fetched)


def body(
    tokens,
    datastore,
    indices,
    lengths,
    proj_weight,
    out_weight,
    proj_bias,
    norm_gain,
    norm_bias,
    inner_weight,
    inner_bias,
    outer_weight,
    outer_bias,
    cotangent,
):
    seq_len = tokens.shape[0]
    score_scale = HD ** (-0.5)
    owners = lax.axis_size("store")
    rows_here = datastore.shape[0]
    capacity = 2 * seq_len * K // owners
    position = jnp.arange(seq_len)
    length = lengths[0]
    allowed = (position[None, :] <= position[:, None]) & (position[None, :] < length)
    valid = (position < length)[:, None]
    dense = is_dense(owners, rows_here)
    if dense:
        plan = plan_store(indices, rows_here)
        found_first, found_second, which_half, plan = fetch_dense(datastore, indices, plan)
    else:
        target, request = route_slots(indices, rows_here, owners, capacity)
        returned, _ = fetch_rows(request, datastore)
        fetched = returned.reshape(owners * capacity, D)[target].reshape(seq_len, K, D)
    self_bias = jnp.concatenate([proj_bias[:, 0], jnp.zeros((D,), jnp.float32), proj_bias[:, 1]])
    self_proj = proj_weight[:, 0:3, :].reshape(D, 3 * D)
    joined = (product(tokens, self_proj) + self_bias).astype(jnp.bfloat16)
    queries = joined[:, :D].reshape(seq_len, H, HD)
    self_keys = joined[:, D : 2 * D].reshape(seq_len, H, HD)
    values = joined[:, 2 * D :].reshape(seq_len, H, HD)
    scores = self_scores(queries, self_keys, allowed, score_scale)
    self_lse = log_total(scores)
    self_probs = jnp.exp(scores - self_lse).astype(jnp.bfloat16)
    self_mixed = (
        jnp.einsum("hqk,khe->qhe", self_probs, values, preferred_element_type=jnp.float32)
        .reshape(seq_len, D)
        .astype(jnp.bfloat16)
    )
    first_pre = tokens.astype(jnp.float32) + (
        product(self_mixed, out_weight[:, 0, :]) + proj_bias[:, 2]
    )
    first_out, first_normed, first_inverse = norm_forward(
        first_pre, norm_gain[:, 0], norm_bias[:, 0]
    )
    first_low = first_out.astype(jnp.bfloat16)
    cross_query = (
        (product(first_low, proj_weight[:, 3, :]) + proj_bias[:, 3])
        .astype(jnp.bfloat16)
        .reshape(seq_len, H, HD)
    )
    key_heads = proj_weight[:, 4, :].reshape(D, H, HD)
    folded = (
        jnp.einsum("the,dhe->thd", cross_query, key_heads, preferred_element_type=jnp.float32)
        * score_scale
    ).astype(jnp.bfloat16)
    if dense:
        folded_heads = jnp.transpose(folded, (1, 0, 2))
        fetched, summary = cross_forward(folded_heads, found_first, found_second, which_half)
        summary = jnp.transpose(summary, (1, 0, 2))
    else:
        cross_scores = jnp.einsum("thd,tkd->thk", folded, fetched, preferred_element_type=jnp.float32)
        cross_lse = log_total(cross_scores)
        cross_full = jnp.exp(cross_scores - cross_lse)
        cross_probs = cross_full.astype(jnp.bfloat16)
        summary = jnp.einsum(
            "thk,tkd->thd", cross_probs, fetched, preferred_element_type=jnp.float32
        ).astype(jnp.bfloat16)
    value_heads = proj_weight[:, 5, :].reshape(D, H, HD)
    cross_mixed = (
        jnp.einsum(
            "thd,dhe->the", summary, value_heads, preferred_element_type=jnp.float32
        ).reshape(seq_len, D)
        + proj_bias[:, 4]
    ).astype(jnp.bfloat16)
    second_pre = first_out + (product(cross_mixed, out_weight[:, 1, :]) + proj_bias[:, 5])
    second_out, second_normed, second_inverse = norm_forward(
        second_pre, norm_gain[:, 1], norm_bias[:, 1]
    )
    second_low = second_out.astype(jnp.bfloat16)
    inner_pre = product(second_low, inner_weight) + inner_bias
    activated = jax.nn.gelu(inner_pre, approximate=False).astype(jnp.bfloat16)
    third_pre = second_out + (product(activated, outer_weight) + outer_bias)
    third_out, third_normed, third_inverse = norm_forward(
        third_pre, norm_gain[:, 2], norm_bias[:, 2]
    )
    output = jnp.where(valid, third_out, 0.0).astype(jnp.bfloat16)
    upstream = jnp.where(valid, cotangent.astype(jnp.float32), 0.0)
    third_grad, gain_three, shift_three = norm_backward(
        upstream, third_normed, third_inverse, norm_gain[:, 2]
    )
    outer_low = third_grad.astype(jnp.bfloat16)
    grad_outer_weight = contract_rows(activated, outer_low)
    grad_outer_bias = column_sum(outer_low)
    act_grad = product_back(outer_low, outer_weight)
    slope = jax.vjp(lambda activation_in: jax.nn.gelu(activation_in, approximate=False), inner_pre)[
        1
    ](act_grad)[0]
    inner_low = slope.astype(jnp.bfloat16)
    grad_inner_weight = contract_rows(second_low, inner_low)
    grad_inner_bias = column_sum(inner_low)
    second_up = third_grad + product_back(inner_low, inner_weight)
    second_grad, gain_two, shift_two = norm_backward(
        second_up, second_normed, second_inverse, norm_gain[:, 1]
    )
    cross_out_low = second_grad.astype(jnp.bfloat16)
    grad_cross_out = contract_rows(cross_mixed, cross_out_low)
    bias_five = column_sum(cross_out_low)
    mixed_low = product_back(cross_out_low, out_weight[:, 1, :]).astype(jnp.bfloat16)
    bias_four = column_sum(mixed_low)
    mixed_heads = mixed_low.reshape(seq_len, H, HD)
    grad_value_heads = jnp.einsum(
        "thd,the->dhe", summary, mixed_heads, preferred_element_type=jnp.float32
    )
    if dense:
        packed_early = pack_early(grad_inner_weight, grad_outer_weight, (grad_cross_out,))
        mixed_heads, packed_early = lax.optimization_barrier((mixed_heads, packed_early))
        share_early = reduce_packed(packed_early)
    summary_low = jnp.einsum(
        "the,dhe->thd", mixed_heads, value_heads, preferred_element_type=jnp.float32
    ).astype(jnp.bfloat16)
    if dense:
        own_grad, folded_low = cross_backward(
            folded_heads, jnp.transpose(summary_low, (1, 0, 2)), fetched
        )
        folded_low = jnp.transpose(folded_low, (1, 0, 2))
        other_grad = lax.ppermute(own_grad, "dp", PAIRS)
    else:
        returned_again, asked_back = fetch_again(request, datastore)
        fetched_back = returned_again.reshape(owners * capacity, D)[target].reshape(seq_len, K, D)
        prob_grad = jnp.einsum(
            "thd,tkd->thk", summary_low, fetched_back, preferred_element_type=jnp.float32
        )
        score_low = (
            cross_full * (prob_grad - jnp.sum(cross_full * prob_grad, axis=-1, keepdims=True))
        ).astype(jnp.bfloat16)
        row_grad = (
            jnp.einsum("thk,thd->tkd", cross_probs, summary_low, preferred_element_type=jnp.float32)
            + jnp.einsum("thk,thd->tkd", score_low, folded, preferred_element_type=jnp.float32)
        ).astype(jnp.bfloat16)
        folded_low = jnp.einsum(
            "thk,tkd->thd", score_low, fetched_back, preferred_element_type=jnp.float32
        ).astype(jnp.bfloat16)
    grad_key_heads = (
        jnp.einsum("thd,the->dhe", folded_low, cross_query, preferred_element_type=jnp.float32)
        * score_scale
    )
    query_low = (
        (
            jnp.einsum("thd,dhe->the", folded_low, key_heads, preferred_element_type=jnp.float32)
            * score_scale
        )
        .astype(jnp.bfloat16)
        .reshape(seq_len, D)
    )
    if dense:
        query_low, other_grad = lax.optimization_barrier((query_low, other_grad))
        send_a, send_b, keep = add_store(plan, own_grad, other_grad, rows_here)
        query_low, mixed_heads, send_a, send_b, keep = lax.optimization_barrier(
            (query_low, mixed_heads, send_a, send_b, keep)
        )
        grad_value_heads = jnp.einsum(
            "thd,the->dhe", summary, mixed_heads, preferred_element_type=jnp.float32
        )
        came_a, came_b = swap_store(send_a, send_b)
    bias_three = column_sum(query_low)
    grad_cross_query = contract_rows(first_low, query_low)
    if not dense:
        grad_buffer = (
            jnp.zeros((owners * capacity, D), jnp.bfloat16)
            .at[target]
            .set(row_grad.reshape(-1, D))
            .reshape(owners, capacity, D)
        )
        arrived = lax.all_to_all(grad_buffer, "store", split_axis=0, concat_axis=0, tiled=True)
        partial_store = (
            jnp.zeros((rows_here, D), jnp.float32)
            .at[asked_back.reshape(-1)]
            .add(arrived.reshape(-1, D).astype(jnp.float32))
        )
        grad_store = lax.psum(partial_store.astype(jnp.bfloat16), "dp").astype(jnp.float32)
    first_up = second_grad + product_back(query_low, proj_weight[:, 3, :])
    first_grad, gain_one, shift_one = norm_backward(
        first_up, first_normed, first_inverse, norm_gain[:, 0]
    )
    self_out_low = first_grad.astype(jnp.bfloat16)
    grad_self_out = contract_rows(self_mixed, self_out_low)
    bias_two = column_sum(self_out_low)
    self_mixed_low = (
        product_back(self_out_low, out_weight[:, 0, :]).astype(jnp.bfloat16).reshape(seq_len, H, HD)
    )
    value_grad = jnp.einsum(
        "hqk,qhe->khe", self_probs, self_mixed_low, preferred_element_type=jnp.float32
    )
    attend_grad = jnp.einsum(
        "qhe,khe->hqk", self_mixed_low, values, preferred_element_type=jnp.float32
    )
    self_full = jnp.exp(self_scores(queries, self_keys, allowed, score_scale) - self_lse)
    self_score_low = (
        self_full * (attend_grad - jnp.sum(self_full * attend_grad, axis=-1, keepdims=True))
    ).astype(jnp.bfloat16)
    query_grad = (
        jnp.einsum("hqk,khe->qhe", self_score_low, self_keys, preferred_element_type=jnp.float32)
        * score_scale
    )
    key_grad = (
        jnp.einsum("hqk,qhe->khe", self_score_low, queries, preferred_element_type=jnp.float32)
        * score_scale
    )
    joined_low = jnp.concatenate(
        [
            query_grad.reshape(seq_len, D),
            key_grad.reshape(seq_len, D),
            value_grad.reshape(seq_len, D),
        ],
        axis=1,
    ).astype(jnp.bfloat16)
    grad_self_proj = contract_rows(tokens, joined_low).reshape(D, 3, D)
    bias_zero = column_sum(joined_low[:, :D])
    bias_one = column_sum(joined_low[:, 2 * D :])
    grad_tokens = (first_grad + product_back(joined_low, self_proj)).astype(jnp.bfloat16)
    if dense:
        packed_late = pack_late(
            (
                grad_self_proj[:, 0],
                grad_self_proj[:, 1],
                grad_self_proj[:, 2],
                grad_cross_query,
                grad_key_heads.reshape(D, D),
                grad_value_heads.reshape(D, D),
                grad_self_out,
            ),
            (bias_zero, bias_one, bias_two, bias_three, bias_four, bias_five)
            + (gain_one, gain_two, gain_three)
            + (shift_one, shift_two, shift_three)
            + (grad_outer_bias,),
            grad_inner_bias,
        )
        share_late = reduce_packed(packed_late)
        keep, came_a, came_b, share_early = lax.optimization_barrier(
            (keep, came_a, came_b, share_early)
        )
        wide = grad_inner_bias.shape[0] // D
        inner_total, outer_total, early = unpack_early(all_copies(share_early), wide)
        grad_store = reduce_rows(keep, came_a, came_b)
        grad_store, share_late = lax.optimization_barrier((grad_store, share_late))
        grad_store = grad_store.astype(jnp.float32)
        late, table, bias_inner = unpack_late(all_copies(share_late), 7, 13, wide)
        return (
            output,
            grad_tokens,
            grad_store,
            jnp.stack([late[0], late[1], late[2], late[3], late[4], late[5]], axis=1),
            jnp.stack([late[6], early[0]], axis=1),
            jnp.transpose(table[0:6]),
            jnp.transpose(table[6:9]),
            jnp.transpose(table[9:12]),
            inner_total,
            bias_inner,
            outer_total,
            table[12],
        )
    grad_proj = jnp.stack(
        [
            grad_self_proj[:, 0],
            grad_self_proj[:, 1],
            grad_self_proj[:, 2],
            grad_cross_query,
            grad_key_heads.reshape(D, D),
            grad_value_heads.reshape(D, D),
        ],
        axis=1,
    )
    grad_out = jnp.stack([grad_self_out, grad_cross_out], axis=1)
    grad_bias = jnp.stack([bias_zero, bias_one, bias_two, bias_three, bias_four, bias_five], axis=1)
    grad_gain = jnp.stack([gain_one, gain_two, gain_three], axis=1)
    grad_shift = jnp.stack([shift_one, shift_two, shift_three], axis=1)
    shares = (
        lax.psum_scatter(
            grad_proj.astype(jnp.bfloat16), "store", scatter_dimension=0, tiled=True
        ).astype(jnp.float32),
        lax.psum_scatter(
            grad_out.astype(jnp.bfloat16), "store", scatter_dimension=0, tiled=True
        ).astype(jnp.float32),
        lax.psum_scatter(
            grad_bias.astype(jnp.bfloat16), "store", scatter_dimension=0, tiled=True
        ).astype(jnp.float32),
        lax.psum_scatter(
            grad_gain.astype(jnp.bfloat16), "store", scatter_dimension=0, tiled=True
        ).astype(jnp.float32),
        lax.psum_scatter(
            grad_shift.astype(jnp.bfloat16), "store", scatter_dimension=0, tiled=True
        ).astype(jnp.float32),
        lax.psum_scatter(
            grad_inner_weight.astype(jnp.bfloat16), "store", scatter_dimension=0, tiled=True
        ).astype(jnp.float32),
        lax.psum_scatter(
            grad_inner_bias.astype(jnp.bfloat16), "store", scatter_dimension=0, tiled=True
        ).astype(jnp.float32),
        lax.psum_scatter(
            grad_outer_weight.astype(jnp.bfloat16), "store", scatter_dimension=0, tiled=True
        ).astype(jnp.float32),
        lax.psum_scatter(
            grad_outer_bias.astype(jnp.bfloat16), "store", scatter_dimension=0, tiled=True
        ).astype(jnp.float32),
    )
    totals = (
        lax.psum(shares[0].astype(jnp.bfloat16), "dp").astype(jnp.float32),
        lax.psum(shares[1].astype(jnp.bfloat16), "dp").astype(jnp.float32),
        lax.psum(shares[2].astype(jnp.bfloat16), "dp").astype(jnp.float32),
        lax.psum(shares[3].astype(jnp.bfloat16), "dp").astype(jnp.float32),
        lax.psum(shares[4].astype(jnp.bfloat16), "dp").astype(jnp.float32),
        lax.psum(shares[5].astype(jnp.bfloat16), "dp").astype(jnp.float32),
        lax.psum(shares[6].astype(jnp.bfloat16), "dp").astype(jnp.float32),
        lax.psum(shares[7].astype(jnp.bfloat16), "dp").astype(jnp.float32),
        lax.psum(shares[8].astype(jnp.bfloat16), "dp").astype(jnp.float32),
    )
    return (
        output,
        grad_tokens,
        grad_store,
        totals[0],
        totals[1],
        totals[2],
        totals[3],
        totals[4],
        totals[5],
        totals[6],
        totals[7],
        totals[8],
    )


def solution(mesh):
    in_specs = (
        P(("dp", "store"), None),
        P("store", None),
        P(("dp", "store"), None),
        P(("dp", "store")),
        P(),
        P(),
        P(),
        P(),
        P(),
        P(),
        P(),
        P(),
        P(),
        P(("dp", "store"), None),
    )
    out_specs = (
        P(("dp", "store"), None),
        P(("dp", "store"), None),
        P("store", None),
        P("store", None, None),
        P("store", None, None),
        P("store", None),
        P("store", None),
        P("store", None),
        P("store", None),
        P("store"),
        P("store", None),
        P("store"),
    )

    return jax.shard_map(body, mesh=mesh, in_specs=in_specs, out_specs=out_specs, check_vma=False)
```

```python
import functools

import jax
import jax.numpy as jnp
from jax import lax
from jax.experimental import pallas as pl
from jax.experimental.pallas import tpu as pltpu
from jax.sharding import PartitionSpec as P


D = 768
H = 12
HD = 64
K = 16


EPSILON = 1e-05


def product(matrix, factor):
    return jnp.dot(matrix, factor, preferred_element_type=jnp.float32)


def product_back(matrix, weight):
    return jnp.einsum("tf,df->td", matrix, weight, preferred_element_type=jnp.float32)


def contract_rows(matrix, factor):
    return jnp.einsum("td,tf->df", matrix, factor, preferred_element_type=jnp.float32)


def column_sum(matrix):
    return jnp.sum(matrix.astype(jnp.float32), axis=0)


def norm_forward(hidden, norm_weight, norm_shift):
    centered = hidden - jnp.mean(hidden, axis=-1, keepdims=True)
    inverse = lax.rsqrt(jnp.mean(centered * centered, axis=-1, keepdims=True) + EPSILON)
    normed = centered * inverse
    return (normed * norm_weight + norm_shift, normed, inverse)


def norm_backward(upstream, normed, inverse, norm_weight):
    scaled = upstream * norm_weight
    plain_mean = jnp.mean(scaled, axis=-1, keepdims=True)
    normed_mean = jnp.mean(scaled * normed, axis=-1, keepdims=True)
    return (
        inverse * (scaled - plain_mean - normed * normed_mean),
        jnp.sum(upstream * normed, axis=0),
        jnp.sum(upstream, axis=0),
    )


def log_total(scores):
    highest = jnp.max(scores, axis=-1, keepdims=True)
    return highest + jnp.log(jnp.sum(jnp.exp(scores - highest), axis=-1, keepdims=True))


def route_slots(picked, rows_here, owners, capacity):
    flat_ids = picked.reshape(-1)
    owner_of = flat_ids // rows_here
    local_row = flat_ids % rows_here
    by_owner = jnp.argsort(owner_of, stable=True)
    sorted_owner = owner_of[by_owner]
    owner_loads = jnp.sum(
        (owner_of[:, None] == jnp.arange(owners, dtype=jnp.int32)[None, :]).astype(jnp.int32),
        axis=0,
    )
    starts = jnp.cumsum(owner_loads) - owner_loads
    within = jnp.arange(flat_ids.shape[0], dtype=jnp.int32) - starts[sorted_owner]
    placed = jnp.zeros_like(flat_ids).at[by_owner].set(within)
    target = owner_of * capacity + placed
    request = jnp.zeros((owners * capacity,), jnp.int32).at[target].set(local_row)
    return (target, request.reshape(owners, capacity))


def fetch_rows(request, datastore):
    asked_rows = lax.all_to_all(request, "store", split_axis=0, concat_axis=0, tiled=True)
    found_rows = datastore[asked_rows.reshape(-1)].reshape(asked_rows.shape + (datastore.shape[1],))
    return (
        lax.all_to_all(found_rows, "store", split_axis=0, concat_axis=0, tiled=True),
        asked_rows,
    )


def fetch_again(request, datastore):
    asked_rows = lax.all_to_all(request, "store", split_axis=0, concat_axis=0, tiled=True)
    found_rows = datastore[asked_rows.reshape(-1)].reshape(asked_rows.shape + (datastore.shape[1],))
    return (
        lax.all_to_all(found_rows, "store", split_axis=0, concat_axis=0, tiled=True),
        asked_rows,
    )


def self_scores(queries, self_keys, allowed, score_scale):
    scores = (
        jnp.einsum("qhe,khe->hqk", queries, self_keys, preferred_element_type=jnp.float32)
        * score_scale
    )
    return jnp.where(allowed[None], scores, -1e30)


DENSE_LIMIT = 1 << 16


def is_dense(owners, rows_here):
    fits = owners * rows_here <= DENSE_LIMIT and rows_here % (8 * CHUNK) == 0
    return fits and owners == 8 and lax.axis_size("dp") == 4


STORE_PARTS = 2


def fetch_dense(datastore, indices, plan):
    copies = lax.axis_size("dp")
    rows_here = datastore.shape[0]
    share = rows_here // copies
    part = share // STORE_PARTS
    flat = indices.reshape(-1)
    which = (flat % share) // part
    local = (flat // share) * part + flat % part
    start = lax.axis_index("dp") * share
    found = []
    earlier = None
    for index in range(STORE_PARTS):
        mine = lax.dynamic_slice_in_dim(datastore, start + index * part, part, axis=0)
        if earlier is not None:
            mine, earlier = lax.optimization_barrier((mine, earlier))
        table = lax.all_gather(mine, ("store", "dp"), axis=0, tiled=True)
        earlier = mine
        if index == STORE_PARTS - 1:
            which, plan = lax.optimization_barrier((which, plan))
        found.append(table[local])
    return found[0], found[1], which[:, None], plan


MESH_ID = pl.DeviceIdType.MESH
VMEM_LIMIT = 67043328
CHUNK = 64


GROUP = 8


SPLIT = D // 128


def scatter_kernel(steps, block, out_rows, row_ref, from_ref, twice_ref, groups_ref, own_ref, other_ref, *rest):
    outs, (total, wide) = rest[:-2], rest[-2:]
    step = pl.program_id(0)

    @pl.when(step == 0)
    def _():
        def clear(i, carry):
            total[pl.ds(i * 192, 192), :] = jnp.zeros((192, 128), jnp.float32)
            return carry

        lax.fori_loop(0, total.shape[0] // 192, clear, 0)

    def widen(ref):
        def strip(i, carry):
            first = pl.multiple_of(i * 32, 32)
            value = ref[pl.ds(first, 32), :].astype(jnp.float32)
            for part in range(SPLIT):
                wide[pl.ds(first * SPLIT + part, 32, stride=SPLIT), :] = value[:, part * 128 : (part + 1) * 128]
            return carry

        lax.fori_loop(0, block // 32, strip, 0)

    @pl.when(step < steps // 2)
    def _():
        widen(own_ref)

    @pl.when((step >= steps // 2) & (step < steps))
    def _():
        widen(other_ref)

    @pl.when(step < steps)
    def _():
        def group(i, carry):
            first = step * block + i * GROUP
            rows = [row_ref[first + k] for k in range(GROUP)]
            came = [from_ref[first + k] for k in range(GROUP)]
            twice = twice_ref[step * (block // GROUP) + i]

            @pl.when(twice == 0)
            def _():
                sums = [total[pl.ds(rows[k], SPLIT), :] + wide[pl.ds(came[k], SPLIT), :] for k in range(GROUP)]
                for k in range(GROUP):
                    total[pl.ds(rows[k], SPLIT), :] = sums[k]

            @pl.when(twice != 0)
            def _():
                for k in range(GROUP):
                    total[pl.ds(rows[k], SPLIT), :] = total[pl.ds(rows[k], SPLIT), :] + wide[pl.ds(came[k], SPLIT), :]

            return carry

        lax.fori_loop(0, groups_ref[step], group, 0)

    def narrow(out_ref):
        def strip(i, carry):
            first = pl.multiple_of((step - steps) * out_rows * SPLIT + i * (32 * SPLIT), 32 * SPLIT)
            for part in range(SPLIT):
                value = total[pl.ds(first + part, 32, stride=SPLIT), :]
                out_ref[pl.ds(pl.multiple_of(i * 32, 32), 32), part * 128 : (part + 1) * 128] = value.astype(jnp.bfloat16)
            return carry

        lax.fori_loop(0, out_rows // 32, strip, 0)

    quarter = (total.shape[0] // SPLIT // 4) // out_rows
    for index, out_ref in enumerate(outs):
        last = quarter * (index + 1 if index < 2 else 4)

        @pl.when((step >= steps + quarter * index) & (step < steps + last))
        def _(out_ref=out_ref):
            narrow(out_ref)


SCATTER_BLOCK = 1024


def scatter_plan(where, rows):
    keys = jnp.arange(where.shape[0], dtype=jnp.int32).reshape(-1, SCATTER_BLOCK) % SCATTER_BLOCK
    where = where.reshape(-1, SCATTER_BLOCK)
    skipped = where >= rows
    keys, where = lax.sort((jnp.where(skipped, keys + SCATTER_BLOCK, keys), where), dimension=1, num_keys=1)
    count = jnp.sum((~skipped).astype(jnp.int32), axis=1)
    groups = (count + GROUP - 1) // GROUP
    where = jnp.where(keys >= SCATTER_BLOCK, rows + keys % GROUP, where)
    spare = lax.broadcasted_iota(jnp.int32, where.shape, 1) % GROUP
    where = jnp.where(keys >= SCATTER_BLOCK, rows + spare, where)
    eights = where.reshape(-1, GROUP)
    twice = jnp.zeros((eights.shape[0],), jnp.int32)
    for shift in range(1, GROUP):
        same = eights[:, shift:] == eights[:, :-shift]
        twice = twice | jnp.any(same, axis=1).astype(jnp.int32)
    return SPLIT * where.reshape(-1), SPLIT * (keys % SCATTER_BLOCK).reshape(-1), twice, groups


def scatter_rows(plan, own, other, rows, out_rows=512):
    block = SCATTER_BLOCK
    half = own.shape[0] // block
    steps = 2 * half
    quarter = rows // 4 // out_rows

    def part(first, count):
        return pl.BlockSpec((out_rows, D), lambda i, *_: (jnp.clip(i - steps - first, 0, count - 1), 0))

    return pl.pallas_call(
        functools.partial(scatter_kernel, steps, block, out_rows),
        out_shape=[
            jax.ShapeDtypeStruct((rows // 4, D), jnp.bfloat16),
            jax.ShapeDtypeStruct((rows // 4, D), jnp.bfloat16),
            jax.ShapeDtypeStruct((rows // 2, D), jnp.bfloat16),
        ],
        grid_spec=pltpu.PrefetchScalarGridSpec(
            num_scalar_prefetch=4,
            grid=(steps + rows // out_rows,),
            in_specs=[
                pl.BlockSpec((block, D), lambda i, *_: (jnp.minimum(i, half - 1), 0)),
                pl.BlockSpec((block, D), lambda i, *_: (jnp.clip(i - half, 0, half - 1), 0)),
            ],
            out_specs=[part(0, quarter), part(quarter, quarter), part(2 * quarter, 2 * quarter)],
            scratch_shapes=[
                pltpu.VMEM(((rows + 32) * SPLIT, 128), jnp.float32),
                pltpu.VMEM((block * SPLIT, 128), jnp.float32),
            ],
        ),
        compiler_params=pltpu.CompilerParams(vmem_limit_bytes=VMEM_LIMIT),
        cost_estimate=pl.CostEstimate(flops=0, transcendentals=0, bytes_accessed=220_000_000),
        name="scatter_rows",
    )(*plan, own, other)


SIGNALS = 26


def plus(first, second):
    return (first.astype(jnp.float32) + second.astype(jnp.float32)).astype(jnp.bfloat16)


class Unit:
    def __init__(self, place, signals, spare, out):
        self.x, self.y, self.z, self.core, self.inner, self.peers = place
        self.signals = signals
        self.keep_a, self.keep_b, self.one_a, self.one_b, self.two_a, self.two_b = spare[:6]
        self.layer, self.three, self.merged, self.near, self.far, self.done = spare[6:]
        self.out = out

    def remote(self, src, dst, send, recv, peer):
        return pltpu.make_async_remote_copy(
            src_ref=src, dst_ref=dst, send_sem=self.signals(send), recv_sem=self.signals(recv),
            device_id=peer, device_id_type=MESH_ID,
        )

    def loads(self, sources):
        places = (self.keep_a, self.keep_b, self.one_a, self.one_b)
        return [
            pltpu.make_async_copy(source, place, self.signals(index))
            for index, (source, place) in enumerate(zip(sources, places))
        ]

    def firsts(self, send_a, send_b):
        return [
            self.remote(send_a, self.one_a, 22, 24, self.peers["x"]),
            self.remote(send_b, self.one_b, 23, 25, self.peers["y"]),
        ]

    def seconds(self):
        return [
            self.remote(self.keep_a.at[:, 1 - self.y], self.two_a, 4, 6, self.peers["y"]),
            self.remote(self.keep_b.at[:, 1 - self.x], self.two_b, 5, 7, self.peers["x"]),
        ]

    def merge_first(self):
        def body(i, carry):
            for half in range(2):
                self.keep_a[i, half] = plus(self.keep_a[i, half], self.one_a[i, half])
                self.keep_b[i, half] = plus(self.keep_b[i, half], self.one_b[i, half])
            return carry

        lax.fori_loop(0, 4, body, 0)
        for copy in self.seconds():
            copy.start()

    def from_end(self):
        first = 1 - lax.div(self.z, 3)
        return self.remote(self.layer.at[pl.ds(first, 3)], self.three, 8, 9, self.peers["beside"])

    def to_end(self):
        return self.remote(self.layer.at[self.peers["end_z"]], self.near, 10, 11, self.peers["beside"])

    def across_inner(self):
        return self.remote(self.merged.at[0], self.far, 12, 14, self.peers["other_inner"])

    def across_end(self):
        return self.remote(self.merged.at[1], self.far, 13, 14, self.peers["far_end"])

    def merge_second(self):
        for copy in self.seconds():
            copy.wait_recv()

        def body(i, carry):
            self.layer[i, 0] = plus(self.keep_a[i, self.y], self.two_a[i])
            self.layer[i, 1] = plus(self.keep_b[i, self.x], self.two_b[i])
            return carry

        lax.fori_loop(0, 4, body, 0)

        @pl.when(self.inner)
        def _():
            self.to_end().start()

        @pl.when(jnp.logical_not(self.inner))
        def _():
            self.from_end().start()

    def merge_third(self):
        @pl.when(self.inner)
        def _():
            self.from_end().wait_recv()

            def body(i, carry):
                self.merged[0, i] = plus(self.layer[3 - self.z, i], self.three[1, i])
                self.merged[1, i] = plus(self.layer[6 - 3 * self.z, i], self.three[4 - 2 * self.z, i])
                return carry

            lax.fori_loop(0, 2, body, 0)
            self.across_inner().start()
            self.across_end().start()

    def own(self):
        return pltpu.make_async_copy(self.done, self.out(self.core, self.y), self.signals(15))

    def to_y(self):
        return self.remote(self.done, self.out(self.core, self.y), 16, 17, self.peers["y"])

    def to_core(self):
        return self.remote(self.done, self.out(self.core, self.y), 18, 19, self.peers["core"])

    def passed(self):
        place = self.out(self.core, 1 - self.y)
        return self.remote(place, place, 20, 21, self.peers["core"])

    def finish(self):
        self.across_inner().wait_recv()

        @pl.when(self.inner)
        def _():
            def body(i, carry):
                total = self.layer[self.z, i].astype(jnp.float32) + self.far[i].astype(jnp.float32)
                total = total + self.three[2 * self.z - 2, i].astype(jnp.float32)
                self.done[i] = total.astype(jnp.bfloat16)
                return carry

            lax.fori_loop(0, 2, body, 0)

        @pl.when(jnp.logical_not(self.inner))
        def _():
            self.to_end().wait_recv()

            def body(i, carry):
                total = self.layer[self.z, i].astype(jnp.float32) + self.far[i].astype(jnp.float32)
                total = total + self.near[i].astype(jnp.float32)
                self.done[i] = total.astype(jnp.bfloat16)
                return carry

            lax.fori_loop(0, 2, body, 0)

        self.own().start()
        self.to_y().start()
        self.to_core().start()

    def hand_on(self):
        self.to_y().wait_recv()
        self.passed().start()

    def drain(self):
        for copy in self.seconds():
            copy.wait_send()

        @pl.when(self.inner)
        def _():
            self.to_end().wait_send()
            self.across_inner().wait_send()
            self.across_end().wait_send()

        @pl.when(jnp.logical_not(self.inner))
        def _():
            self.from_end().wait_send()

        self.own().wait()
        self.to_y().wait_send()
        self.to_core().wait()
        self.passed().wait()


def reduce_kernel(chunks, keep_ref, came_a, came_b, weight_ref, out_ref, weight_out, *scratch):
    rows, weights, signals = scratch[:12], scratch[12:24], scratch[24]
    dp = lax.axis_index("dp")
    store = lax.axis_index("store")
    y, core = lax.div(dp, 2), lax.rem(dp, 2)
    z, x = lax.div(store, 2), lax.rem(store, 2)
    inner = (z == 1) | (z == 2)
    beside = z + 1 - 2 * lax.rem(z, 2)
    along = lambda to: (dp, to * 2 + x)
    peers = {
        "x": (dp, z * 2 + (1 - x)),
        "y": ((1 - y) * 2 + core, store),
        "core": (y * 2 + (1 - core), store),
        "beside": along(beside),
        "end_z": 3 * lax.div(z, 2),
        "other_inner": along(3 - z),
        "far_end": along(3 - 3 * lax.div(z, 2)),
    }
    place = (x, y, z, core, inner, peers)

    barrier = pltpu.get_barrier_semaphore()
    for peer in (peers["x"], peers["y"], peers["core"]) + tuple(along(lax.rem(z + hop, 4)) for hop in (1, 2, 3)):
        pl.semaphore_signal(barrier, inc=1, device_id=peer, device_id_type=MESH_ID)
    pl.semaphore_wait(barrier, 6)

    units = [
        Unit(
            place, lambda kind, q=q: signals.at[kind, q], [ref.at[q] for ref in rows],
            lambda c, h, q=q: out_ref.at[c, h, :, q],
        )
        for q in range(chunks)
    ]
    extra = Unit(
        place, lambda kind: signals.at[kind, chunks], weights, lambda c, h: weight_out.at[c, h]
    )
    extra_first = extra.firsts(weight_ref.at[:, 1 - x, :, 0], weight_ref.at[:, :, 1 - y, 1])
    extra_loads = extra.loads((weight_ref.at[:, x, :, 0], weight_ref.at[:, :, y, 1]))
    loads = [
        unit.loads((keep_ref.at[0, :, :, q], keep_ref.at[1, :, :, q], came_a.at[:, :, q], came_b.at[:, :, q]))
        for q, unit in enumerate(units)
    ]
    for copy in loads[0] + extra_first + extra_loads:
        copy.start()
    for some in loads[1:]:
        for copy in some:
            copy.start()
    for step in range(chunks + 4):
        if step < chunks:
            for copy in loads[step]:
                copy.wait()
            units[step].merge_first()
        if step == 2:
            for copy in extra_loads:
                copy.wait()
            for copy in extra_first:
                copy.wait_recv()
            extra.merge_first()
        for stage, name in enumerate(("merge_second", "merge_third", "finish", "hand_on")):
            if 0 <= step - 1 - stage < chunks:
                getattr(units[step - 1 - stage], name)()
            if step == 4 + stage:
                getattr(extra, name)()
    for copy in extra_first:
        copy.wait_send()
    for unit in units + [extra]:
        unit.drain()


def reduce_rows(keep, came_a, came_b, weights, collective_id=0):
    rows = keep.shape[0] // 4
    chunks = rows // (4 * CHUNK)
    high = weights.shape[0] // 32

    def spare(high, *lead):
        return [
            pltpu.VMEM(lead + part + (high, D), jnp.bfloat16)
            for part in ((4, 2),) * 4 + ((4,), (4,), (4, 2), (3, 2), (2, 2), (2,), (2,), (2,))
        ]

    out, weights = pl.pallas_call(
        functools.partial(reduce_kernel, chunks),
        out_shape=[
            jax.ShapeDtypeStruct((2, 2, 2, chunks, CHUNK, D), jnp.bfloat16),
            jax.ShapeDtypeStruct((2, 2, 2, high, D), jnp.bfloat16),
        ],
        in_specs=[pl.BlockSpec(memory_space=pl.ANY)] * 4,
        out_specs=[pl.BlockSpec(memory_space=pl.ANY)] * 2,
        scratch_shapes=spare(CHUNK, chunks) + spare(high) + [pltpu.SemaphoreType.DMA((SIGNALS, chunks + 1))],
        compiler_params=pltpu.CompilerParams(
            collective_id=collective_id, has_side_effects=True, vmem_limit_bytes=VMEM_LIMIT
        ),
        cost_estimate=pl.CostEstimate(flops=0, transcendentals=0, bytes_accessed=450_000_000),
        name="reduce_rows",
    )(
        keep.reshape(2, 4, 2, chunks, CHUNK, D),
        came_a.reshape(4, 2, chunks, CHUNK, D),
        came_b.reshape(4, 2, chunks, CHUNK, D),
        weights.reshape(4, 2, 2, 2, high, D),
    )
    return out.reshape(2 * rows, D), weights.reshape(8 * high, D)


PAIRS = ((0, 1), (1, 0), (2, 3), (3, 2))


def own_rows(flat, rows_here):
    half = rows_here // 2
    quarter = half // 4
    dp = lax.axis_index("dp")
    here_y, core = dp // 2, dp % 2
    here_x = lax.axis_index("store") % 2
    owner, local = flat // rows_here, flat % rows_here
    z, x = owner // 2, owner % 2
    y = (local % half) // (2 * quarter)
    second = (local // quarter) % 2
    stays = jnp.where(second == 0, x == here_x, y == here_y)
    pair = jnp.where(second == 0, y, x)
    rows = 8 * half
    target = (2 * stays + second) * (rows // 4) + (2 * z + pair) * quarter + local % quarter
    return jnp.where(local // half == core, target, rows)


def plan_store(indices, rows_here):
    flat = indices.reshape(-1)
    other = lax.ppermute(flat, "dp", PAIRS)
    where = jnp.concatenate([own_rows(flat, rows_here), own_rows(other, rows_here)])
    return scatter_plan(where, lax.axis_size("store") * rows_here // 2)


def add_store(plan, own, other, rows_here):
    return scatter_rows(plan, own, other, lax.axis_size("store") * rows_here // 2)


def swap_store(send_a, send_b):
    owners = lax.axis_size("store")
    came_a = lax.ppermute(send_a, "store", [(i, i ^ 1) for i in range(owners)])
    came_b = lax.ppermute(send_b, "dp", [(i, i ^ 2) for i in range(4)])
    return came_a, came_b


def by_owner(matrix):
    owners = lax.axis_size("store")
    return matrix.astype(jnp.bfloat16).reshape(owners, -1, D)


def reduce_packed(packed):
    return lax.psum_scatter(packed.reshape(-1, D), ("store", "dp"), scatter_dimension=0, tiled=True)


def all_copies(share):
    return lax.all_gather(share, "dp", axis=0, tiled=True).astype(jnp.float32)


def pack_early(inner, outer, squares):
    blocks = [inner[:, block * D : (block + 1) * D] for block in range(inner.shape[1] // D)]
    return jnp.concatenate([by_owner(piece) for piece in blocks + [outer] + list(squares)], axis=1)


def unpack_early(total, wide):
    part = D // lax.axis_size("store")
    inner_total = jnp.transpose(total[: wide * part].reshape(wide, part, D), (1, 0, 2))
    rest = total[wide * part :]
    return (
        inner_total.reshape(part, wide * D),
        rest[: wide * part],
        rest[wide * part :].reshape(-1, part, D),
    )


def pack_late(squares, features, inner_bias):
    owners = lax.axis_size("store")
    part = D // owners
    wide = inner_bias.shape[0] // D
    small = jnp.concatenate(
        [feature.astype(jnp.bfloat16).reshape(owners, part) for feature in features]
        + [inner_bias.astype(jnp.bfloat16).reshape(owners, wide * part)],
        axis=1,
    )
    small = jnp.pad(small, ((0, 0), (0, part * D - small.shape[1]))).reshape(owners, part, D)
    return jnp.concatenate([by_owner(square) for square in squares] + [small], axis=1)


def add_cores(packed):
    core = lax.axis_index("dp") % 2
    halves = packed.reshape(packed.shape[0], 2, -1, D)
    mine = lax.dynamic_index_in_dim(halves, core, axis=1, keepdims=False)
    other = lax.dynamic_index_in_dim(halves, 1 - core, axis=1, keepdims=False)
    other = lax.ppermute(other, "dp", PAIRS)
    return plus(mine, other).reshape(-1, D)


def unpack_late(total, count, features, wide):
    part = D // lax.axis_size("store")
    tail = total[count * part :].reshape(-1)
    table = tail[: features * part].reshape(features, part)
    return (
        total[: count * part].reshape(count, part, D),
        table,
        tail[features * part :][: wide * part],
    )


def cross_probs_of(folded, rows):
    scores = lax.dot_general(folded, rows, (((1,), (1,)), ((), ())), preferred_element_type=jnp.float32)
    token = lax.broadcasted_iota(jnp.int32, scores.shape, 0) % CROSS_TOKENS
    owner = lax.broadcasted_iota(jnp.int32, scores.shape, 1) // K
    scores = jnp.where(token == owner, scores, -1e30)
    raised = jnp.exp(scores - jnp.max(scores, axis=1, keepdims=True))
    return raised * (1.0 / jnp.sum(raised, axis=1, keepdims=True))


def cross_tiles(ref):
    tokens = ref.shape[1]
    for first in range(0, tokens, CROSS_TOKENS):
        yield pl.ds(first, CROSS_TOKENS), pl.ds(first * K, CROSS_TOKENS * K)


def cross_forward_kernel(folded_ref, first_ref, second_ref, which_ref, rows_ref, summary_ref):
    for some, slots in cross_tiles(folded_ref):
        which = which_ref[slots, :] != 0
        rows = jnp.where(
            which, second_ref[slots, :].astype(jnp.float32), first_ref[slots, :].astype(jnp.float32)
        ).astype(jnp.bfloat16)
        rows_ref[slots, :] = rows
        probs = cross_probs_of(folded_ref[:, some, :].reshape(H * CROSS_TOKENS, D), rows)
        summary = jnp.dot(probs.astype(jnp.bfloat16), rows, preferred_element_type=jnp.float32)
        summary_ref[:, some, :] = summary.astype(jnp.bfloat16).reshape(H, CROSS_TOKENS, D)


def cross_backward_kernel(folded_ref, grad_ref, rows_ref, row_grad_ref, folded_grad_ref):
    for some, slots in cross_tiles(folded_ref):
        rows = rows_ref[slots, :]
        folded = folded_ref[:, some, :].reshape(H * CROSS_TOKENS, D)
        grad = grad_ref[:, some, :].reshape(H * CROSS_TOKENS, D)
        probs = cross_probs_of(folded, rows)
        prob_grad = lax.dot_general(
            grad, rows, (((1,), (1,)), ((), ())), preferred_element_type=jnp.float32
        )
        total = jnp.sum(probs * prob_grad, axis=1, keepdims=True)
        score_low = (probs * (prob_grad - total)).astype(jnp.bfloat16)
        turned = (((0,), (0,)), ((), ()))
        row_grad = lax.dot_general(
            probs.astype(jnp.bfloat16), grad, turned, preferred_element_type=jnp.float32
        )
        row_grad += lax.dot_general(score_low, folded, turned, preferred_element_type=jnp.float32)
        row_grad_ref[slots, :] = row_grad.astype(jnp.bfloat16)
        folded_grad = jnp.dot(score_low, rows, preferred_element_type=jnp.float32)
        folded_grad_ref[:, some, :] = folded_grad.astype(jnp.bfloat16).reshape(H, CROSS_TOKENS, D)


CROSS_TOKENS = 16
CROSS_STEP = 64


def cross_specs():
    heads = pl.BlockSpec((H, CROSS_STEP, D), lambda i: (0, i, 0))
    rows = pl.BlockSpec((CROSS_STEP * K, D), lambda i: (i, 0))
    return heads, rows


def cross_forward(folded, first, second, which):
    heads, rows = cross_specs()
    tokens = folded.shape[1]
    return pl.pallas_call(
        cross_forward_kernel,
        out_shape=[
            jax.ShapeDtypeStruct((tokens * K, D), jnp.bfloat16),
            jax.ShapeDtypeStruct((H, tokens, D), jnp.bfloat16),
        ],
        grid=(tokens // CROSS_STEP,),
        in_specs=[heads, rows, rows, pl.BlockSpec((CROSS_STEP * K, 1), lambda i: (i, 0))],
        out_specs=[rows, heads],
        cost_estimate=pl.CostEstimate(flops=0, transcendentals=0, bytes_accessed=65_000_000),
        name="cross_forward",
    )(folded, first, second, which)


def cross_backward(folded, grad, fetched):
    heads, rows = cross_specs()
    tokens = folded.shape[1]
    return pl.pallas_call(
        cross_backward_kernel,
        out_shape=[
            jax.ShapeDtypeStruct((tokens * K, D), jnp.bfloat16),
            jax.ShapeDtypeStruct((H, tokens, D), jnp.bfloat16),
        ],
        grid=(tokens // CROSS_STEP,),
        in_specs=[heads, heads, rows],
        out_specs=[rows, heads],
        cost_estimate=pl.CostEstimate(flops=0, transcendentals=0, bytes_accessed=100_000_000),
        name="cross_backward",
    )(folded, grad, fetched)


def body(
    tokens,
    datastore,
    indices,
    lengths,
    proj_weight,
    out_weight,
    proj_bias,
    norm_gain,
    norm_bias,
    inner_weight,
    inner_bias,
    outer_weight,
    outer_bias,
    cotangent,
):
    seq_len = tokens.shape[0]
    score_scale = HD ** (-0.5)
    owners = lax.axis_size("store")
    rows_here = datastore.shape[0]
    capacity = 2 * seq_len * K // owners
    position = jnp.arange(seq_len)
    length = lengths[0]
    allowed = (position[None, :] <= position[:, None]) & (position[None, :] < length)
    valid = (position < length)[:, None]
    dense = is_dense(owners, rows_here)
    if dense:
        plan = plan_store(indices, rows_here)
        found_first, found_second, which_half, plan = fetch_dense(datastore, indices, plan)
    else:
        target, request = route_slots(indices, rows_here, owners, capacity)
        returned, _ = fetch_rows(request, datastore)
        fetched = returned.reshape(owners * capacity, D)[target].reshape(seq_len, K, D)
    self_bias = jnp.concatenate([proj_bias[:, 0], jnp.zeros((D,), jnp.float32), proj_bias[:, 1]])
    self_proj = proj_weight[:, 0:3, :].reshape(D, 3 * D)
    joined = (product(tokens, self_proj) + self_bias).astype(jnp.bfloat16)
    queries = joined[:, :D].reshape(seq_len, H, HD)
    self_keys = joined[:, D : 2 * D].reshape(seq_len, H, HD)
    values = joined[:, 2 * D :].reshape(seq_len, H, HD)
    scores = self_scores(queries, self_keys, allowed, score_scale)
    self_lse = log_total(scores)
    self_probs = jnp.exp(scores - self_lse).astype(jnp.bfloat16)
    self_mixed = (
        jnp.einsum("hqk,khe->qhe", self_probs, values, preferred_element_type=jnp.float32)
        .reshape(seq_len, D)
        .astype(jnp.bfloat16)
    )
    first_pre = tokens.astype(jnp.float32) + (
        product(self_mixed, out_weight[:, 0, :]) + proj_bias[:, 2]
    )
    first_out, first_normed, first_inverse = norm_forward(
        first_pre, norm_gain[:, 0], norm_bias[:, 0]
    )
    first_low = first_out.astype(jnp.bfloat16)
    cross_query = (
        (product(first_low, proj_weight[:, 3, :]) + proj_bias[:, 3])
        .astype(jnp.bfloat16)
        .reshape(seq_len, H, HD)
    )
    key_heads = proj_weight[:, 4, :].reshape(D, H, HD)
    folded = (
        jnp.einsum("the,dhe->thd", cross_query, key_heads, preferred_element_type=jnp.float32)
        * score_scale
    ).astype(jnp.bfloat16)
    if dense:
        folded_heads = jnp.transpose(folded, (1, 0, 2))
        fetched, summary = cross_forward(folded_heads, found_first, found_second, which_half)
        summary = jnp.transpose(summary, (1, 0, 2))
    else:
        cross_scores = jnp.einsum("thd,tkd->thk", folded, fetched, preferred_element_type=jnp.float32)
        cross_lse = log_total(cross_scores)
        cross_full = jnp.exp(cross_scores - cross_lse)
        cross_probs = cross_full.astype(jnp.bfloat16)
        summary = jnp.einsum(
            "thk,tkd->thd", cross_probs, fetched, preferred_element_type=jnp.float32
        ).astype(jnp.bfloat16)
    value_heads = proj_weight[:, 5, :].reshape(D, H, HD)
    cross_mixed = (
        jnp.einsum(
            "thd,dhe->the", summary, value_heads, preferred_element_type=jnp.float32
        ).reshape(seq_len, D)
        + proj_bias[:, 4]
    ).astype(jnp.bfloat16)
    second_pre = first_out + (product(cross_mixed, out_weight[:, 1, :]) + proj_bias[:, 5])
    second_out, second_normed, second_inverse = norm_forward(
        second_pre, norm_gain[:, 1], norm_bias[:, 1]
    )
    second_low = second_out.astype(jnp.bfloat16)
    inner_pre = product(second_low, inner_weight) + inner_bias
    activated = jax.nn.gelu(inner_pre, approximate=False).astype(jnp.bfloat16)
    third_pre = second_out + (product(activated, outer_weight) + outer_bias)
    third_out, third_normed, third_inverse = norm_forward(
        third_pre, norm_gain[:, 2], norm_bias[:, 2]
    )
    output = jnp.where(valid, third_out, 0.0).astype(jnp.bfloat16)
    upstream = jnp.where(valid, cotangent.astype(jnp.float32), 0.0)
    third_grad, gain_three, shift_three = norm_backward(
        upstream, third_normed, third_inverse, norm_gain[:, 2]
    )
    outer_low = third_grad.astype(jnp.bfloat16)
    grad_outer_weight = contract_rows(activated, outer_low)
    grad_outer_bias = column_sum(outer_low)
    act_grad = product_back(outer_low, outer_weight)
    slope = jax.vjp(lambda activation_in: jax.nn.gelu(activation_in, approximate=False), inner_pre)[
        1
    ](act_grad)[0]
    inner_low = slope.astype(jnp.bfloat16)
    grad_inner_weight = contract_rows(second_low, inner_low)
    grad_inner_bias = column_sum(inner_low)
    second_up = third_grad + product_back(inner_low, inner_weight)
    second_grad, gain_two, shift_two = norm_backward(
        second_up, second_normed, second_inverse, norm_gain[:, 1]
    )
    cross_out_low = second_grad.astype(jnp.bfloat16)
    grad_cross_out = contract_rows(cross_mixed, cross_out_low)
    bias_five = column_sum(cross_out_low)
    mixed_low = product_back(cross_out_low, out_weight[:, 1, :]).astype(jnp.bfloat16)
    bias_four = column_sum(mixed_low)
    mixed_heads = mixed_low.reshape(seq_len, H, HD)
    grad_value_heads = jnp.einsum(
        "thd,the->dhe", summary, mixed_heads, preferred_element_type=jnp.float32
    )
    if dense:
        packed_early = pack_early(grad_inner_weight, grad_outer_weight, (grad_cross_out,))
        mixed_heads, packed_early = lax.optimization_barrier((mixed_heads, packed_early))
        share_early = reduce_packed(packed_early)
    summary_low = jnp.einsum(
        "the,dhe->thd", mixed_heads, value_heads, preferred_element_type=jnp.float32
    ).astype(jnp.bfloat16)
    if dense:
        own_grad, folded_low = cross_backward(
            folded_heads, jnp.transpose(summary_low, (1, 0, 2)), fetched
        )
        folded_low = jnp.transpose(folded_low, (1, 0, 2))
        other_grad = lax.ppermute(own_grad, "dp", PAIRS)
    else:
        returned_again, asked_back = fetch_again(request, datastore)
        fetched_back = returned_again.reshape(owners * capacity, D)[target].reshape(seq_len, K, D)
        prob_grad = jnp.einsum(
            "thd,tkd->thk", summary_low, fetched_back, preferred_element_type=jnp.float32
        )
        score_low = (
            cross_full * (prob_grad - jnp.sum(cross_full * prob_grad, axis=-1, keepdims=True))
        ).astype(jnp.bfloat16)
        row_grad = (
            jnp.einsum("thk,thd->tkd", cross_probs, summary_low, preferred_element_type=jnp.float32)
            + jnp.einsum("thk,thd->tkd", score_low, folded, preferred_element_type=jnp.float32)
        ).astype(jnp.bfloat16)
        folded_low = jnp.einsum(
            "thk,tkd->thd", score_low, fetched_back, preferred_element_type=jnp.float32
        ).astype(jnp.bfloat16)
    grad_key_heads = (
        jnp.einsum("thd,the->dhe", folded_low, cross_query, preferred_element_type=jnp.float32)
        * score_scale
    )
    query_low = (
        (
            jnp.einsum("thd,dhe->the", folded_low, key_heads, preferred_element_type=jnp.float32)
            * score_scale
        )
        .astype(jnp.bfloat16)
        .reshape(seq_len, D)
    )
    if dense:
        query_low, other_grad = lax.optimization_barrier((query_low, other_grad))
        send_a, send_b, keep = add_store(plan, own_grad, other_grad, rows_here)
        query_low, mixed_heads, send_a, send_b, keep = lax.optimization_barrier(
            (query_low, mixed_heads, send_a, send_b, keep)
        )
        grad_value_heads = jnp.einsum(
            "thd,the->dhe", summary, mixed_heads, preferred_element_type=jnp.float32
        )
        came_a, came_b = swap_store(send_a, send_b)
    bias_three = column_sum(query_low)
    grad_cross_query = contract_rows(first_low, query_low)
    if not dense:
        grad_buffer = (
            jnp.zeros((owners * capacity, D), jnp.bfloat16)
            .at[target]
            .set(row_grad.reshape(-1, D))
            .reshape(owners, capacity, D)
        )
        arrived = lax.all_to_all(grad_buffer, "store", split_axis=0, concat_axis=0, tiled=True)
        partial_store = (
            jnp.zeros((rows_here, D), jnp.float32)
            .at[asked_back.reshape(-1)]
            .add(arrived.reshape(-1, D).astype(jnp.float32))
        )
        grad_store = lax.psum(partial_store.astype(jnp.bfloat16), "dp").astype(jnp.float32)
    first_up = second_grad + product_back(query_low, proj_weight[:, 3, :])
    first_grad, gain_one, shift_one = norm_backward(
        first_up, first_normed, first_inverse, norm_gain[:, 0]
    )
    self_out_low = first_grad.astype(jnp.bfloat16)
    grad_self_out = contract_rows(self_mixed, self_out_low)
    bias_two = column_sum(self_out_low)
    self_mixed_low = (
        product_back(self_out_low, out_weight[:, 0, :]).astype(jnp.bfloat16).reshape(seq_len, H, HD)
    )
    value_grad = jnp.einsum(
        "hqk,qhe->khe", self_probs, self_mixed_low, preferred_element_type=jnp.float32
    )
    attend_grad = jnp.einsum(
        "qhe,khe->hqk", self_mixed_low, values, preferred_element_type=jnp.float32
    )
    self_full = jnp.exp(self_scores(queries, self_keys, allowed, score_scale) - self_lse)
    self_score_low = (
        self_full * (attend_grad - jnp.sum(self_full * attend_grad, axis=-1, keepdims=True))
    ).astype(jnp.bfloat16)
    query_grad = (
        jnp.einsum("hqk,khe->qhe", self_score_low, self_keys, preferred_element_type=jnp.float32)
        * score_scale
    )
    key_grad = (
        jnp.einsum("hqk,qhe->khe", self_score_low, queries, preferred_element_type=jnp.float32)
        * score_scale
    )
    joined_low = jnp.concatenate(
        [
            query_grad.reshape(seq_len, D),
            key_grad.reshape(seq_len, D),
            value_grad.reshape(seq_len, D),
        ],
        axis=1,
    ).astype(jnp.bfloat16)
    grad_self_proj = contract_rows(tokens, joined_low).reshape(D, 3, D)
    bias_zero = column_sum(joined_low[:, :D])
    bias_one = column_sum(joined_low[:, 2 * D :])
    grad_tokens = (first_grad + product_back(joined_low, self_proj)).astype(jnp.bfloat16)
    if dense:
        packed_late = pack_late(
            (
                grad_self_proj[:, 0],
                grad_self_proj[:, 1],
                grad_self_proj[:, 2],
                grad_cross_query,
                grad_key_heads.reshape(D, D),
                grad_value_heads.reshape(D, D),
                grad_self_out,
            ),
            (bias_zero, bias_one, bias_two, bias_three, bias_four, bias_five)
            + (gain_one, gain_two, gain_three)
            + (shift_one, shift_two, shift_three)
            + (grad_outer_bias,),
            grad_inner_bias,
        )
        wide = grad_inner_bias.shape[0] // D
        early_totals = unpack_early(all_copies(share_early), wide)
        keep, came_a, came_b, output, grad_tokens, early_totals = lax.optimization_barrier(
            (keep, came_a, came_b, output, grad_tokens, early_totals)
        )
        inner_total, outer_total, early = early_totals
        grad_store, total_late = reduce_rows(keep, came_a, came_b, add_cores(packed_late))
        grad_store = grad_store.astype(jnp.float32)
        late, table, bias_inner = unpack_late(total_late.astype(jnp.float32), 7, 13, wide)
        return (
            output,
            grad_tokens,
            grad_store,
            jnp.stack([late[0], late[1], late[2], late[3], late[4], late[5]], axis=1),
            jnp.stack([late[6], early[0]], axis=1),
            jnp.transpose(table[0:6]),
            jnp.transpose(table[6:9]),
            jnp.transpose(table[9:12]),
            inner_total,
            bias_inner,
            outer_total,
            table[12],
        )
    grad_proj = jnp.stack(
        [
            grad_self_proj[:, 0],
            grad_self_proj[:, 1],
            grad_self_proj[:, 2],
            grad_cross_query,
            grad_key_heads.reshape(D, D),
            grad_value_heads.reshape(D, D),
        ],
        axis=1,
    )
    grad_out = jnp.stack([grad_self_out, grad_cross_out], axis=1)
    grad_bias = jnp.stack([bias_zero, bias_one, bias_two, bias_three, bias_four, bias_five], axis=1)
    grad_gain = jnp.stack([gain_one, gain_two, gain_three], axis=1)
    grad_shift = jnp.stack([shift_one, shift_two, shift_three], axis=1)
    shares = (
        lax.psum_scatter(
            grad_proj.astype(jnp.bfloat16), "store", scatter_dimension=0, tiled=True
        ).astype(jnp.float32),
        lax.psum_scatter(
            grad_out.astype(jnp.bfloat16), "store", scatter_dimension=0, tiled=True
        ).astype(jnp.float32),
        lax.psum_scatter(
            grad_bias.astype(jnp.bfloat16), "store", scatter_dimension=0, tiled=True
        ).astype(jnp.float32),
        lax.psum_scatter(
            grad_gain.astype(jnp.bfloat16), "store", scatter_dimension=0, tiled=True
        ).astype(jnp.float32),
        lax.psum_scatter(
            grad_shift.astype(jnp.bfloat16), "store", scatter_dimension=0, tiled=True
        ).astype(jnp.float32),
        lax.psum_scatter(
            grad_inner_weight.astype(jnp.bfloat16), "store", scatter_dimension=0, tiled=True
        ).astype(jnp.float32),
        lax.psum_scatter(
            grad_inner_bias.astype(jnp.bfloat16), "store", scatter_dimension=0, tiled=True
        ).astype(jnp.float32),
        lax.psum_scatter(
            grad_outer_weight.astype(jnp.bfloat16), "store", scatter_dimension=0, tiled=True
        ).astype(jnp.float32),
        lax.psum_scatter(
            grad_outer_bias.astype(jnp.bfloat16), "store", scatter_dimension=0, tiled=True
        ).astype(jnp.float32),
    )
    totals = (
        lax.psum(shares[0].astype(jnp.bfloat16), "dp").astype(jnp.float32),
        lax.psum(shares[1].astype(jnp.bfloat16), "dp").astype(jnp.float32),
        lax.psum(shares[2].astype(jnp.bfloat16), "dp").astype(jnp.float32),
        lax.psum(shares[3].astype(jnp.bfloat16), "dp").astype(jnp.float32),
        lax.psum(shares[4].astype(jnp.bfloat16), "dp").astype(jnp.float32),
        lax.psum(shares[5].astype(jnp.bfloat16), "dp").astype(jnp.float32),
        lax.psum(shares[6].astype(jnp.bfloat16), "dp").astype(jnp.float32),
        lax.psum(shares[7].astype(jnp.bfloat16), "dp").astype(jnp.float32),
        lax.psum(shares[8].astype(jnp.bfloat16), "dp").astype(jnp.float32),
    )
    return (
        output,
        grad_tokens,
        grad_store,
        totals[0],
        totals[1],
        totals[2],
        totals[3],
        totals[4],
        totals[5],
        totals[6],
        totals[7],
        totals[8],
    )


def solution(mesh):
    in_specs = (
        P(("dp", "store"), None),
        P("store", None),
        P(("dp", "store"), None),
        P(("dp", "store")),
        P(),
        P(),
        P(),
        P(),
        P(),
        P(),
        P(),
        P(),
        P(),
        P(("dp", "store"), None),
    )
    out_specs = (
        P(("dp", "store"), None),
        P(("dp", "store"), None),
        P("store", None),
        P("store", None, None),
        P("store", None, None),
        P("store", None),
        P("store", None),
        P("store", None),
        P("store", None),
        P("store"),
        P("store", None),
        P("store"),
    )

    return jax.shard_map(body, mesh=mesh, in_specs=in_specs, out_specs=out_specs, check_vma=False)
```

```python
import functools

import jax
import jax.numpy as jnp
from jax import lax
from jax.experimental import pallas as pl
from jax.experimental.pallas import tpu as pltpu
from jax.sharding import PartitionSpec as P


D = 768
H = 12
HD = 64
K = 16


EPSILON = 1e-05


def product(matrix, factor):
    return jnp.dot(matrix, factor, preferred_element_type=jnp.float32)


def product_back(matrix, weight):
    return jnp.einsum("tf,df->td", matrix, weight, preferred_element_type=jnp.float32)


def contract_rows(matrix, factor):
    return jnp.einsum("td,tf->df", matrix, factor, preferred_element_type=jnp.float32)


def column_sum(matrix):
    return jnp.sum(matrix.astype(jnp.float32), axis=0)


def norm_forward(hidden, norm_weight, norm_shift):
    centered = hidden - jnp.mean(hidden, axis=-1, keepdims=True)
    inverse = lax.rsqrt(jnp.mean(centered * centered, axis=-1, keepdims=True) + EPSILON)
    normed = centered * inverse
    return (normed * norm_weight + norm_shift, normed, inverse)


def norm_backward(upstream, normed, inverse, norm_weight):
    scaled = upstream * norm_weight
    plain_mean = jnp.mean(scaled, axis=-1, keepdims=True)
    normed_mean = jnp.mean(scaled * normed, axis=-1, keepdims=True)
    return (
        inverse * (scaled - plain_mean - normed * normed_mean),
        jnp.sum(upstream * normed, axis=0),
        jnp.sum(upstream, axis=0),
    )


def log_total(scores):
    highest = jnp.max(scores, axis=-1, keepdims=True)
    return highest + jnp.log(jnp.sum(jnp.exp(scores - highest), axis=-1, keepdims=True))


def route_slots(picked, rows_here, owners, capacity):
    flat_ids = picked.reshape(-1)
    owner_of = flat_ids // rows_here
    local_row = flat_ids % rows_here
    by_owner = jnp.argsort(owner_of, stable=True)
    sorted_owner = owner_of[by_owner]
    owner_loads = jnp.sum(
        (owner_of[:, None] == jnp.arange(owners, dtype=jnp.int32)[None, :]).astype(jnp.int32),
        axis=0,
    )
    starts = jnp.cumsum(owner_loads) - owner_loads
    within = jnp.arange(flat_ids.shape[0], dtype=jnp.int32) - starts[sorted_owner]
    placed = jnp.zeros_like(flat_ids).at[by_owner].set(within)
    target = owner_of * capacity + placed
    request = jnp.zeros((owners * capacity,), jnp.int32).at[target].set(local_row)
    return (target, request.reshape(owners, capacity))


def fetch_rows(request, datastore):
    asked_rows = lax.all_to_all(request, "store", split_axis=0, concat_axis=0, tiled=True)
    found_rows = datastore[asked_rows.reshape(-1)].reshape(asked_rows.shape + (datastore.shape[1],))
    return (
        lax.all_to_all(found_rows, "store", split_axis=0, concat_axis=0, tiled=True),
        asked_rows,
    )


def fetch_again(request, datastore):
    asked_rows = lax.all_to_all(request, "store", split_axis=0, concat_axis=0, tiled=True)
    found_rows = datastore[asked_rows.reshape(-1)].reshape(asked_rows.shape + (datastore.shape[1],))
    return (
        lax.all_to_all(found_rows, "store", split_axis=0, concat_axis=0, tiled=True),
        asked_rows,
    )


def self_scores(queries, self_keys, allowed, score_scale):
    scores = (
        jnp.einsum("qhe,khe->hqk", queries, self_keys, preferred_element_type=jnp.float32)
        * score_scale
    )
    return jnp.where(allowed[None], scores, -1e30)


DENSE_LIMIT = 1 << 16


def is_dense(owners, rows_here):
    fits = owners * rows_here <= DENSE_LIMIT and rows_here % (8 * CHUNK) == 0
    return fits and owners == 8 and lax.axis_size("dp") == 4


STORE_PARTS = 2


def fetch_dense(datastore, indices, plan):
    copies = lax.axis_size("dp")
    rows_here = datastore.shape[0]
    share = rows_here // copies
    part = share // STORE_PARTS
    flat = indices.reshape(-1)
    which = (flat % share) // part
    local = (flat // share) * part + flat % part
    start = lax.axis_index("dp") * share
    found = []
    earlier = None
    for index in range(STORE_PARTS):
        mine = lax.dynamic_slice_in_dim(datastore, start + index * part, part, axis=0)
        if earlier is not None:
            mine, earlier = lax.optimization_barrier((mine, earlier))
        table = lax.all_gather(mine, ("store", "dp"), axis=0, tiled=True)
        earlier = mine
        if index == STORE_PARTS - 1:
            which, plan = lax.optimization_barrier((which, plan))
        found.append(table[local])
    return found[0], found[1], which[:, None], plan


MESH_ID = pl.DeviceIdType.MESH
VMEM_LIMIT = 67043328
CHUNK = 32


GROUP = 16


SPLIT = D // 128


def scatter_kernel(steps, block, out_rows, row_ref, from_ref, twice_ref, groups_ref, own_ref, other_ref, *rest):
    outs, (total, wide) = rest[:-2], rest[-2:]
    step = pl.program_id(0)

    @pl.when(step == 0)
    def _():
        def clear(i, carry):
            total[pl.ds(i * 192, 192), :] = jnp.zeros((192, 128), jnp.float32)
            return carry

        lax.fori_loop(0, total.shape[0] // 192, clear, 0, unroll=4)

    def widen(ref):
        def strip(i, carry):
            first = pl.multiple_of(i * 32, 32)
            value = ref[pl.ds(first, 32), :].astype(jnp.float32)
            for part in range(SPLIT):
                wide[pl.ds(first * SPLIT + part, 32, stride=SPLIT), :] = value[:, part * 128 : (part + 1) * 128]
            return carry

        lax.fori_loop(0, block // 32, strip, 0, unroll=4)

    @pl.when(step < steps // 2)
    def _():
        widen(own_ref)

    @pl.when((step >= steps // 2) & (step < steps))
    def _():
        widen(other_ref)

    @pl.when(step < steps)
    def _():
        def group(i, carry):
            first = step * block + i * GROUP
            rows = [row_ref[first + k] for k in range(GROUP)]
            came = [from_ref[first + k] for k in range(GROUP)]
            twice = twice_ref[step * (block // GROUP) + i]

            @pl.when(twice == 0)
            def _():
                sums = [total[pl.ds(rows[k], SPLIT), :] + wide[pl.ds(came[k], SPLIT), :] for k in range(GROUP)]
                for k in range(GROUP):
                    total[pl.ds(rows[k], SPLIT), :] = sums[k]

            @pl.when(twice != 0)
            def _():
                for k in range(GROUP):
                    total[pl.ds(rows[k], SPLIT), :] = total[pl.ds(rows[k], SPLIT), :] + wide[pl.ds(came[k], SPLIT), :]

            return carry

        lax.fori_loop(0, groups_ref[step], group, 0)

    def narrow(out_ref):
        def strip(i, carry):
            first = pl.multiple_of((step - steps) * out_rows * SPLIT + i * (32 * SPLIT), 32 * SPLIT)
            for part in range(SPLIT):
                value = total[pl.ds(first + part, 32, stride=SPLIT), :]
                out_ref[pl.ds(pl.multiple_of(i * 32, 32), 32), part * 128 : (part + 1) * 128] = value.astype(jnp.bfloat16)
            return carry

        lax.fori_loop(0, out_rows // 32, strip, 0, unroll=4)

    quarter = (total.shape[0] // SPLIT // 4) // out_rows
    for index, out_ref in enumerate(outs):
        last = quarter * (index + 1 if index < 2 else 4)

        @pl.when((step >= steps + quarter * index) & (step < steps + last))
        def _(out_ref=out_ref):
            narrow(out_ref)


SCATTER_BLOCK = 1024


def scatter_plan(where, rows):
    keys = jnp.arange(where.shape[0], dtype=jnp.int32).reshape(-1, SCATTER_BLOCK) % SCATTER_BLOCK
    where = where.reshape(-1, SCATTER_BLOCK)
    skipped = where >= rows
    keys, where = lax.sort((jnp.where(skipped, keys + SCATTER_BLOCK, keys), where), dimension=1, num_keys=1)
    count = jnp.sum((~skipped).astype(jnp.int32), axis=1)
    groups = (count + GROUP - 1) // GROUP
    where = jnp.where(keys >= SCATTER_BLOCK, rows + keys % GROUP, where)
    spare = lax.broadcasted_iota(jnp.int32, where.shape, 1) % GROUP
    where = jnp.where(keys >= SCATTER_BLOCK, rows + spare, where)
    eights = where.reshape(-1, GROUP)
    twice = jnp.zeros((eights.shape[0],), jnp.int32)
    for shift in range(1, GROUP):
        same = eights[:, shift:] == eights[:, :-shift]
        twice = twice | jnp.any(same, axis=1).astype(jnp.int32)
    return SPLIT * where.reshape(-1), SPLIT * (keys % SCATTER_BLOCK).reshape(-1), twice, groups


def scatter_rows(plan, own, other, rows, out_rows=512):
    block = SCATTER_BLOCK
    half = own.shape[0] // block
    steps = 2 * half
    quarter = rows // 4 // out_rows

    def part(first, count):
        return pl.BlockSpec((out_rows, D), lambda i, *_: (jnp.clip(i - steps - first, 0, count - 1), 0))

    return pl.pallas_call(
        functools.partial(scatter_kernel, steps, block, out_rows),
        out_shape=[
            jax.ShapeDtypeStruct((rows // 4, D), jnp.bfloat16),
            jax.ShapeDtypeStruct((rows // 4, D), jnp.bfloat16),
            jax.ShapeDtypeStruct((rows // 2, D), jnp.bfloat16),
        ],
        grid_spec=pltpu.PrefetchScalarGridSpec(
            num_scalar_prefetch=4,
            grid=(steps + rows // out_rows,),
            in_specs=[
                pl.BlockSpec((block, D), lambda i, *_: (jnp.minimum(i, half - 1), 0)),
                pl.BlockSpec((block, D), lambda i, *_: (jnp.clip(i - half, 0, half - 1), 0)),
            ],
            out_specs=[part(0, quarter), part(quarter, quarter), part(2 * quarter, 2 * quarter)],
            scratch_shapes=[
                pltpu.VMEM(((rows + 32) * SPLIT, 128), jnp.float32),
                pltpu.VMEM((block * SPLIT, 128), jnp.float32),
            ],
        ),
        compiler_params=pltpu.CompilerParams(vmem_limit_bytes=VMEM_LIMIT),
        cost_estimate=pl.CostEstimate(flops=0, transcendentals=0, bytes_accessed=220_000_000),
        name="scatter_rows",
    )(*plan, own, other)


SIGNALS = 26


def plus(first, second):
    return (first.astype(jnp.float32) + second.astype(jnp.float32)).astype(jnp.bfloat16)


class Unit:
    def __init__(self, place, signals, spare, out):
        self.x, self.y, self.z, self.core, self.inner, self.peers = place
        self.signals = signals
        self.keep_a, self.keep_b, self.one_a, self.one_b, self.two_a, self.two_b = spare[:6]
        self.layer, self.three, self.merged, self.near, self.far, self.done = spare[6:]
        self.out = out

    def remote(self, src, dst, send, recv, peer):
        return pltpu.make_async_remote_copy(
            src_ref=src, dst_ref=dst, send_sem=self.signals(send), recv_sem=self.signals(recv),
            device_id=peer, device_id_type=MESH_ID,
        )

    def loads(self, sources):
        places = (self.keep_a, self.keep_b, self.one_a, self.one_b)
        return [
            pltpu.make_async_copy(source, place, self.signals(index))
            for index, (source, place) in enumerate(zip(sources, places))
        ]

    def firsts(self, send_a, send_b):
        return [
            self.remote(send_a, self.one_a, 22, 24, self.peers["x"]),
            self.remote(send_b, self.one_b, 23, 25, self.peers["y"]),
        ]

    def seconds(self):
        return [
            self.remote(self.keep_a.at[:, 1 - self.y], self.two_a, 4, 6, self.peers["y"]),
            self.remote(self.keep_b.at[:, 1 - self.x], self.two_b, 5, 7, self.peers["x"]),
        ]

    def merge_first(self):
        def body(i, carry):
            for half in range(2):
                self.keep_a[i, half] = plus(self.keep_a[i, half], self.one_a[i, half])
                self.keep_b[i, half] = plus(self.keep_b[i, half], self.one_b[i, half])
            return carry

        lax.fori_loop(0, 4, body, 0)
        for copy in self.seconds():
            copy.start()

    def from_end(self):
        first = 1 - lax.div(self.z, 3)
        return self.remote(self.layer.at[pl.ds(first, 3)], self.three, 8, 9, self.peers["beside"])

    def to_end(self):
        return self.remote(self.layer.at[self.peers["end_z"]], self.near, 10, 11, self.peers["beside"])

    def across_inner(self):
        return self.remote(self.merged.at[0], self.far, 12, 14, self.peers["other_inner"])

    def across_end(self):
        return self.remote(self.merged.at[1], self.far, 13, 14, self.peers["far_end"])

    def merge_second(self):
        for copy in self.seconds():
            copy.wait_recv()

        def body(i, carry):
            self.layer[i, 0] = plus(self.keep_a[i, self.y], self.two_a[i])
            self.layer[i, 1] = plus(self.keep_b[i, self.x], self.two_b[i])
            return carry

        lax.fori_loop(0, 4, body, 0)

        @pl.when(self.inner)
        def _():
            self.to_end().start()

        @pl.when(jnp.logical_not(self.inner))
        def _():
            self.from_end().start()

    def merge_third(self):
        @pl.when(self.inner)
        def _():
            self.from_end().wait_recv()

            def body(i, carry):
                self.merged[0, i] = plus(self.layer[3 - self.z, i], self.three[1, i])
                self.merged[1, i] = plus(self.layer[6 - 3 * self.z, i], self.three[4 - 2 * self.z, i])
                return carry

            lax.fori_loop(0, 2, body, 0)
            self.across_inner().start()
            self.across_end().start()

    def own(self):
        return pltpu.make_async_copy(self.done, self.out(self.core, self.y), self.signals(15))

    def to_y(self):
        return self.remote(self.done, self.out(self.core, self.y), 16, 17, self.peers["y"])

    def to_core(self):
        return self.remote(self.done, self.out(self.core, self.y), 18, 19, self.peers["core"])

    def passed(self):
        place = self.out(self.core, 1 - self.y)
        return self.remote(place, place, 20, 21, self.peers["core"])

    def finish(self):
        self.across_inner().wait_recv()

        @pl.when(self.inner)
        def _():
            def body(i, carry):
                total = self.layer[self.z, i].astype(jnp.float32) + self.far[i].astype(jnp.float32)
                total = total + self.three[2 * self.z - 2, i].astype(jnp.float32)
                self.done[i] = total.astype(jnp.bfloat16)
                return carry

            lax.fori_loop(0, 2, body, 0)

        @pl.when(jnp.logical_not(self.inner))
        def _():
            self.to_end().wait_recv()

            def body(i, carry):
                total = self.layer[self.z, i].astype(jnp.float32) + self.far[i].astype(jnp.float32)
                total = total + self.near[i].astype(jnp.float32)
                self.done[i] = total.astype(jnp.bfloat16)
                return carry

            lax.fori_loop(0, 2, body, 0)

        self.own().start()
        self.to_y().start()
        self.to_core().start()

    def hand_on(self):
        self.to_y().wait_recv()
        self.passed().start()

    def drain(self):
        for copy in self.seconds():
            copy.wait_send()

        @pl.when(self.inner)
        def _():
            self.to_end().wait_send()
            self.across_inner().wait_send()
            self.across_end().wait_send()

        @pl.when(jnp.logical_not(self.inner))
        def _():
            self.from_end().wait_send()

        self.own().wait()
        self.to_y().wait_send()
        self.to_core().wait()
        self.passed().wait()


def reduce_kernel(chunks, keep_ref, came_a, came_b, weight_ref, out_ref, weight_out, *scratch):
    rows, weights, signals = scratch[:12], scratch[12:24], scratch[24]
    dp = lax.axis_index("dp")
    store = lax.axis_index("store")
    y, core = lax.div(dp, 2), lax.rem(dp, 2)
    z, x = lax.div(store, 2), lax.rem(store, 2)
    inner = (z == 1) | (z == 2)
    beside = z + 1 - 2 * lax.rem(z, 2)
    along = lambda to: (dp, to * 2 + x)
    peers = {
        "x": (dp, z * 2 + (1 - x)),
        "y": ((1 - y) * 2 + core, store),
        "core": (y * 2 + (1 - core), store),
        "beside": along(beside),
        "end_z": 3 * lax.div(z, 2),
        "other_inner": along(3 - z),
        "far_end": along(3 - 3 * lax.div(z, 2)),
    }
    place = (x, y, z, core, inner, peers)

    barrier = pltpu.get_barrier_semaphore()
    for peer in (peers["x"], peers["y"], peers["core"]) + tuple(along(lax.rem(z + hop, 4)) for hop in (1, 2, 3)):
        pl.semaphore_signal(barrier, inc=1, device_id=peer, device_id_type=MESH_ID)
    pl.semaphore_wait(barrier, 6)

    units = [
        Unit(
            place, lambda kind, q=q: signals.at[kind, q], [ref.at[q] for ref in rows],
            lambda c, h, q=q: out_ref.at[c, h, :, q],
        )
        for q in range(chunks)
    ]
    extra = Unit(
        place, lambda kind: signals.at[kind, chunks], weights, lambda c, h: weight_out.at[c, h]
    )
    extra_first = extra.firsts(weight_ref.at[:, 1 - x, :, 0], weight_ref.at[:, :, 1 - y, 1])
    extra_loads = extra.loads((weight_ref.at[:, x, :, 0], weight_ref.at[:, :, y, 1]))
    loads = [
        unit.loads((keep_ref.at[0, :, :, q], keep_ref.at[1, :, :, q], came_a.at[:, :, q], came_b.at[:, :, q]))
        for q, unit in enumerate(units)
    ]
    for copy in loads[0] + extra_first + extra_loads:
        copy.start()
    for some in loads[1:]:
        for copy in some:
            copy.start()
    for step in range(chunks + 4):
        if step < chunks:
            for copy in loads[step]:
                copy.wait()
            units[step].merge_first()
        if step == 4:
            for copy in extra_loads:
                copy.wait()
            for copy in extra_first:
                copy.wait_recv()
            extra.merge_first()
        for stage, name in enumerate(("merge_second", "merge_third", "finish", "hand_on")):
            if 0 <= step - 1 - stage < chunks:
                getattr(units[step - 1 - stage], name)()
            if step == 6 + 2 * stage:
                getattr(extra, name)()
    for copy in extra_first:
        copy.wait_send()
    for unit in units + [extra]:
        unit.drain()


def reduce_rows(keep, came_a, came_b, weights, collective_id=0):
    rows = keep.shape[0] // 4
    chunks = rows // (4 * CHUNK)
    high = weights.shape[0] // 32

    def spare(high, *lead):
        return [
            pltpu.VMEM(lead + part + (high, D), jnp.bfloat16)
            for part in ((4, 2),) * 4 + ((4,), (4,), (4, 2), (3, 2), (2, 2), (2,), (2,), (2,))
        ]

    out, weights = pl.pallas_call(
        functools.partial(reduce_kernel, chunks),
        out_shape=[
            jax.ShapeDtypeStruct((2, 2, 2, chunks, CHUNK, D), jnp.bfloat16),
            jax.ShapeDtypeStruct((2, 2, 2, high, D), jnp.bfloat16),
        ],
        in_specs=[pl.BlockSpec(memory_space=pl.ANY)] * 4,
        out_specs=[pl.BlockSpec(memory_space=pl.ANY)] * 2,
        scratch_shapes=spare(CHUNK, chunks) + spare(high) + [pltpu.SemaphoreType.DMA((SIGNALS, chunks + 1))],
        compiler_params=pltpu.CompilerParams(
            collective_id=collective_id, has_side_effects=True, vmem_limit_bytes=VMEM_LIMIT
        ),
        cost_estimate=pl.CostEstimate(flops=0, transcendentals=0, bytes_accessed=450_000_000),
        name="reduce_rows",
    )(
        keep.reshape(2, 4, 2, chunks, CHUNK, D),
        came_a.reshape(4, 2, chunks, CHUNK, D),
        came_b.reshape(4, 2, chunks, CHUNK, D),
        weights.reshape(4, 2, 2, 2, high, D),
    )
    return out.reshape(2 * rows, D), weights.reshape(8 * high, D)


PAIRS = ((0, 1), (1, 0), (2, 3), (3, 2))


def own_rows(flat, rows_here):
    half = rows_here // 2
    quarter = half // 4
    dp = lax.axis_index("dp")
    here_y, core = dp // 2, dp % 2
    here_x = lax.axis_index("store") % 2
    owner, local = flat // rows_here, flat % rows_here
    z, x = owner // 2, owner % 2
    y = (local % half) // (2 * quarter)
    second = (local // quarter) % 2
    stays = jnp.where(second == 0, x == here_x, y == here_y)
    pair = jnp.where(second == 0, y, x)
    rows = 8 * half
    target = (2 * stays + second) * (rows // 4) + (2 * z + pair) * quarter + local % quarter
    return jnp.where(local // half == core, target, rows)


def plan_store(indices, rows_here):
    flat = indices.reshape(-1)
    other = lax.ppermute(flat, "dp", PAIRS)
    where = jnp.concatenate([own_rows(flat, rows_here), own_rows(other, rows_here)])
    return scatter_plan(where, lax.axis_size("store") * rows_here // 2)


def add_store(plan, own, other, rows_here):
    return scatter_rows(plan, own, other, lax.axis_size("store") * rows_here // 2)


def swap_store(send_a, send_b):
    owners = lax.axis_size("store")
    came_a = lax.ppermute(send_a, "store", [(i, i ^ 1) for i in range(owners)])
    came_b = lax.ppermute(send_b, "dp", [(i, i ^ 2) for i in range(4)])
    return came_a, came_b


def by_owner(matrix):
    owners = lax.axis_size("store")
    return matrix.astype(jnp.bfloat16).reshape(owners, -1, D)


def reduce_packed(packed):
    return lax.psum_scatter(packed.reshape(-1, D), ("store", "dp"), scatter_dimension=0, tiled=True)


def all_copies(share):
    return lax.all_gather(share, "dp", axis=0, tiled=True).astype(jnp.float32)


def pack_early(inner, outer, squares):
    blocks = [inner[:, block * D : (block + 1) * D] for block in range(inner.shape[1] // D)]
    return jnp.concatenate([by_owner(piece) for piece in blocks + [outer] + list(squares)], axis=1)


def unpack_early(total, wide):
    part = D // lax.axis_size("store")
    inner_total = jnp.transpose(total[: wide * part].reshape(wide, part, D), (1, 0, 2))
    rest = total[wide * part :]
    return (
        inner_total.reshape(part, wide * D),
        rest[: wide * part],
        rest[wide * part :].reshape(-1, part, D),
    )


def pack_late(squares, features, inner_bias):
    owners = lax.axis_size("store")
    part = D // owners
    wide = inner_bias.shape[0] // D
    small = jnp.concatenate(
        [feature.astype(jnp.bfloat16).reshape(owners, part) for feature in features]
        + [inner_bias.astype(jnp.bfloat16).reshape(owners, wide * part)],
        axis=1,
    )
    small = jnp.pad(small, ((0, 0), (0, part * D - small.shape[1]))).reshape(owners, part, D)
    return jnp.concatenate([by_owner(square) for square in squares] + [small], axis=1)


def add_cores(packed):
    core = lax.axis_index("dp") % 2
    halves = packed.reshape(packed.shape[0], 2, -1, D)
    mine = lax.dynamic_index_in_dim(halves, core, axis=1, keepdims=False)
    other = lax.dynamic_index_in_dim(halves, 1 - core, axis=1, keepdims=False)
    other = lax.ppermute(other, "dp", PAIRS)
    return plus(mine, other).reshape(-1, D)


def unpack_late(total, count, features, wide):
    part = D // lax.axis_size("store")
    tail = total[count * part :].reshape(-1)
    table = tail[: features * part].reshape(features, part)
    return (
        total[: count * part].reshape(count, part, D),
        table,
        tail[features * part :][: wide * part],
    )


def cross_probs_of(folded, rows):
    scores = lax.dot_general(folded, rows, (((1,), (1,)), ((), ())), preferred_element_type=jnp.float32)
    token = lax.broadcasted_iota(jnp.int32, scores.shape, 0) % CROSS_TOKENS
    owner = lax.broadcasted_iota(jnp.int32, scores.shape, 1) // K
    scores = jnp.where(token == owner, scores, -1e30)
    raised = jnp.exp(scores - jnp.max(scores, axis=1, keepdims=True))
    return raised * (1.0 / jnp.sum(raised, axis=1, keepdims=True))


def cross_tiles(ref):
    tokens = ref.shape[1]
    for first in range(0, tokens, CROSS_TOKENS):
        yield pl.ds(first, CROSS_TOKENS), pl.ds(first * K, CROSS_TOKENS * K)


def cross_forward_kernel(folded_ref, first_ref, second_ref, which_ref, rows_ref, summary_ref):
    for some, slots in cross_tiles(folded_ref):
        which = which_ref[slots, :] != 0
        rows = jnp.where(
            which, second_ref[slots, :].astype(jnp.float32), first_ref[slots, :].astype(jnp.float32)
        ).astype(jnp.bfloat16)
        rows_ref[slots, :] = rows
        probs = cross_probs_of(folded_ref[:, some, :].reshape(H * CROSS_TOKENS, D), rows)
        summary = jnp.dot(probs.astype(jnp.bfloat16), rows, preferred_element_type=jnp.float32)
        summary_ref[:, some, :] = summary.astype(jnp.bfloat16).reshape(H, CROSS_TOKENS, D)


def cross_backward_kernel(folded_ref, grad_ref, rows_ref, row_grad_ref, folded_grad_ref):
    for some, slots in cross_tiles(folded_ref):
        rows = rows_ref[slots, :]
        folded = folded_ref[:, some, :].reshape(H * CROSS_TOKENS, D)
        grad = grad_ref[:, some, :].reshape(H * CROSS_TOKENS, D)
        probs = cross_probs_of(folded, rows)
        prob_grad = lax.dot_general(
            grad, rows, (((1,), (1,)), ((), ())), preferred_element_type=jnp.float32
        )
        total = jnp.sum(probs * prob_grad, axis=1, keepdims=True)
        score_low = (probs * (prob_grad - total)).astype(jnp.bfloat16)
        turned = (((0,), (0,)), ((), ()))
        row_grad = lax.dot_general(
            probs.astype(jnp.bfloat16), grad, turned, preferred_element_type=jnp.float32
        )
        row_grad += lax.dot_general(score_low, folded, turned, preferred_element_type=jnp.float32)
        row_grad_ref[slots, :] = row_grad.astype(jnp.bfloat16)
        folded_grad = jnp.dot(score_low, rows, preferred_element_type=jnp.float32)
        folded_grad_ref[:, some, :] = folded_grad.astype(jnp.bfloat16).reshape(H, CROSS_TOKENS, D)


CROSS_TOKENS = 16
CROSS_STEP = 64


def cross_specs():
    heads = pl.BlockSpec((H, CROSS_STEP, D), lambda i: (0, i, 0))
    rows = pl.BlockSpec((CROSS_STEP * K, D), lambda i: (i, 0))
    return heads, rows


def cross_forward(folded, first, second, which):
    heads, rows = cross_specs()
    tokens = folded.shape[1]
    return pl.pallas_call(
        cross_forward_kernel,
        out_shape=[
            jax.ShapeDtypeStruct((tokens * K, D), jnp.bfloat16),
            jax.ShapeDtypeStruct((H, tokens, D), jnp.bfloat16),
        ],
        grid=(tokens // CROSS_STEP,),
        in_specs=[heads, rows, rows, pl.BlockSpec((CROSS_STEP * K, 1), lambda i: (i, 0))],
        out_specs=[rows, heads],
        cost_estimate=pl.CostEstimate(flops=0, transcendentals=0, bytes_accessed=65_000_000),
        name="cross_forward",
    )(folded, first, second, which)


def cross_backward(folded, grad, fetched):
    heads, rows = cross_specs()
    tokens = folded.shape[1]
    return pl.pallas_call(
        cross_backward_kernel,
        out_shape=[
            jax.ShapeDtypeStruct((tokens * K, D), jnp.bfloat16),
            jax.ShapeDtypeStruct((H, tokens, D), jnp.bfloat16),
        ],
        grid=(tokens // CROSS_STEP,),
        in_specs=[heads, heads, rows],
        out_specs=[rows, heads],
        cost_estimate=pl.CostEstimate(flops=0, transcendentals=0, bytes_accessed=100_000_000),
        name="cross_backward",
    )(folded, grad, fetched)


def body(
    tokens,
    datastore,
    indices,
    lengths,
    proj_weight,
    out_weight,
    proj_bias,
    norm_gain,
    norm_bias,
    inner_weight,
    inner_bias,
    outer_weight,
    outer_bias,
    cotangent,
):
    seq_len = tokens.shape[0]
    score_scale = HD ** (-0.5)
    owners = lax.axis_size("store")
    rows_here = datastore.shape[0]
    capacity = 2 * seq_len * K // owners
    position = jnp.arange(seq_len)
    length = lengths[0]
    allowed = (position[None, :] <= position[:, None]) & (position[None, :] < length)
    valid = (position < length)[:, None]
    dense = is_dense(owners, rows_here)
    if dense:
        plan = plan_store(indices, rows_here)
        found_first, found_second, which_half, plan = fetch_dense(datastore, indices, plan)
    else:
        target, request = route_slots(indices, rows_here, owners, capacity)
        returned, _ = fetch_rows(request, datastore)
        fetched = returned.reshape(owners * capacity, D)[target].reshape(seq_len, K, D)
    self_bias = jnp.concatenate([proj_bias[:, 0], jnp.zeros((D,), jnp.float32), proj_bias[:, 1]])
    self_proj = proj_weight[:, 0:3, :].reshape(D, 3 * D)
    joined = (product(tokens, self_proj) + self_bias).astype(jnp.bfloat16)
    queries = joined[:, :D].reshape(seq_len, H, HD)
    self_keys = joined[:, D : 2 * D].reshape(seq_len, H, HD)
    values = joined[:, 2 * D :].reshape(seq_len, H, HD)
    scores = self_scores(queries, self_keys, allowed, score_scale)
    self_lse = log_total(scores)
    self_probs = jnp.exp(scores - self_lse).astype(jnp.bfloat16)
    self_mixed = (
        jnp.einsum("hqk,khe->qhe", self_probs, values, preferred_element_type=jnp.float32)
        .reshape(seq_len, D)
        .astype(jnp.bfloat16)
    )
    first_pre = tokens.astype(jnp.float32) + (
        product(self_mixed, out_weight[:, 0, :]) + proj_bias[:, 2]
    )
    first_out, first_normed, first_inverse = norm_forward(
        first_pre, norm_gain[:, 0], norm_bias[:, 0]
    )
    first_low = first_out.astype(jnp.bfloat16)
    cross_query = (
        (product(first_low, proj_weight[:, 3, :]) + proj_bias[:, 3])
        .astype(jnp.bfloat16)
        .reshape(seq_len, H, HD)
    )
    key_heads = proj_weight[:, 4, :].reshape(D, H, HD)
    folded = (
        jnp.einsum("the,dhe->thd", cross_query, key_heads, preferred_element_type=jnp.float32)
        * score_scale
    ).astype(jnp.bfloat16)
    if dense:
        folded_heads = jnp.transpose(folded, (1, 0, 2))
        fetched, summary = cross_forward(folded_heads, found_first, found_second, which_half)
        summary = jnp.transpose(summary, (1, 0, 2))
    else:
        cross_scores = jnp.einsum("thd,tkd->thk", folded, fetched, preferred_element_type=jnp.float32)
        cross_lse = log_total(cross_scores)
        cross_full = jnp.exp(cross_scores - cross_lse)
        cross_probs = cross_full.astype(jnp.bfloat16)
        summary = jnp.einsum(
            "thk,tkd->thd", cross_probs, fetched, preferred_element_type=jnp.float32
        ).astype(jnp.bfloat16)
    value_heads = proj_weight[:, 5, :].reshape(D, H, HD)
    cross_mixed = (
        jnp.einsum(
            "thd,dhe->the", summary, value_heads, preferred_element_type=jnp.float32
        ).reshape(seq_len, D)
        + proj_bias[:, 4]
    ).astype(jnp.bfloat16)
    second_pre = first_out + (product(cross_mixed, out_weight[:, 1, :]) + proj_bias[:, 5])
    second_out, second_normed, second_inverse = norm_forward(
        second_pre, norm_gain[:, 1], norm_bias[:, 1]
    )
    second_low = second_out.astype(jnp.bfloat16)
    inner_pre = product(second_low, inner_weight) + inner_bias
    activated = jax.nn.gelu(inner_pre, approximate=False).astype(jnp.bfloat16)
    third_pre = second_out + (product(activated, outer_weight) + outer_bias)
    third_out, third_normed, third_inverse = norm_forward(
        third_pre, norm_gain[:, 2], norm_bias[:, 2]
    )
    output = jnp.where(valid, third_out, 0.0).astype(jnp.bfloat16)
    upstream = jnp.where(valid, cotangent.astype(jnp.float32), 0.0)
    third_grad, gain_three, shift_three = norm_backward(
        upstream, third_normed, third_inverse, norm_gain[:, 2]
    )
    outer_low = third_grad.astype(jnp.bfloat16)
    grad_outer_weight = contract_rows(activated, outer_low)
    grad_outer_bias = column_sum(outer_low)
    act_grad = product_back(outer_low, outer_weight)
    slope = jax.vjp(lambda activation_in: jax.nn.gelu(activation_in, approximate=False), inner_pre)[
        1
    ](act_grad)[0]
    inner_low = slope.astype(jnp.bfloat16)
    grad_inner_weight = contract_rows(second_low, inner_low)
    grad_inner_bias = column_sum(inner_low)
    second_up = third_grad + product_back(inner_low, inner_weight)
    second_grad, gain_two, shift_two = norm_backward(
        second_up, second_normed, second_inverse, norm_gain[:, 1]
    )
    cross_out_low = second_grad.astype(jnp.bfloat16)
    grad_cross_out = contract_rows(cross_mixed, cross_out_low)
    bias_five = column_sum(cross_out_low)
    mixed_low = product_back(cross_out_low, out_weight[:, 1, :]).astype(jnp.bfloat16)
    bias_four = column_sum(mixed_low)
    mixed_heads = mixed_low.reshape(seq_len, H, HD)
    grad_value_heads = jnp.einsum(
        "thd,the->dhe", summary, mixed_heads, preferred_element_type=jnp.float32
    )
    if dense:
        packed_early = pack_early(grad_inner_weight, grad_outer_weight, (grad_cross_out,))
        mixed_heads, packed_early = lax.optimization_barrier((mixed_heads, packed_early))
        share_early = reduce_packed(packed_early)
    summary_low = jnp.einsum(
        "the,dhe->thd", mixed_heads, value_heads, preferred_element_type=jnp.float32
    ).astype(jnp.bfloat16)
    if dense:
        own_grad, folded_low = cross_backward(
            folded_heads, jnp.transpose(summary_low, (1, 0, 2)), fetched
        )
        folded_low = jnp.transpose(folded_low, (1, 0, 2))
        other_grad = lax.ppermute(own_grad, "dp", PAIRS)
    else:
        returned_again, asked_back = fetch_again(request, datastore)
        fetched_back = returned_again.reshape(owners * capacity, D)[target].reshape(seq_len, K, D)
        prob_grad = jnp.einsum(
            "thd,tkd->thk", summary_low, fetched_back, preferred_element_type=jnp.float32
        )
        score_low = (
            cross_full * (prob_grad - jnp.sum(cross_full * prob_grad, axis=-1, keepdims=True))
        ).astype(jnp.bfloat16)
        row_grad = (
            jnp.einsum("thk,thd->tkd", cross_probs, summary_low, preferred_element_type=jnp.float32)
            + jnp.einsum("thk,thd->tkd", score_low, folded, preferred_element_type=jnp.float32)
        ).astype(jnp.bfloat16)
        folded_low = jnp.einsum(
            "thk,tkd->thd", score_low, fetched_back, preferred_element_type=jnp.float32
        ).astype(jnp.bfloat16)
    grad_key_heads = (
        jnp.einsum("thd,the->dhe", folded_low, cross_query, preferred_element_type=jnp.float32)
        * score_scale
    )
    query_low = (
        (
            jnp.einsum("thd,dhe->the", folded_low, key_heads, preferred_element_type=jnp.float32)
            * score_scale
        )
        .astype(jnp.bfloat16)
        .reshape(seq_len, D)
    )
    if dense:
        query_low, other_grad = lax.optimization_barrier((query_low, other_grad))
        send_a, send_b, keep = add_store(plan, own_grad, other_grad, rows_here)
        query_low, mixed_heads, send_a, send_b, keep = lax.optimization_barrier(
            (query_low, mixed_heads, send_a, send_b, keep)
        )
        grad_value_heads = jnp.einsum(
            "thd,the->dhe", summary, mixed_heads, preferred_element_type=jnp.float32
        )
        came_a, came_b = swap_store(send_a, send_b)
    bias_three = column_sum(query_low)
    grad_cross_query = contract_rows(first_low, query_low)
    if not dense:
        grad_buffer = (
            jnp.zeros((owners * capacity, D), jnp.bfloat16)
            .at[target]
            .set(row_grad.reshape(-1, D))
            .reshape(owners, capacity, D)
        )
        arrived = lax.all_to_all(grad_buffer, "store", split_axis=0, concat_axis=0, tiled=True)
        partial_store = (
            jnp.zeros((rows_here, D), jnp.float32)
            .at[asked_back.reshape(-1)]
            .add(arrived.reshape(-1, D).astype(jnp.float32))
        )
        grad_store = lax.psum(partial_store.astype(jnp.bfloat16), "dp").astype(jnp.float32)
    first_up = second_grad + product_back(query_low, proj_weight[:, 3, :])
    first_grad, gain_one, shift_one = norm_backward(
        first_up, first_normed, first_inverse, norm_gain[:, 0]
    )
    self_out_low = first_grad.astype(jnp.bfloat16)
    grad_self_out = contract_rows(self_mixed, self_out_low)
    bias_two = column_sum(self_out_low)
    self_mixed_low = (
        product_back(self_out_low, out_weight[:, 0, :]).astype(jnp.bfloat16).reshape(seq_len, H, HD)
    )
    value_grad = jnp.einsum(
        "hqk,qhe->khe", self_probs, self_mixed_low, preferred_element_type=jnp.float32
    )
    attend_grad = jnp.einsum(
        "qhe,khe->hqk", self_mixed_low, values, preferred_element_type=jnp.float32
    )
    self_full = jnp.exp(self_scores(queries, self_keys, allowed, score_scale) - self_lse)
    self_score_low = (
        self_full * (attend_grad - jnp.sum(self_full * attend_grad, axis=-1, keepdims=True))
    ).astype(jnp.bfloat16)
    query_grad = (
        jnp.einsum("hqk,khe->qhe", self_score_low, self_keys, preferred_element_type=jnp.float32)
        * score_scale
    )
    key_grad = (
        jnp.einsum("hqk,qhe->khe", self_score_low, queries, preferred_element_type=jnp.float32)
        * score_scale
    )
    joined_low = jnp.concatenate(
        [
            query_grad.reshape(seq_len, D),
            key_grad.reshape(seq_len, D),
            value_grad.reshape(seq_len, D),
        ],
        axis=1,
    ).astype(jnp.bfloat16)
    grad_self_proj = contract_rows(tokens, joined_low).reshape(D, 3, D)
    bias_zero = column_sum(joined_low[:, :D])
    bias_one = column_sum(joined_low[:, 2 * D :])
    grad_tokens = (first_grad + product_back(joined_low, self_proj)).astype(jnp.bfloat16)
    if dense:
        packed_late = pack_late(
            (
                grad_self_proj[:, 0],
                grad_self_proj[:, 1],
                grad_self_proj[:, 2],
                grad_cross_query,
                grad_key_heads.reshape(D, D),
                grad_value_heads.reshape(D, D),
                grad_self_out,
            ),
            (bias_zero, bias_one, bias_two, bias_three, bias_four, bias_five)
            + (gain_one, gain_two, gain_three)
            + (shift_one, shift_two, shift_three)
            + (grad_outer_bias,),
            grad_inner_bias,
        )
        wide = grad_inner_bias.shape[0] // D
        early_totals = unpack_early(all_copies(share_early), wide)
        keep, came_a, came_b, output, grad_tokens, early_totals = lax.optimization_barrier(
            (keep, came_a, came_b, output, grad_tokens, early_totals)
        )
        inner_total, outer_total, early = early_totals
        grad_store, total_late = reduce_rows(keep, came_a, came_b, add_cores(packed_late))
        grad_store = grad_store.astype(jnp.float32)
        late, table, bias_inner = unpack_late(total_late.astype(jnp.float32), 7, 13, wide)
        return (
            output,
            grad_tokens,
            grad_store,
            jnp.stack([late[0], late[1], late[2], late[3], late[4], late[5]], axis=1),
            jnp.stack([late[6], early[0]], axis=1),
            jnp.transpose(table[0:6]),
            jnp.transpose(table[6:9]),
            jnp.transpose(table[9:12]),
            inner_total,
            bias_inner,
            outer_total,
            table[12],
        )
    grad_proj = jnp.stack(
        [
            grad_self_proj[:, 0],
            grad_self_proj[:, 1],
            grad_self_proj[:, 2],
            grad_cross_query,
            grad_key_heads.reshape(D, D),
            grad_value_heads.reshape(D, D),
        ],
        axis=1,
    )
    grad_out = jnp.stack([grad_self_out, grad_cross_out], axis=1)
    grad_bias = jnp.stack([bias_zero, bias_one, bias_two, bias_three, bias_four, bias_five], axis=1)
    grad_gain = jnp.stack([gain_one, gain_two, gain_three], axis=1)
    grad_shift = jnp.stack([shift_one, shift_two, shift_three], axis=1)
    shares = (
        lax.psum_scatter(
            grad_proj.astype(jnp.bfloat16), "store", scatter_dimension=0, tiled=True
        ).astype(jnp.float32),
        lax.psum_scatter(
            grad_out.astype(jnp.bfloat16), "store", scatter_dimension=0, tiled=True
        ).astype(jnp.float32),
        lax.psum_scatter(
            grad_bias.astype(jnp.bfloat16), "store", scatter_dimension=0, tiled=True
        ).astype(jnp.float32),
        lax.psum_scatter(
            grad_gain.astype(jnp.bfloat16), "store", scatter_dimension=0, tiled=True
        ).astype(jnp.float32),
        lax.psum_scatter(
            grad_shift.astype(jnp.bfloat16), "store", scatter_dimension=0, tiled=True
        ).astype(jnp.float32),
        lax.psum_scatter(
            grad_inner_weight.astype(jnp.bfloat16), "store", scatter_dimension=0, tiled=True
        ).astype(jnp.float32),
        lax.psum_scatter(
            grad_inner_bias.astype(jnp.bfloat16), "store", scatter_dimension=0, tiled=True
        ).astype(jnp.float32),
        lax.psum_scatter(
            grad_outer_weight.astype(jnp.bfloat16), "store", scatter_dimension=0, tiled=True
        ).astype(jnp.float32),
        lax.psum_scatter(
            grad_outer_bias.astype(jnp.bfloat16), "store", scatter_dimension=0, tiled=True
        ).astype(jnp.float32),
    )
    totals = (
        lax.psum(shares[0].astype(jnp.bfloat16), "dp").astype(jnp.float32),
        lax.psum(shares[1].astype(jnp.bfloat16), "dp").astype(jnp.float32),
        lax.psum(shares[2].astype(jnp.bfloat16), "dp").astype(jnp.float32),
        lax.psum(shares[3].astype(jnp.bfloat16), "dp").astype(jnp.float32),
        lax.psum(shares[4].astype(jnp.bfloat16), "dp").astype(jnp.float32),
        lax.psum(shares[5].astype(jnp.bfloat16), "dp").astype(jnp.float32),
        lax.psum(shares[6].astype(jnp.bfloat16), "dp").astype(jnp.float32),
        lax.psum(shares[7].astype(jnp.bfloat16), "dp").astype(jnp.float32),
        lax.psum(shares[8].astype(jnp.bfloat16), "dp").astype(jnp.float32),
    )
    return (
        output,
        grad_tokens,
        grad_store,
        totals[0],
        totals[1],
        totals[2],
        totals[3],
        totals[4],
        totals[5],
        totals[6],
        totals[7],
        totals[8],
    )


def solution(mesh):
    in_specs = (
        P(("dp", "store"), None),
        P("store", None),
        P(("dp", "store"), None),
        P(("dp", "store")),
        P(),
        P(),
        P(),
        P(),
        P(),
        P(),
        P(),
        P(),
        P(),
        P(("dp", "store"), None),
    )
    out_specs = (
        P(("dp", "store"), None),
        P(("dp", "store"), None),
        P("store", None),
        P("store", None, None),
        P("store", None, None),
        P("store", None),
        P("store", None),
        P("store", None),
        P("store", None),
        P("store"),
        P("store", None),
        P("store"),
    )

    return jax.shard_map(body, mesh=mesh, in_specs=in_specs, out_specs=out_specs, check_vma=False)
```

```python
import functools

import jax
import jax.numpy as jnp
from jax import lax
from jax.experimental import pallas as pl
from jax.experimental.pallas import tpu as pltpu
from jax.sharding import PartitionSpec as P


D = 768
H = 12
HD = 64
K = 16


EPSILON = 1e-05


def product(matrix, factor):
    return jnp.dot(matrix, factor, preferred_element_type=jnp.float32)


def product_back(matrix, weight):
    return jnp.einsum("tf,df->td", matrix, weight, preferred_element_type=jnp.float32)


def contract_rows(matrix, factor):
    return jnp.einsum("td,tf->df", matrix, factor, preferred_element_type=jnp.float32)


def column_sum(matrix):
    return jnp.sum(matrix.astype(jnp.float32), axis=0)


def norm_forward(hidden, norm_weight, norm_shift):
    centered = hidden - jnp.mean(hidden, axis=-1, keepdims=True)
    inverse = lax.rsqrt(jnp.mean(centered * centered, axis=-1, keepdims=True) + EPSILON)
    normed = centered * inverse
    return (normed * norm_weight + norm_shift, normed, inverse)


def norm_backward(upstream, normed, inverse, norm_weight):
    scaled = upstream * norm_weight
    plain_mean = jnp.mean(scaled, axis=-1, keepdims=True)
    normed_mean = jnp.mean(scaled * normed, axis=-1, keepdims=True)
    return (
        inverse * (scaled - plain_mean - normed * normed_mean),
        jnp.sum(upstream * normed, axis=0),
        jnp.sum(upstream, axis=0),
    )


def log_total(scores):
    highest = jnp.max(scores, axis=-1, keepdims=True)
    return highest + jnp.log(jnp.sum(jnp.exp(scores - highest), axis=-1, keepdims=True))


def route_slots(picked, rows_here, owners, capacity):
    flat_ids = picked.reshape(-1)
    owner_of = flat_ids // rows_here
    local_row = flat_ids % rows_here
    by_owner = jnp.argsort(owner_of, stable=True)
    sorted_owner = owner_of[by_owner]
    owner_loads = jnp.sum(
        (owner_of[:, None] == jnp.arange(owners, dtype=jnp.int32)[None, :]).astype(jnp.int32),
        axis=0,
    )
    starts = jnp.cumsum(owner_loads) - owner_loads
    within = jnp.arange(flat_ids.shape[0], dtype=jnp.int32) - starts[sorted_owner]
    placed = jnp.zeros_like(flat_ids).at[by_owner].set(within)
    target = owner_of * capacity + placed
    request = jnp.zeros((owners * capacity,), jnp.int32).at[target].set(local_row)
    return (target, request.reshape(owners, capacity))


def fetch_rows(request, datastore):
    asked_rows = lax.all_to_all(request, "store", split_axis=0, concat_axis=0, tiled=True)
    found_rows = datastore[asked_rows.reshape(-1)].reshape(asked_rows.shape + (datastore.shape[1],))
    return (
        lax.all_to_all(found_rows, "store", split_axis=0, concat_axis=0, tiled=True),
        asked_rows,
    )


def fetch_again(request, datastore):
    asked_rows = lax.all_to_all(request, "store", split_axis=0, concat_axis=0, tiled=True)
    found_rows = datastore[asked_rows.reshape(-1)].reshape(asked_rows.shape + (datastore.shape[1],))
    return (
        lax.all_to_all(found_rows, "store", split_axis=0, concat_axis=0, tiled=True),
        asked_rows,
    )


def self_scores(queries, self_keys, allowed, score_scale):
    scores = (
        jnp.einsum("qhe,khe->hqk", queries, self_keys, preferred_element_type=jnp.float32)
        * score_scale
    )
    return jnp.where(allowed[None], scores, -1e30)


DENSE_LIMIT = 1 << 16


def is_dense(owners, rows_here):
    fits = owners * rows_here <= DENSE_LIMIT and rows_here % (8 * CHUNK) == 0 and owners * rows_here % GATHER_BLOCK == 0
    return fits and owners == 8 and lax.axis_size("dp") == 4


def fetch_dense(datastore, indices, plan):
    copies = lax.axis_size("dp")
    rows_here = datastore.shape[0]
    share = rows_here // copies
    mine = lax.dynamic_slice_in_dim(datastore, lax.axis_index("dp") * share, share, axis=0)
    table = lax.all_gather(mine, ("store", "dp"), axis=0, tiled=True)
    picks = gather_plan(indices, table.shape[0])
    picks, plan = lax.optimization_barrier((picks, plan))
    return gather_rows(picks, table, indices.size), plan


MESH_ID = pl.DeviceIdType.MESH
VMEM_LIMIT = 67043328
CHUNK = 64


GROUP = 8


SPLIT = D // 128


def widen(ref, wide):
    def strip(i, carry):
        first = pl.multiple_of(i * 32, 32)
        value = ref[pl.ds(first, 32), :].astype(jnp.float32)
        for part in range(SPLIT):
            wide[pl.ds(first * SPLIT + part, 32, stride=SPLIT), :] = value[:, part * 128 : (part + 1) * 128]
        return carry

    lax.fori_loop(0, ref.shape[0] // 32, strip, 0, unroll=4)


def narrow(total, start, out_ref):
    def strip(i, carry):
        first = pl.multiple_of(start * SPLIT + i * (32 * SPLIT), 32 * SPLIT)
        for part in range(SPLIT):
            value = total[pl.ds(first + part, 32, stride=SPLIT), :]
            out_ref[pl.ds(pl.multiple_of(i * 32, 32), 32), part * 128 : (part + 1) * 128] = value.astype(jnp.bfloat16)
        return carry

    lax.fori_loop(0, out_ref.shape[0] // 32, strip, 0, unroll=4)


GATHER_BLOCK = 2048


def gather_kernel(blocks, out_rows, row_ref, to_ref, start_ref, table_ref, out_ref, wide, found):
    step = pl.program_id(0)

    @pl.when(step < blocks)
    def _():
        widen(table_ref, wide)
        base = step * (GATHER_BLOCK * SPLIT)
        first = start_ref[step]

        def group(i, carry):
            at = first + i * GROUP
            rows = [
                jnp.minimum(row_ref[at + k] - base, (GATHER_BLOCK - 1) * SPLIT) for k in range(GROUP)
            ]
            places = [to_ref[at + k] for k in range(GROUP)]
            values = [wide[pl.ds(row, SPLIT), :] for row in rows]
            for place, value in zip(places, values):
                found[pl.ds(place, SPLIT), :] = value
            return carry

        lax.fori_loop(0, lax.div(start_ref[step + 1] - first + GROUP - 1, GROUP), group, 0)

    @pl.when(step >= blocks)
    def _():
        narrow(found, (step - blocks) * out_rows, out_ref)


def gather_plan(indices, rows):
    flat = indices.reshape(-1)
    count = flat.shape[0]
    row, place = lax.sort((flat, jnp.arange(count, dtype=jnp.int32)), dimension=0, num_keys=1)
    bounds = jnp.arange(rows // GATHER_BLOCK + 1, dtype=jnp.int32) * GATHER_BLOCK
    starts = jnp.sum((flat[:, None] < bounds[None, :]).astype(jnp.int32), axis=0)
    row = jnp.concatenate([row, jnp.full((GROUP,), rows - 1, jnp.int32)])
    place = jnp.concatenate([place, jnp.full((GROUP,), count, jnp.int32)])
    return SPLIT * row, SPLIT * place, starts


def gather_rows(plan, table, count, out_rows=1024):
    blocks = table.shape[0] // GATHER_BLOCK
    return pl.pallas_call(
        functools.partial(gather_kernel, blocks, out_rows),
        out_shape=jax.ShapeDtypeStruct((count, D), jnp.bfloat16),
        grid_spec=pltpu.PrefetchScalarGridSpec(
            num_scalar_prefetch=3,
            grid=(blocks + count // out_rows,),
            in_specs=[pl.BlockSpec((GATHER_BLOCK, D), lambda i, *_: (jnp.minimum(i, blocks - 1), 0))],
            out_specs=pl.BlockSpec((out_rows, D), lambda i, *_: (jnp.maximum(i - blocks, 0), 0)),
            scratch_shapes=[
                pltpu.VMEM((GATHER_BLOCK * SPLIT, 128), jnp.float32),
                pltpu.VMEM(((count + 8) * SPLIT, 128), jnp.float32),
            ],
        ),
        compiler_params=pltpu.CompilerParams(vmem_limit_bytes=VMEM_LIMIT),
        cost_estimate=pl.CostEstimate(flops=0, transcendentals=0, bytes_accessed=160_000_000),
        name="gather_rows",
    )(*plan, table)


def scatter_kernel(steps, block, out_rows, row_ref, from_ref, twice_ref, groups_ref, own_ref, other_ref, *rest):
    outs, (total, wide) = rest[:-2], rest[-2:]
    step = pl.program_id(0)

    @pl.when(step == 0)
    def _():
        def clear(i, carry):
            total[pl.ds(i * 192, 192), :] = jnp.zeros((192, 128), jnp.float32)
            return carry

        lax.fori_loop(0, total.shape[0] // 192, clear, 0, unroll=4)

    @pl.when(step < steps // 2)
    def _():
        widen(own_ref, wide)

    @pl.when((step >= steps // 2) & (step < steps))
    def _():
        widen(other_ref, wide)

    @pl.when(step < steps)
    def _():
        def group(i, carry):
            first = step * block + i * GROUP
            rows = [row_ref[first + k] for k in range(GROUP)]
            came = [from_ref[first + k] for k in range(GROUP)]
            twice = twice_ref[step * (block // GROUP) + i]

            @pl.when(twice == 0)
            def _():
                sums = [total[pl.ds(rows[k], SPLIT), :] + wide[pl.ds(came[k], SPLIT), :] for k in range(GROUP)]
                for k in range(GROUP):
                    total[pl.ds(rows[k], SPLIT), :] = sums[k]

            @pl.when(twice != 0)
            def _():
                for k in range(GROUP):
                    total[pl.ds(rows[k], SPLIT), :] = total[pl.ds(rows[k], SPLIT), :] + wide[pl.ds(came[k], SPLIT), :]

            return carry

        lax.fori_loop(0, groups_ref[step], group, 0)

    quarter = (total.shape[0] // SPLIT // 4) // out_rows
    for index, out_ref in enumerate(outs):
        last = quarter * (index + 1 if index < 2 else 4)

        @pl.when((step >= steps + quarter * index) & (step < steps + last))
        def _(out_ref=out_ref):
            narrow(total, (step - steps) * out_rows, out_ref)


SCATTER_BLOCK = 1024


def scatter_plan(where, rows):
    keys = jnp.arange(where.shape[0], dtype=jnp.int32).reshape(-1, SCATTER_BLOCK) % SCATTER_BLOCK
    where = where.reshape(-1, SCATTER_BLOCK)
    skipped = where >= rows
    keys, where = lax.sort((jnp.where(skipped, keys + SCATTER_BLOCK, keys), where), dimension=1, num_keys=1)
    count = jnp.sum((~skipped).astype(jnp.int32), axis=1)
    groups = (count + GROUP - 1) // GROUP
    where = jnp.where(keys >= SCATTER_BLOCK, rows + keys % GROUP, where)
    spare = lax.broadcasted_iota(jnp.int32, where.shape, 1) % GROUP
    where = jnp.where(keys >= SCATTER_BLOCK, rows + spare, where)
    eights = where.reshape(-1, GROUP)
    twice = jnp.zeros((eights.shape[0],), jnp.int32)
    for shift in range(1, GROUP):
        same = eights[:, shift:] == eights[:, :-shift]
        twice = twice | jnp.any(same, axis=1).astype(jnp.int32)
    return SPLIT * where.reshape(-1), SPLIT * (keys % SCATTER_BLOCK).reshape(-1), twice, groups


def scatter_rows(plan, own, other, rows, out_rows=512):
    block = SCATTER_BLOCK
    half = own.shape[0] // block
    steps = 2 * half
    quarter = rows // 4 // out_rows

    def part(first, count):
        return pl.BlockSpec((out_rows, D), lambda i, *_: (jnp.clip(i - steps - first, 0, count - 1), 0))

    return pl.pallas_call(
        functools.partial(scatter_kernel, steps, block, out_rows),
        out_shape=[
            jax.ShapeDtypeStruct((rows // 4, D), jnp.bfloat16),
            jax.ShapeDtypeStruct((rows // 4, D), jnp.bfloat16),
            jax.ShapeDtypeStruct((rows // 2, D), jnp.bfloat16),
        ],
        grid_spec=pltpu.PrefetchScalarGridSpec(
            num_scalar_prefetch=4,
            grid=(steps + rows // out_rows,),
            in_specs=[
                pl.BlockSpec((block, D), lambda i, *_: (jnp.minimum(i, half - 1), 0)),
                pl.BlockSpec((block, D), lambda i, *_: (jnp.clip(i - half, 0, half - 1), 0)),
            ],
            out_specs=[part(0, quarter), part(quarter, quarter), part(2 * quarter, 2 * quarter)],
            scratch_shapes=[
                pltpu.VMEM(((rows + 32) * SPLIT, 128), jnp.float32),
                pltpu.VMEM((block * SPLIT, 128), jnp.float32),
            ],
        ),
        compiler_params=pltpu.CompilerParams(vmem_limit_bytes=VMEM_LIMIT),
        cost_estimate=pl.CostEstimate(flops=0, transcendentals=0, bytes_accessed=220_000_000),
        name="scatter_rows",
    )(*plan, own, other)


SIGNALS = 26
LAG = 2


def plus(first, second):
    return (first.astype(jnp.float32) + second.astype(jnp.float32)).astype(jnp.bfloat16)


class Unit:
    def __init__(self, place, signals, spare, out):
        self.x, self.y, self.z, self.core, self.inner, self.peers = place
        self.signals = signals
        self.keep_a, self.keep_b, self.one_a, self.one_b, self.two_a, self.two_b = spare[:6]
        self.layer, self.three, self.merged, self.near, self.far, self.done = spare[6:]
        self.out = out

    def remote(self, src, dst, send, recv, peer):
        return pltpu.make_async_remote_copy(
            src_ref=src, dst_ref=dst, send_sem=self.signals(send), recv_sem=self.signals(recv),
            device_id=peer, device_id_type=MESH_ID,
        )

    def loads(self, sources):
        places = (self.keep_a, self.keep_b, self.one_a, self.one_b)
        return [
            pltpu.make_async_copy(source, place, self.signals(index))
            for index, (source, place) in enumerate(zip(sources, places))
        ]

    def firsts(self, send_a, send_b):
        return [
            self.remote(send_a, self.one_a, 22, 24, self.peers["x"]),
            self.remote(send_b, self.one_b, 23, 25, self.peers["y"]),
        ]

    def seconds(self):
        return [
            self.remote(self.keep_a.at[:, 1 - self.y], self.two_a, 4, 6, self.peers["y"]),
            self.remote(self.keep_b.at[:, 1 - self.x], self.two_b, 5, 7, self.peers["x"]),
        ]

    def merge_first(self):
        def body(i, carry):
            for half in range(2):
                self.keep_a[i, half] = plus(self.keep_a[i, half], self.one_a[i, half])
                self.keep_b[i, half] = plus(self.keep_b[i, half], self.one_b[i, half])
            return carry

        lax.fori_loop(0, 4, body, 0)
        for copy in self.seconds():
            copy.start()

    def from_end(self):
        first = 1 - lax.div(self.z, 3)
        return self.remote(self.layer.at[pl.ds(first, 3)], self.three, 8, 9, self.peers["beside"])

    def to_end(self):
        return self.remote(self.layer.at[self.peers["end_z"]], self.near, 10, 11, self.peers["beside"])

    def across_inner(self):
        return self.remote(self.merged.at[0], self.far, 12, 14, self.peers["other_inner"])

    def across_end(self):
        return self.remote(self.merged.at[1], self.far, 13, 14, self.peers["far_end"])

    def merge_second(self):
        for copy in self.seconds():
            copy.wait_recv()

        def body(i, carry):
            self.layer[i, 0] = plus(self.keep_a[i, self.y], self.two_a[i])
            self.layer[i, 1] = plus(self.keep_b[i, self.x], self.two_b[i])
            return carry

        lax.fori_loop(0, 4, body, 0)

        @pl.when(self.inner)
        def _():
            self.to_end().start()

        @pl.when(jnp.logical_not(self.inner))
        def _():
            self.from_end().start()

    def merge_third(self):
        @pl.when(self.inner)
        def _():
            self.from_end().wait_recv()

            def body(i, carry):
                self.merged[0, i] = plus(self.layer[3 - self.z, i], self.three[1, i])
                self.merged[1, i] = plus(self.layer[6 - 3 * self.z, i], self.three[4 - 2 * self.z, i])
                return carry

            lax.fori_loop(0, 2, body, 0)
            self.across_inner().start()
            self.across_end().start()

    def own(self):
        return pltpu.make_async_copy(self.done, self.out(self.core, self.y), self.signals(15))

    def to_y(self):
        return self.remote(self.done, self.out(self.core, self.y), 16, 17, self.peers["y"])

    def to_core(self):
        return self.remote(self.done, self.out(self.core, self.y), 18, 19, self.peers["core"])

    def passed(self):
        place = self.out(self.core, 1 - self.y)
        return self.remote(place, place, 20, 21, self.peers["core"])

    def finish(self):
        self.across_inner().wait_recv()

        @pl.when(self.inner)
        def _():
            def body(i, carry):
                total = self.layer[self.z, i].astype(jnp.float32) + self.far[i].astype(jnp.float32)
                total = total + self.three[2 * self.z - 2, i].astype(jnp.float32)
                self.done[i] = total.astype(jnp.bfloat16)
                return carry

            lax.fori_loop(0, 2, body, 0)

        @pl.when(jnp.logical_not(self.inner))
        def _():
            self.to_end().wait_recv()

            def body(i, carry):
                total = self.layer[self.z, i].astype(jnp.float32) + self.far[i].astype(jnp.float32)
                total = total + self.near[i].astype(jnp.float32)
                self.done[i] = total.astype(jnp.bfloat16)
                return carry

            lax.fori_loop(0, 2, body, 0)

        self.own().start()
        self.to_y().start()
        self.to_core().start()

    def hand_on(self):
        self.to_y().wait_recv()
        self.passed().start()

    def drain(self):
        for copy in self.seconds():
            copy.wait_send()

        @pl.when(self.inner)
        def _():
            self.to_end().wait_send()
            self.across_inner().wait_send()
            self.across_end().wait_send()

        @pl.when(jnp.logical_not(self.inner))
        def _():
            self.from_end().wait_send()

        self.own().wait()
        self.to_y().wait_send()
        self.to_core().wait()
        self.passed().wait()


def reduce_kernel(chunks, keep_ref, came_a, came_b, weight_ref, out_ref, weight_out, *scratch):
    rows, weights, signals = scratch[:12], scratch[12:24], scratch[24]
    dp = lax.axis_index("dp")
    store = lax.axis_index("store")
    y, core = lax.div(dp, 2), lax.rem(dp, 2)
    z, x = lax.div(store, 2), lax.rem(store, 2)
    inner = (z == 1) | (z == 2)
    beside = z + 1 - 2 * lax.rem(z, 2)
    along = lambda to: (dp, to * 2 + x)
    peers = {
        "x": (dp, z * 2 + (1 - x)),
        "y": ((1 - y) * 2 + core, store),
        "core": (y * 2 + (1 - core), store),
        "beside": along(beside),
        "end_z": 3 * lax.div(z, 2),
        "other_inner": along(3 - z),
        "far_end": along(3 - 3 * lax.div(z, 2)),
    }
    place = (x, y, z, core, inner, peers)

    barrier = pltpu.get_barrier_semaphore()
    for peer in (peers["x"], peers["y"], peers["core"]) + tuple(along(lax.rem(z + hop, 4)) for hop in (1, 2, 3)):
        pl.semaphore_signal(barrier, inc=1, device_id=peer, device_id_type=MESH_ID)
    pl.semaphore_wait(barrier, 6)

    units = [
        Unit(
            place, lambda kind, q=q: signals.at[kind, q], [ref.at[q] for ref in rows],
            lambda c, h, q=q: out_ref.at[c, h, :, q],
        )
        for q in range(chunks)
    ]
    extra = Unit(
        place, lambda kind: signals.at[kind, chunks], weights, lambda c, h: weight_out.at[c, h]
    )
    extra_first = extra.firsts(weight_ref.at[:, 1 - x, :, 0], weight_ref.at[:, :, 1 - y, 1])
    extra_loads = extra.loads((weight_ref.at[:, x, :, 0], weight_ref.at[:, :, y, 1]))
    loads = [
        unit.loads((keep_ref.at[0, :, :, q], keep_ref.at[1, :, :, q], came_a.at[:, :, q], came_b.at[:, :, q]))
        for q, unit in enumerate(units)
    ]
    for copy in loads[0] + extra_first + extra_loads:
        copy.start()
    for some in loads[1:]:
        for copy in some:
            copy.start()
    stages = ("merge_second", "merge_third", "finish", "hand_on")
    for step in range(chunks + LAG * len(stages)):
        if step < chunks:
            for copy in loads[step]:
                copy.wait()
            units[step].merge_first()
        if step == 2:
            for copy in extra_loads:
                copy.wait()
            for copy in extra_first:
                copy.wait_recv()
            extra.merge_first()
        for stage, name in enumerate(stages, 1):
            if 0 <= step - LAG * stage < chunks:
                getattr(units[step - LAG * stage], name)()
            if step == 2 + LAG * stage:
                getattr(extra, name)()
    for copy in extra_first:
        copy.wait_send()
    for unit in units + [extra]:
        unit.drain()


def reduce_rows(keep, came_a, came_b, weights, collective_id=0):
    rows = keep.shape[0] // 4
    chunks = rows // (4 * CHUNK)
    high = weights.shape[0] // 32

    def spare(high, *lead):
        return [
            pltpu.VMEM(lead + part + (high, D), jnp.bfloat16)
            for part in ((4, 2),) * 4 + ((4,), (4,), (4, 2), (3, 2), (2, 2), (2,), (2,), (2,))
        ]

    out, weights = pl.pallas_call(
        functools.partial(reduce_kernel, chunks),
        out_shape=[
            jax.ShapeDtypeStruct((2, 2, 2, chunks, CHUNK, D), jnp.bfloat16),
            jax.ShapeDtypeStruct((2, 2, 2, high, D), jnp.bfloat16),
        ],
        in_specs=[pl.BlockSpec(memory_space=pl.ANY)] * 4,
        out_specs=[pl.BlockSpec(memory_space=pl.ANY)] * 2,
        scratch_shapes=spare(CHUNK, chunks) + spare(high) + [pltpu.SemaphoreType.DMA((SIGNALS, chunks + 1))],
        compiler_params=pltpu.CompilerParams(
            collective_id=collective_id, has_side_effects=True, vmem_limit_bytes=VMEM_LIMIT
        ),
        cost_estimate=pl.CostEstimate(flops=0, transcendentals=0, bytes_accessed=450_000_000),
        name="reduce_rows",
    )(
        keep.reshape(2, 4, 2, chunks, CHUNK, D),
        came_a.reshape(4, 2, chunks, CHUNK, D),
        came_b.reshape(4, 2, chunks, CHUNK, D),
        weights.reshape(4, 2, 2, 2, high, D),
    )
    return out.reshape(2 * rows, D), weights.reshape(8 * high, D)


PAIRS = ((0, 1), (1, 0), (2, 3), (3, 2))


def own_rows(flat, rows_here):
    half = rows_here // 2
    quarter = half // 4
    dp = lax.axis_index("dp")
    here_y, core = dp // 2, dp % 2
    here_x = lax.axis_index("store") % 2
    owner, local = flat // rows_here, flat % rows_here
    z, x = owner // 2, owner % 2
    y = (local % half) // (2 * quarter)
    second = (local // quarter) % 2
    stays = jnp.where(second == 0, x == here_x, y == here_y)
    pair = jnp.where(second == 0, y, x)
    rows = 8 * half
    target = (2 * stays + second) * (rows // 4) + (2 * z + pair) * quarter + local % quarter
    return jnp.where(local // half == core, target, rows)


def plan_store(indices, rows_here):
    flat = indices.reshape(-1)
    other = lax.ppermute(flat, "dp", PAIRS)
    where = jnp.concatenate([own_rows(flat, rows_here), own_rows(other, rows_here)])
    return scatter_plan(where, lax.axis_size("store") * rows_here // 2)


def add_store(plan, own, other, rows_here):
    return scatter_rows(plan, own, other, lax.axis_size("store") * rows_here // 2)


def swap_store(send_a, send_b):
    owners = lax.axis_size("store")
    came_a = lax.ppermute(send_a, "store", [(i, i ^ 1) for i in range(owners)])
    came_b = lax.ppermute(send_b, "dp", [(i, i ^ 2) for i in range(4)])
    return came_a, came_b


def by_owner(matrix):
    owners = lax.axis_size("store")
    return matrix.astype(jnp.bfloat16).reshape(owners, -1, D)


def reduce_packed(packed):
    return lax.psum_scatter(
        packed.reshape(-1, D), ("store", "dp"), scatter_dimension=0, tiled=True
    )


def all_copies(share):
    return lax.all_gather(share, "dp", axis=0, tiled=True).astype(jnp.float32)


def pack_early(inner, outer, squares):
    blocks = [inner[:, block * D : (block + 1) * D] for block in range(inner.shape[1] // D)]
    return jnp.concatenate([by_owner(piece) for piece in blocks + [outer] + list(squares)], axis=1)


def unpack_early(total, wide):
    part = D // lax.axis_size("store")
    inner_total = jnp.transpose(total[: wide * part].reshape(wide, part, D), (1, 0, 2))
    rest = total[wide * part :]
    return (
        inner_total.reshape(part, wide * D),
        rest[: wide * part],
        rest[wide * part :].reshape(-1, part, D),
    )


def pack_late(squares, features, inner_bias):
    owners = lax.axis_size("store")
    part = D // owners
    wide = inner_bias.shape[0] // D
    small = jnp.concatenate(
        [feature.astype(jnp.bfloat16).reshape(owners, part) for feature in features]
        + [inner_bias.astype(jnp.bfloat16).reshape(owners, wide * part)],
        axis=1,
    )
    small = jnp.pad(small, ((0, 0), (0, part * D - small.shape[1]))).reshape(owners, part, D)
    return jnp.concatenate([by_owner(square) for square in squares] + [small], axis=1)


def add_cores(packed):
    core = lax.axis_index("dp") % 2
    halves = packed.reshape(packed.shape[0], 2, -1, D)
    mine = lax.dynamic_index_in_dim(halves, core, axis=1, keepdims=False)
    other = lax.dynamic_index_in_dim(halves, 1 - core, axis=1, keepdims=False)
    other = lax.ppermute(other, "dp", PAIRS)
    return plus(mine, other).reshape(-1, D)


def unpack_late(total, count, features, wide):
    part = D // lax.axis_size("store")
    tail = total[count * part :].reshape(-1)
    table = tail[: features * part].reshape(features, part)
    return (
        total[: count * part].reshape(count, part, D),
        table,
        tail[features * part :][: wide * part],
    )


def cross_probs_of(folded, rows):
    scores = lax.dot_general(folded, rows, (((1,), (1,)), ((), ())), preferred_element_type=jnp.float32)
    token = lax.broadcasted_iota(jnp.int32, scores.shape, 0) % CROSS_TOKENS
    owner = lax.broadcasted_iota(jnp.int32, scores.shape, 1) // K
    scores = jnp.where(token == owner, scores, -1e30)
    raised = jnp.exp(scores - jnp.max(scores, axis=1, keepdims=True))
    return raised * (1.0 / jnp.sum(raised, axis=1, keepdims=True))


def cross_tiles(ref):
    tokens = ref.shape[1]
    for first in range(0, tokens, CROSS_TOKENS):
        yield pl.ds(first, CROSS_TOKENS), pl.ds(first * K, CROSS_TOKENS * K)


def cross_forward_kernel(folded_ref, rows_ref, summary_ref):
    for some, slots in cross_tiles(folded_ref):
        rows = rows_ref[slots, :]
        probs = cross_probs_of(folded_ref[:, some, :].reshape(H * CROSS_TOKENS, D), rows)
        summary = jnp.dot(probs.astype(jnp.bfloat16), rows, preferred_element_type=jnp.float32)
        summary_ref[:, some, :] = summary.astype(jnp.bfloat16).reshape(H, CROSS_TOKENS, D)


def cross_backward_kernel(folded_ref, grad_ref, rows_ref, row_grad_ref, folded_grad_ref):
    for some, slots in cross_tiles(folded_ref):
        rows = rows_ref[slots, :]
        folded = folded_ref[:, some, :].reshape(H * CROSS_TOKENS, D)
        grad = grad_ref[:, some, :].reshape(H * CROSS_TOKENS, D)
        probs = cross_probs_of(folded, rows)
        prob_grad = lax.dot_general(
            grad, rows, (((1,), (1,)), ((), ())), preferred_element_type=jnp.float32
        )
        total = jnp.sum(probs * prob_grad, axis=1, keepdims=True)
        score_low = (probs * (prob_grad - total)).astype(jnp.bfloat16)
        turned = (((0,), (0,)), ((), ()))
        row_grad = lax.dot_general(
            probs.astype(jnp.bfloat16), grad, turned, preferred_element_type=jnp.float32
        )
        row_grad += lax.dot_general(score_low, folded, turned, preferred_element_type=jnp.float32)
        row_grad_ref[slots, :] = row_grad.astype(jnp.bfloat16)
        folded_grad = jnp.dot(score_low, rows, preferred_element_type=jnp.float32)
        folded_grad_ref[:, some, :] = folded_grad.astype(jnp.bfloat16).reshape(H, CROSS_TOKENS, D)


CROSS_TOKENS = 16
CROSS_STEP = 64


def cross_specs():
    heads = pl.BlockSpec((H, CROSS_STEP, D), lambda i: (0, i, 0))
    rows = pl.BlockSpec((CROSS_STEP * K, D), lambda i: (i, 0))
    return heads, rows


def cross_forward(folded, fetched):
    heads, rows = cross_specs()
    tokens = folded.shape[1]
    return pl.pallas_call(
        cross_forward_kernel,
        out_shape=jax.ShapeDtypeStruct((H, tokens, D), jnp.bfloat16),
        grid=(tokens // CROSS_STEP,),
        in_specs=[heads, rows],
        out_specs=heads,
        cost_estimate=pl.CostEstimate(flops=0, transcendentals=0, bytes_accessed=55_000_000),
        name="cross_forward",
    )(folded, fetched)


def cross_backward(folded, grad, fetched):
    heads, rows = cross_specs()
    tokens = folded.shape[1]
    return pl.pallas_call(
        cross_backward_kernel,
        out_shape=[
            jax.ShapeDtypeStruct((tokens * K, D), jnp.bfloat16),
            jax.ShapeDtypeStruct((H, tokens, D), jnp.bfloat16),
        ],
        grid=(tokens // CROSS_STEP,),
        in_specs=[heads, heads, rows],
        out_specs=[rows, heads],
        cost_estimate=pl.CostEstimate(flops=0, transcendentals=0, bytes_accessed=100_000_000),
        name="cross_backward",
    )(folded, grad, fetched)


def body(
    tokens,
    datastore,
    indices,
    lengths,
    proj_weight,
    out_weight,
    proj_bias,
    norm_gain,
    norm_bias,
    inner_weight,
    inner_bias,
    outer_weight,
    outer_bias,
    cotangent,
):
    seq_len = tokens.shape[0]
    score_scale = HD ** (-0.5)
    owners = lax.axis_size("store")
    rows_here = datastore.shape[0]
    capacity = 2 * seq_len * K // owners
    position = jnp.arange(seq_len)
    length = lengths[0]
    allowed = (position[None, :] <= position[:, None]) & (position[None, :] < length)
    valid = (position < length)[:, None]
    dense = is_dense(owners, rows_here)
    if dense:
        plan = plan_store(indices, rows_here)
        fetched, plan = fetch_dense(datastore, indices, plan)
    else:
        target, request = route_slots(indices, rows_here, owners, capacity)
        returned, _ = fetch_rows(request, datastore)
        fetched = returned.reshape(owners * capacity, D)[target].reshape(seq_len, K, D)
    self_bias = jnp.concatenate([proj_bias[:, 0], jnp.zeros((D,), jnp.float32), proj_bias[:, 1]])
    self_proj = proj_weight[:, 0:3, :].reshape(D, 3 * D)
    joined = (product(tokens, self_proj) + self_bias).astype(jnp.bfloat16)
    queries = joined[:, :D].reshape(seq_len, H, HD)
    self_keys = joined[:, D : 2 * D].reshape(seq_len, H, HD)
    values = joined[:, 2 * D :].reshape(seq_len, H, HD)
    scores = self_scores(queries, self_keys, allowed, score_scale)
    self_lse = log_total(scores)
    self_probs = jnp.exp(scores - self_lse).astype(jnp.bfloat16)
    self_mixed = (
        jnp.einsum("hqk,khe->qhe", self_probs, values, preferred_element_type=jnp.float32)
        .reshape(seq_len, D)
        .astype(jnp.bfloat16)
    )
    first_pre = tokens.astype(jnp.float32) + (
        product(self_mixed, out_weight[:, 0, :]) + proj_bias[:, 2]
    )
    first_out, first_normed, first_inverse = norm_forward(
        first_pre, norm_gain[:, 0], norm_bias[:, 0]
    )
    first_low = first_out.astype(jnp.bfloat16)
    cross_query = (
        (product(first_low, proj_weight[:, 3, :]) + proj_bias[:, 3])
        .astype(jnp.bfloat16)
        .reshape(seq_len, H, HD)
    )
    key_heads = proj_weight[:, 4, :].reshape(D, H, HD)
    folded = (
        jnp.einsum("the,dhe->thd", cross_query, key_heads, preferred_element_type=jnp.float32)
        * score_scale
    ).astype(jnp.bfloat16)
    if dense:
        folded_heads = jnp.transpose(folded, (1, 0, 2))
        summary = jnp.transpose(cross_forward(folded_heads, fetched), (1, 0, 2))
    else:
        cross_scores = jnp.einsum("thd,tkd->thk", folded, fetched, preferred_element_type=jnp.float32)
        cross_lse = log_total(cross_scores)
        cross_full = jnp.exp(cross_scores - cross_lse)
        cross_probs = cross_full.astype(jnp.bfloat16)
        summary = jnp.einsum(
            "thk,tkd->thd", cross_probs, fetched, preferred_element_type=jnp.float32
        ).astype(jnp.bfloat16)
    value_heads = proj_weight[:, 5, :].reshape(D, H, HD)
    cross_mixed = (
        jnp.einsum(
            "thd,dhe->the", summary, value_heads, preferred_element_type=jnp.float32
        ).reshape(seq_len, D)
        + proj_bias[:, 4]
    ).astype(jnp.bfloat16)
    second_pre = first_out + (product(cross_mixed, out_weight[:, 1, :]) + proj_bias[:, 5])
    second_out, second_normed, second_inverse = norm_forward(
        second_pre, norm_gain[:, 1], norm_bias[:, 1]
    )
    second_low = second_out.astype(jnp.bfloat16)
    inner_pre = product(second_low, inner_weight) + inner_bias
    activated = jax.nn.gelu(inner_pre, approximate=False).astype(jnp.bfloat16)
    third_pre = second_out + (product(activated, outer_weight) + outer_bias)
    third_out, third_normed, third_inverse = norm_forward(
        third_pre, norm_gain[:, 2], norm_bias[:, 2]
    )
    output = jnp.where(valid, third_out, 0.0).astype(jnp.bfloat16)
    upstream = jnp.where(valid, cotangent.astype(jnp.float32), 0.0)
    third_grad, gain_three, shift_three = norm_backward(
        upstream, third_normed, third_inverse, norm_gain[:, 2]
    )
    outer_low = third_grad.astype(jnp.bfloat16)
    grad_outer_weight = contract_rows(activated, outer_low)
    grad_outer_bias = column_sum(outer_low)
    act_grad = product_back(outer_low, outer_weight)
    slope = jax.vjp(lambda activation_in: jax.nn.gelu(activation_in, approximate=False), inner_pre)[
        1
    ](act_grad)[0]
    inner_low = slope.astype(jnp.bfloat16)
    grad_inner_weight = contract_rows(second_low, inner_low)
    grad_inner_bias = column_sum(inner_low)
    second_up = third_grad + product_back(inner_low, inner_weight)
    second_grad, gain_two, shift_two = norm_backward(
        second_up, second_normed, second_inverse, norm_gain[:, 1]
    )
    cross_out_low = second_grad.astype(jnp.bfloat16)
    grad_cross_out = contract_rows(cross_mixed, cross_out_low)
    bias_five = column_sum(cross_out_low)
    mixed_low = product_back(cross_out_low, out_weight[:, 1, :]).astype(jnp.bfloat16)
    bias_four = column_sum(mixed_low)
    mixed_heads = mixed_low.reshape(seq_len, H, HD)
    grad_value_heads = jnp.einsum(
        "thd,the->dhe", summary, mixed_heads, preferred_element_type=jnp.float32
    )
    if dense:
        packed_early = pack_early(grad_inner_weight, grad_outer_weight, (grad_cross_out,))
        mixed_heads, packed_early = lax.optimization_barrier((mixed_heads, packed_early))
        share_early = reduce_packed(packed_early)
    summary_low = jnp.einsum(
        "the,dhe->thd", mixed_heads, value_heads, preferred_element_type=jnp.float32
    ).astype(jnp.bfloat16)
    if dense:
        own_grad, folded_low = cross_backward(
            folded_heads, jnp.transpose(summary_low, (1, 0, 2)), fetched
        )
        folded_low = jnp.transpose(folded_low, (1, 0, 2))
        other_grad = lax.ppermute(own_grad, "dp", PAIRS)
    else:
        returned_again, asked_back = fetch_again(request, datastore)
        fetched_back = returned_again.reshape(owners * capacity, D)[target].reshape(seq_len, K, D)
        prob_grad = jnp.einsum(
            "thd,tkd->thk", summary_low, fetched_back, preferred_element_type=jnp.float32
        )
        score_low = (
            cross_full * (prob_grad - jnp.sum(cross_full * prob_grad, axis=-1, keepdims=True))
        ).astype(jnp.bfloat16)
        row_grad = (
            jnp.einsum("thk,thd->tkd", cross_probs, summary_low, preferred_element_type=jnp.float32)
            + jnp.einsum("thk,thd->tkd", score_low, folded, preferred_element_type=jnp.float32)
        ).astype(jnp.bfloat16)
        folded_low = jnp.einsum(
            "thk,tkd->thd", score_low, fetched_back, preferred_element_type=jnp.float32
        ).astype(jnp.bfloat16)
    grad_key_heads = (
        jnp.einsum("thd,the->dhe", folded_low, cross_query, preferred_element_type=jnp.float32)
        * score_scale
    )
    query_low = (
        (
            jnp.einsum("thd,dhe->the", folded_low, key_heads, preferred_element_type=jnp.float32)
            * score_scale
        )
        .astype(jnp.bfloat16)
        .reshape(seq_len, D)
    )
    if dense:
        query_low, other_grad = lax.optimization_barrier((query_low, other_grad))
        send_a, send_b, keep = add_store(plan, own_grad, other_grad, rows_here)
        query_low, mixed_heads, send_a, send_b, keep = lax.optimization_barrier(
            (query_low, mixed_heads, send_a, send_b, keep)
        )
        grad_value_heads = jnp.einsum(
            "thd,the->dhe", summary, mixed_heads, preferred_element_type=jnp.float32
        )
        came_a, came_b = swap_store(send_a, send_b)
    bias_three = column_sum(query_low)
    grad_cross_query = contract_rows(first_low, query_low)
    if not dense:
        grad_buffer = (
            jnp.zeros((owners * capacity, D), jnp.bfloat16)
            .at[target]
            .set(row_grad.reshape(-1, D))
            .reshape(owners, capacity, D)
        )
        arrived = lax.all_to_all(grad_buffer, "store", split_axis=0, concat_axis=0, tiled=True)
        partial_store = (
            jnp.zeros((rows_here, D), jnp.float32)
            .at[asked_back.reshape(-1)]
            .add(arrived.reshape(-1, D).astype(jnp.float32))
        )
        grad_store = lax.psum(partial_store.astype(jnp.bfloat16), "dp").astype(jnp.float32)
    first_up = second_grad + product_back(query_low, proj_weight[:, 3, :])
    first_grad, gain_one, shift_one = norm_backward(
        first_up, first_normed, first_inverse, norm_gain[:, 0]
    )
    self_out_low = first_grad.astype(jnp.bfloat16)
    grad_self_out = contract_rows(self_mixed, self_out_low)
    bias_two = column_sum(self_out_low)
    self_mixed_low = (
        product_back(self_out_low, out_weight[:, 0, :]).astype(jnp.bfloat16).reshape(seq_len, H, HD)
    )
    value_grad = jnp.einsum(
        "hqk,qhe->khe", self_probs, self_mixed_low, preferred_element_type=jnp.float32
    )
    attend_grad = jnp.einsum(
        "qhe,khe->hqk", self_mixed_low, values, preferred_element_type=jnp.float32
    )
    self_full = jnp.exp(self_scores(queries, self_keys, allowed, score_scale) - self_lse)
    self_score_low = (
        self_full * (attend_grad - jnp.sum(self_full * attend_grad, axis=-1, keepdims=True))
    ).astype(jnp.bfloat16)
    query_grad = (
        jnp.einsum("hqk,khe->qhe", self_score_low, self_keys, preferred_element_type=jnp.float32)
        * score_scale
    )
    key_grad = (
        jnp.einsum("hqk,qhe->khe", self_score_low, queries, preferred_element_type=jnp.float32)
        * score_scale
    )
    joined_low = jnp.concatenate(
        [
            query_grad.reshape(seq_len, D),
            key_grad.reshape(seq_len, D),
            value_grad.reshape(seq_len, D),
        ],
        axis=1,
    ).astype(jnp.bfloat16)
    grad_self_proj = contract_rows(tokens, joined_low).reshape(D, 3, D)
    bias_zero = column_sum(joined_low[:, :D])
    bias_one = column_sum(joined_low[:, 2 * D :])
    grad_tokens = (first_grad + product_back(joined_low, self_proj)).astype(jnp.bfloat16)
    if dense:
        packed_late = pack_late(
            (
                grad_self_proj[:, 0],
                grad_self_proj[:, 1],
                grad_self_proj[:, 2],
                grad_cross_query,
                grad_key_heads.reshape(D, D),
                grad_value_heads.reshape(D, D),
                grad_self_out,
            ),
            (bias_zero, bias_one, bias_two, bias_three, bias_four, bias_five)
            + (gain_one, gain_two, gain_three)
            + (shift_one, shift_two, shift_three)
            + (grad_outer_bias,),
            grad_inner_bias,
        )
        wide = grad_inner_bias.shape[0] // D
        early_totals = unpack_early(all_copies(share_early), wide)
        keep, came_a, came_b, output, grad_tokens, early_totals = lax.optimization_barrier(
            (keep, came_a, came_b, output, grad_tokens, early_totals)
        )
        inner_total, outer_total, early = early_totals
        grad_store, total_late = reduce_rows(keep, came_a, came_b, add_cores(packed_late))
        grad_store = grad_store.astype(jnp.float32)
        late, table, bias_inner = unpack_late(total_late.astype(jnp.float32), 7, 13, wide)
        return (
            output,
            grad_tokens,
            grad_store,
            jnp.stack([late[0], late[1], late[2], late[3], late[4], late[5]], axis=1),
            jnp.stack([late[6], early[0]], axis=1),
            jnp.transpose(table[0:6]),
            jnp.transpose(table[6:9]),
            jnp.transpose(table[9:12]),
            inner_total,
            bias_inner,
            outer_total,
            table[12],
        )
    grad_proj = jnp.stack(
        [
            grad_self_proj[:, 0],
            grad_self_proj[:, 1],
            grad_self_proj[:, 2],
            grad_cross_query,
            grad_key_heads.reshape(D, D),
            grad_value_heads.reshape(D, D),
        ],
        axis=1,
    )
    grad_out = jnp.stack([grad_self_out, grad_cross_out], axis=1)
    grad_bias = jnp.stack([bias_zero, bias_one, bias_two, bias_three, bias_four, bias_five], axis=1)
    grad_gain = jnp.stack([gain_one, gain_two, gain_three], axis=1)
    grad_shift = jnp.stack([shift_one, shift_two, shift_three], axis=1)
    shares = (
        lax.psum_scatter(
            grad_proj.astype(jnp.bfloat16), "store", scatter_dimension=0, tiled=True
        ).astype(jnp.float32),
        lax.psum_scatter(
            grad_out.astype(jnp.bfloat16), "store", scatter_dimension=0, tiled=True
        ).astype(jnp.float32),
        lax.psum_scatter(
            grad_bias.astype(jnp.bfloat16), "store", scatter_dimension=0, tiled=True
        ).astype(jnp.float32),
        lax.psum_scatter(
            grad_gain.astype(jnp.bfloat16), "store", scatter_dimension=0, tiled=True
        ).astype(jnp.float32),
        lax.psum_scatter(
            grad_shift.astype(jnp.bfloat16), "store", scatter_dimension=0, tiled=True
        ).astype(jnp.float32),
        lax.psum_scatter(
            grad_inner_weight.astype(jnp.bfloat16), "store", scatter_dimension=0, tiled=True
        ).astype(jnp.float32),
        lax.psum_scatter(
            grad_inner_bias.astype(jnp.bfloat16), "store", scatter_dimension=0, tiled=True
        ).astype(jnp.float32),
        lax.psum_scatter(
            grad_outer_weight.astype(jnp.bfloat16), "store", scatter_dimension=0, tiled=True
        ).astype(jnp.float32),
        lax.psum_scatter(
            grad_outer_bias.astype(jnp.bfloat16), "store", scatter_dimension=0, tiled=True
        ).astype(jnp.float32),
    )
    totals = (
        lax.psum(shares[0].astype(jnp.bfloat16), "dp").astype(jnp.float32),
        lax.psum(shares[1].astype(jnp.bfloat16), "dp").astype(jnp.float32),
        lax.psum(shares[2].astype(jnp.bfloat16), "dp").astype(jnp.float32),
        lax.psum(shares[3].astype(jnp.bfloat16), "dp").astype(jnp.float32),
        lax.psum(shares[4].astype(jnp.bfloat16), "dp").astype(jnp.float32),
        lax.psum(shares[5].astype(jnp.bfloat16), "dp").astype(jnp.float32),
        lax.psum(shares[6].astype(jnp.bfloat16), "dp").astype(jnp.float32),
        lax.psum(shares[7].astype(jnp.bfloat16), "dp").astype(jnp.float32),
        lax.psum(shares[8].astype(jnp.bfloat16), "dp").astype(jnp.float32),
    )
    return (
        output,
        grad_tokens,
        grad_store,
        totals[0],
        totals[1],
        totals[2],
        totals[3],
        totals[4],
        totals[5],
        totals[6],
        totals[7],
        totals[8],
    )


def solution(mesh):
    in_specs = (
        P(("dp", "store"), None),
        P("store", None),
        P(("dp", "store"), None),
        P(("dp", "store")),
        P(),
        P(),
        P(),
        P(),
        P(),
        P(),
        P(),
        P(),
        P(),
        P(("dp", "store"), None),
    )
    out_specs = (
        P(("dp", "store"), None),
        P(("dp", "store"), None),
        P("store", None),
        P("store", None, None),
        P("store", None, None),
        P("store", None),
        P("store", None),
        P("store", None),
        P("store", None),
        P("store"),
        P("store", None),
        P("store"),
    )

    return jax.shard_map(body, mesh=mesh, in_specs=in_specs, out_specs=out_specs, check_vma=False)
```

```python
import functools

import jax
import jax.numpy as jnp
from jax import lax
from jax.experimental import pallas as pl
from jax.experimental.pallas import tpu as pltpu
from jax.sharding import PartitionSpec as P


D = 768
H = 12
HD = 64
K = 16


EPSILON = 1e-05


def product(matrix, factor):
    return jnp.dot(matrix, factor, preferred_element_type=jnp.float32)


def product_back(matrix, weight):
    return jnp.einsum("tf,df->td", matrix, weight, preferred_element_type=jnp.float32)


def contract_rows(matrix, factor):
    return jnp.einsum("td,tf->df", matrix, factor, preferred_element_type=jnp.float32)


def column_sum(matrix):
    return jnp.sum(matrix.astype(jnp.float32), axis=0)


def norm_forward(hidden, norm_weight, norm_shift):
    centered = hidden - jnp.mean(hidden, axis=-1, keepdims=True)
    inverse = lax.rsqrt(jnp.mean(centered * centered, axis=-1, keepdims=True) + EPSILON)
    normed = centered * inverse
    return (normed * norm_weight + norm_shift, normed, inverse)


def norm_backward(upstream, normed, inverse, norm_weight):
    scaled = upstream * norm_weight
    plain_mean = jnp.mean(scaled, axis=-1, keepdims=True)
    normed_mean = jnp.mean(scaled * normed, axis=-1, keepdims=True)
    return (
        inverse * (scaled - plain_mean - normed * normed_mean),
        jnp.sum(upstream * normed, axis=0),
        jnp.sum(upstream, axis=0),
    )


def log_total(scores):
    highest = jnp.max(scores, axis=-1, keepdims=True)
    return highest + jnp.log(jnp.sum(jnp.exp(scores - highest), axis=-1, keepdims=True))


def route_slots(picked, rows_here, owners, capacity):
    flat_ids = picked.reshape(-1)
    owner_of = flat_ids // rows_here
    local_row = flat_ids % rows_here
    by_owner = jnp.argsort(owner_of, stable=True)
    sorted_owner = owner_of[by_owner]
    owner_loads = jnp.sum(
        (owner_of[:, None] == jnp.arange(owners, dtype=jnp.int32)[None, :]).astype(jnp.int32),
        axis=0,
    )
    starts = jnp.cumsum(owner_loads) - owner_loads
    within = jnp.arange(flat_ids.shape[0], dtype=jnp.int32) - starts[sorted_owner]
    placed = jnp.zeros_like(flat_ids).at[by_owner].set(within)
    target = owner_of * capacity + placed
    request = jnp.zeros((owners * capacity,), jnp.int32).at[target].set(local_row)
    return (target, request.reshape(owners, capacity))


def fetch_rows(request, datastore):
    asked_rows = lax.all_to_all(request, "store", split_axis=0, concat_axis=0, tiled=True)
    found_rows = datastore[asked_rows.reshape(-1)].reshape(asked_rows.shape + (datastore.shape[1],))
    return (
        lax.all_to_all(found_rows, "store", split_axis=0, concat_axis=0, tiled=True),
        asked_rows,
    )


def fetch_again(request, datastore):
    asked_rows = lax.all_to_all(request, "store", split_axis=0, concat_axis=0, tiled=True)
    found_rows = datastore[asked_rows.reshape(-1)].reshape(asked_rows.shape + (datastore.shape[1],))
    return (
        lax.all_to_all(found_rows, "store", split_axis=0, concat_axis=0, tiled=True),
        asked_rows,
    )


def self_scores(queries, self_keys, allowed, score_scale):
    scores = (
        jnp.einsum("qhe,khe->hqk", queries, self_keys, preferred_element_type=jnp.float32)
        * score_scale
    )
    return jnp.where(allowed[None], scores, -1e30)


DENSE_LIMIT = 1 << 16


def is_dense(owners, rows_here):
    fits = owners * rows_here <= DENSE_LIMIT and rows_here % (8 * CHUNK) == 0 and owners * rows_here % GATHER_BLOCK == 0
    return fits and owners == 8 and lax.axis_size("dp") == 4


def fetch_dense(datastore, indices, plan):
    copies = lax.axis_size("dp")
    rows_here = datastore.shape[0]
    share = rows_here // copies
    mine = lax.dynamic_slice_in_dim(datastore, lax.axis_index("dp") * share, share, axis=0)
    table = lax.all_gather(mine, ("store", "dp"), axis=0, tiled=True)
    picks = gather_plan(indices, table.shape[0])
    picks, plan = lax.optimization_barrier((picks, plan))
    return gather_rows(picks, table, indices.size), plan


MESH_ID = pl.DeviceIdType.MESH
VMEM_LIMIT = 67043328
CHUNK = 64


GROUP = 8


SPLIT = D // 128


def widen(ref, wide):
    def strip(i, carry):
        first = pl.multiple_of(i * 32, 32)
        value = ref[pl.ds(first, 32), :].astype(jnp.float32)
        for part in range(SPLIT):
            wide[pl.ds(first * SPLIT + part, 32, stride=SPLIT), :] = value[:, part * 128 : (part + 1) * 128]
        return carry

    lax.fori_loop(0, ref.shape[0] // 32, strip, 0, unroll=4)


def narrow(total, start, out_ref):
    def strip(i, carry):
        first = pl.multiple_of(start * SPLIT + i * (32 * SPLIT), 32 * SPLIT)
        for part in range(SPLIT):
            value = total[pl.ds(first + part, 32, stride=SPLIT), :]
            out_ref[pl.ds(pl.multiple_of(i * 32, 32), 32), part * 128 : (part + 1) * 128] = value.astype(jnp.bfloat16)
        return carry

    lax.fori_loop(0, out_ref.shape[0] // 32, strip, 0, unroll=4)


GATHER_BLOCK = 4096


def gather_kernel(blocks, out_rows, row_ref, to_ref, start_ref, table_ref, out_ref, wide, found):
    step = pl.program_id(0)

    @pl.when(step < blocks)
    def _():
        widen(table_ref, wide)
        base = step * (GATHER_BLOCK * SPLIT)
        first = start_ref[step]

        def group(i, carry):
            at = first + i * GROUP
            rows = [
                jnp.minimum(row_ref[at + k] - base, (GATHER_BLOCK - 1) * SPLIT) for k in range(GROUP)
            ]
            places = [to_ref[at + k] for k in range(GROUP)]
            values = [wide[pl.ds(row, SPLIT), :] for row in rows]
            for place, value in zip(places, values):
                found[pl.ds(place, SPLIT), :] = value
            return carry

        lax.fori_loop(0, lax.div(start_ref[step + 1] - first + GROUP - 1, GROUP), group, 0)

    @pl.when(step >= blocks)
    def _():
        narrow(found, (step - blocks) * out_rows, out_ref)


def gather_plan(indices, rows):
    flat = indices.reshape(-1)
    count = flat.shape[0]
    row, place = lax.sort((flat, jnp.arange(count, dtype=jnp.int32)), dimension=0, num_keys=1)
    bounds = jnp.arange(rows // GATHER_BLOCK + 1, dtype=jnp.int32) * GATHER_BLOCK
    starts = jnp.sum((flat[:, None] < bounds[None, :]).astype(jnp.int32), axis=0)
    row = jnp.concatenate([row, jnp.full((GROUP,), rows - 1, jnp.int32)])
    place = jnp.concatenate([place, jnp.full((GROUP,), count, jnp.int32)])
    return SPLIT * row, SPLIT * place, starts


def gather_rows(plan, table, count, out_rows=2048):
    blocks = table.shape[0] // GATHER_BLOCK
    return pl.pallas_call(
        functools.partial(gather_kernel, blocks, out_rows),
        out_shape=jax.ShapeDtypeStruct((count, D), jnp.bfloat16),
        grid_spec=pltpu.PrefetchScalarGridSpec(
            num_scalar_prefetch=3,
            grid=(blocks + count // out_rows,),
            in_specs=[pl.BlockSpec((GATHER_BLOCK, D), lambda i, *_: (jnp.minimum(i, blocks - 1), 0))],
            out_specs=pl.BlockSpec((out_rows, D), lambda i, *_: (jnp.maximum(i - blocks, 0), 0)),
            scratch_shapes=[
                pltpu.VMEM((GATHER_BLOCK * SPLIT, 128), jnp.float32),
                pltpu.VMEM(((count + 8) * SPLIT, 128), jnp.float32),
            ],
        ),
        compiler_params=pltpu.CompilerParams(vmem_limit_bytes=VMEM_LIMIT),
        cost_estimate=pl.CostEstimate(flops=0, transcendentals=0, bytes_accessed=160_000_000),
        name="gather_rows",
    )(*plan, table)


def scatter_kernel(steps, block, out_rows, row_ref, from_ref, twice_ref, groups_ref, own_ref, other_ref, *rest):
    outs, (total, wide) = rest[:-2], rest[-2:]
    step = pl.program_id(0)

    @pl.when(step == 0)
    def _():
        def clear(i, carry):
            total[pl.ds(i * 192, 192), :] = jnp.zeros((192, 128), jnp.float32)
            return carry

        lax.fori_loop(0, total.shape[0] // 192, clear, 0, unroll=4)

    @pl.when(step < steps // 2)
    def _():
        widen(own_ref, wide)

    @pl.when((step >= steps // 2) & (step < steps))
    def _():
        widen(other_ref, wide)

    @pl.when(step < steps)
    def _():
        def group(i, carry):
            first = step * block + i * GROUP
            rows = [row_ref[first + k] for k in range(GROUP)]
            came = [from_ref[first + k] for k in range(GROUP)]
            twice = twice_ref[step * (block // GROUP) + i]

            @pl.when(twice == 0)
            def _():
                sums = [total[pl.ds(rows[k], SPLIT), :] + wide[pl.ds(came[k], SPLIT), :] for k in range(GROUP)]
                for k in range(GROUP):
                    total[pl.ds(rows[k], SPLIT), :] = sums[k]

            @pl.when(twice != 0)
            def _():
                for k in range(GROUP):
                    total[pl.ds(rows[k], SPLIT), :] = total[pl.ds(rows[k], SPLIT), :] + wide[pl.ds(came[k], SPLIT), :]

            return carry

        lax.fori_loop(0, groups_ref[step], group, 0)

    quarter = (total.shape[0] // SPLIT // 4) // out_rows
    for index, out_ref in enumerate(outs):
        last = quarter * (index + 1 if index < 2 else 4)

        @pl.when((step >= steps + quarter * index) & (step < steps + last))
        def _(out_ref=out_ref):
            narrow(total, (step - steps) * out_rows, out_ref)


SCATTER_BLOCK = 1024


def scatter_plan(where, rows):
    keys = jnp.arange(where.shape[0], dtype=jnp.int32).reshape(-1, SCATTER_BLOCK) % SCATTER_BLOCK
    where = where.reshape(-1, SCATTER_BLOCK)
    skipped = where >= rows
    keys, where = lax.sort((jnp.where(skipped, keys + SCATTER_BLOCK, keys), where), dimension=1, num_keys=1)
    count = jnp.sum((~skipped).astype(jnp.int32), axis=1)
    groups = (count + GROUP - 1) // GROUP
    where = jnp.where(keys >= SCATTER_BLOCK, rows + keys % GROUP, where)
    spare = lax.broadcasted_iota(jnp.int32, where.shape, 1) % GROUP
    where = jnp.where(keys >= SCATTER_BLOCK, rows + spare, where)
    eights = where.reshape(-1, GROUP)
    twice = jnp.zeros((eights.shape[0],), jnp.int32)
    for shift in range(1, GROUP):
        same = eights[:, shift:] == eights[:, :-shift]
        twice = twice | jnp.any(same, axis=1).astype(jnp.int32)
    return SPLIT * where.reshape(-1), SPLIT * (keys % SCATTER_BLOCK).reshape(-1), twice, groups


def scatter_rows(plan, own, other, rows, out_rows=512):
    block = SCATTER_BLOCK
    half = own.shape[0] // block
    steps = 2 * half
    quarter = rows // 4 // out_rows

    def part(first, count):
        return pl.BlockSpec((out_rows, D), lambda i, *_: (jnp.clip(i - steps - first, 0, count - 1), 0))

    return pl.pallas_call(
        functools.partial(scatter_kernel, steps, block, out_rows),
        out_shape=[
            jax.ShapeDtypeStruct((rows // 4, D), jnp.bfloat16),
            jax.ShapeDtypeStruct((rows // 4, D), jnp.bfloat16),
            jax.ShapeDtypeStruct((rows // 2, D), jnp.bfloat16),
        ],
        grid_spec=pltpu.PrefetchScalarGridSpec(
            num_scalar_prefetch=4,
            grid=(steps + rows // out_rows,),
            in_specs=[
                pl.BlockSpec((block, D), lambda i, *_: (jnp.minimum(i, half - 1), 0)),
                pl.BlockSpec((block, D), lambda i, *_: (jnp.clip(i - half, 0, half - 1), 0)),
            ],
            out_specs=[part(0, quarter), part(quarter, quarter), part(2 * quarter, 2 * quarter)],
            scratch_shapes=[
                pltpu.VMEM(((rows + 32) * SPLIT, 128), jnp.float32),
                pltpu.VMEM((block * SPLIT, 128), jnp.float32),
            ],
        ),
        compiler_params=pltpu.CompilerParams(vmem_limit_bytes=VMEM_LIMIT),
        cost_estimate=pl.CostEstimate(flops=0, transcendentals=0, bytes_accessed=220_000_000),
        name="scatter_rows",
    )(*plan, own, other)


SIGNALS = 26
LAG = 2


def plus(first, second):
    return (first.astype(jnp.float32) + second.astype(jnp.float32)).astype(jnp.bfloat16)


class Unit:
    def __init__(self, place, signals, spare, out):
        self.x, self.y, self.z, self.core, self.inner, self.peers = place
        self.signals = signals
        self.keep_a, self.keep_b, self.one_a, self.one_b, self.two_a, self.two_b = spare[:6]
        self.layer, self.three, self.merged, self.near, self.far, self.done = spare[6:]
        self.out = out

    def remote(self, src, dst, send, recv, peer):
        return pltpu.make_async_remote_copy(
            src_ref=src, dst_ref=dst, send_sem=self.signals(send), recv_sem=self.signals(recv),
            device_id=peer, device_id_type=MESH_ID,
        )

    def loads(self, sources):
        places = (self.keep_a, self.keep_b, self.one_a, self.one_b)
        return [
            pltpu.make_async_copy(source, place, self.signals(index))
            for index, (source, place) in enumerate(zip(sources, places))
        ]

    def firsts(self, send_a, send_b):
        return [
            self.remote(send_a, self.one_a, 22, 24, self.peers["x"]),
            self.remote(send_b, self.one_b, 23, 25, self.peers["y"]),
        ]

    def seconds(self):
        return [
            self.remote(self.keep_a.at[:, 1 - self.y], self.two_a, 4, 6, self.peers["y"]),
            self.remote(self.keep_b.at[:, 1 - self.x], self.two_b, 5, 7, self.peers["x"]),
        ]

    def merge_first(self):
        def body(i, carry):
            for half in range(2):
                self.keep_a[i, half] = plus(self.keep_a[i, half], self.one_a[i, half])
                self.keep_b[i, half] = plus(self.keep_b[i, half], self.one_b[i, half])
            return carry

        lax.fori_loop(0, 4, body, 0)
        for copy in self.seconds():
            copy.start()

    def from_end(self):
        first = 1 - lax.div(self.z, 3)
        return self.remote(self.layer.at[pl.ds(first, 3)], self.three, 8, 9, self.peers["beside"])

    def to_end(self):
        return self.remote(self.layer.at[self.peers["end_z"]], self.near, 10, 11, self.peers["beside"])

    def across_inner(self):
        return self.remote(self.merged.at[0], self.far, 12, 14, self.peers["other_inner"])

    def across_end(self):
        return self.remote(self.merged.at[1], self.far, 13, 14, self.peers["far_end"])

    def merge_second(self):
        for copy in self.seconds():
            copy.wait_recv()

        def body(i, carry):
            self.layer[i, 0] = plus(self.keep_a[i, self.y], self.two_a[i])
            self.layer[i, 1] = plus(self.keep_b[i, self.x], self.two_b[i])
            return carry

        lax.fori_loop(0, 4, body, 0)

        @pl.when(self.inner)
        def _():
            self.to_end().start()

        @pl.when(jnp.logical_not(self.inner))
        def _():
            self.from_end().start()

    def merge_third(self):
        @pl.when(self.inner)
        def _():
            self.from_end().wait_recv()

            def body(i, carry):
                self.merged[0, i] = plus(self.layer[3 - self.z, i], self.three[1, i])
                self.merged[1, i] = plus(self.layer[6 - 3 * self.z, i], self.three[4 - 2 * self.z, i])
                return carry

            lax.fori_loop(0, 2, body, 0)
            self.across_inner().start()
            self.across_end().start()

    def own(self):
        return pltpu.make_async_copy(self.done, self.out(self.core, self.y), self.signals(15))

    def to_y(self):
        return self.remote(self.done, self.out(self.core, self.y), 16, 17, self.peers["y"])

    def to_core(self):
        return self.remote(self.done, self.out(self.core, self.y), 18, 19, self.peers["core"])

    def passed(self):
        place = self.out(self.core, 1 - self.y)
        return self.remote(place, place, 20, 21, self.peers["core"])

    def finish(self):
        self.across_inner().wait_recv()

        @pl.when(self.inner)
        def _():
            def body(i, carry):
                total = self.layer[self.z, i].astype(jnp.float32) + self.far[i].astype(jnp.float32)
                total = total + self.three[2 * self.z - 2, i].astype(jnp.float32)
                self.done[i] = total.astype(jnp.bfloat16)
                return carry

            lax.fori_loop(0, 2, body, 0)

        @pl.when(jnp.logical_not(self.inner))
        def _():
            self.to_end().wait_recv()

            def body(i, carry):
                total = self.layer[self.z, i].astype(jnp.float32) + self.far[i].astype(jnp.float32)
                total = total + self.near[i].astype(jnp.float32)
                self.done[i] = total.astype(jnp.bfloat16)
                return carry

            lax.fori_loop(0, 2, body, 0)

        self.own().start()
        self.to_y().start()
        self.to_core().start()

    def hand_on(self):
        self.to_y().wait_recv()
        self.passed().start()

    def drain(self):
        for copy in self.seconds():
            copy.wait_send()

        @pl.when(self.inner)
        def _():
            self.to_end().wait_send()
            self.across_inner().wait_send()
            self.across_end().wait_send()

        @pl.when(jnp.logical_not(self.inner))
        def _():
            self.from_end().wait_send()

        self.own().wait()
        self.to_y().wait_send()
        self.to_core().wait()
        self.passed().wait()


def reduce_kernel(chunks, keep_ref, came_a, came_b, weight_ref, out_ref, weight_out, *scratch):
    rows, weights, signals = scratch[:12], scratch[12:24], scratch[24]
    dp = lax.axis_index("dp")
    store = lax.axis_index("store")
    y, core = lax.div(dp, 2), lax.rem(dp, 2)
    z, x = lax.div(store, 2), lax.rem(store, 2)
    inner = (z == 1) | (z == 2)
    beside = z + 1 - 2 * lax.rem(z, 2)
    along = lambda to: (dp, to * 2 + x)
    peers = {
        "x": (dp, z * 2 + (1 - x)),
        "y": ((1 - y) * 2 + core, store),
        "core": (y * 2 + (1 - core), store),
        "beside": along(beside),
        "end_z": 3 * lax.div(z, 2),
        "other_inner": along(3 - z),
        "far_end": along(3 - 3 * lax.div(z, 2)),
    }
    place = (x, y, z, core, inner, peers)

    barrier = pltpu.get_barrier_semaphore()
    for peer in (peers["x"], peers["y"], peers["core"]) + tuple(along(lax.rem(z + hop, 4)) for hop in (1, 2, 3)):
        pl.semaphore_signal(barrier, inc=1, device_id=peer, device_id_type=MESH_ID)
    pl.semaphore_wait(barrier, 6)

    units = [
        Unit(
            place, lambda kind, q=q: signals.at[kind, q], [ref.at[q] for ref in rows],
            lambda c, h, q=q: out_ref.at[c, h, :, q],
        )
        for q in range(chunks)
    ]
    extra = Unit(
        place, lambda kind: signals.at[kind, chunks], weights, lambda c, h: weight_out.at[c, h]
    )
    extra_first = extra.firsts(weight_ref.at[:, 1 - x, :, 0], weight_ref.at[:, :, 1 - y, 1])
    extra_loads = extra.loads((weight_ref.at[:, x, :, 0], weight_ref.at[:, :, y, 1]))
    loads = [
        unit.loads((keep_ref.at[0, :, :, q], keep_ref.at[1, :, :, q], came_a.at[:, :, q], came_b.at[:, :, q]))
        for q, unit in enumerate(units)
    ]
    for some in loads + [extra_loads]:
        for copy in some:
            copy.start()
    stages = ("merge_second", "merge_third", "finish", "hand_on")
    for step in range(chunks + LAG * len(stages) + 1):
        if step < chunks:
            for copy in loads[step]:
                copy.wait()
            units[step].merge_first()
        for stage, name in enumerate(stages, 1):
            if 0 <= step - LAG * stage < chunks:
                getattr(units[step - LAG * stage], name)()
            if step == chunks + LAG * stage:
                getattr(extra, name)()
        if step == 3:
            for copy in extra_first:
                copy.start()
        if step == chunks:
            for copy in extra_loads:
                copy.wait()
            for copy in extra_first:
                copy.wait_recv()
            extra.merge_first()
    for copy in extra_first:
        copy.wait_send()
    for unit in units + [extra]:
        unit.drain()


def reduce_rows(keep, came_a, came_b, weights, collective_id=0):
    rows = keep.shape[0] // 4
    chunks = rows // (4 * CHUNK)
    high = weights.shape[0] // 32

    def spare(high, *lead):
        return [
            pltpu.VMEM(lead + part + (high, D), jnp.bfloat16)
            for part in ((4, 2),) * 4 + ((4,), (4,), (4, 2), (3, 2), (2, 2), (2,), (2,), (2,))
        ]

    out, weights = pl.pallas_call(
        functools.partial(reduce_kernel, chunks),
        out_shape=[
            jax.ShapeDtypeStruct((2, 2, 2, chunks, CHUNK, D), jnp.bfloat16),
            jax.ShapeDtypeStruct((2, 2, 2, high, D), jnp.bfloat16),
        ],
        in_specs=[pl.BlockSpec(memory_space=pl.ANY)] * 4,
        out_specs=[pl.BlockSpec(memory_space=pl.ANY)] * 2,
        scratch_shapes=spare(CHUNK, chunks) + spare(high) + [pltpu.SemaphoreType.DMA((SIGNALS, chunks + 1))],
        compiler_params=pltpu.CompilerParams(
            collective_id=collective_id, has_side_effects=True, vmem_limit_bytes=VMEM_LIMIT
        ),
        cost_estimate=pl.CostEstimate(flops=0, transcendentals=0, bytes_accessed=450_000_000),
        name="reduce_rows",
    )(
        keep.reshape(2, 4, 2, chunks, CHUNK, D),
        came_a.reshape(4, 2, chunks, CHUNK, D),
        came_b.reshape(4, 2, chunks, CHUNK, D),
        weights.reshape(4, 2, 2, 2, high, D),
    )
    return out.reshape(2 * rows, D), weights.reshape(8 * high, D)


PAIRS = ((0, 1), (1, 0), (2, 3), (3, 2))


def own_rows(flat, rows_here):
    half = rows_here // 2
    quarter = half // 4
    dp = lax.axis_index("dp")
    here_y, core = dp // 2, dp % 2
    here_x = lax.axis_index("store") % 2
    owner, local = flat // rows_here, flat % rows_here
    z, x = owner // 2, owner % 2
    y = (local % half) // (2 * quarter)
    second = (local // quarter) % 2
    stays = jnp.where(second == 0, x == here_x, y == here_y)
    pair = jnp.where(second == 0, y, x)
    rows = 8 * half
    target = (2 * stays + second) * (rows // 4) + (2 * z + pair) * quarter + local % quarter
    return jnp.where(local // half == core, target, rows)


def plan_store(indices, rows_here):
    flat = indices.reshape(-1)
    other = lax.ppermute(flat, "dp", PAIRS)
    where = jnp.concatenate([own_rows(flat, rows_here), own_rows(other, rows_here)])
    return scatter_plan(where, lax.axis_size("store") * rows_here // 2)


def add_store(plan, own, other, rows_here):
    return scatter_rows(plan, own, other, lax.axis_size("store") * rows_here // 2)


def swap_store(send_a, send_b):
    owners = lax.axis_size("store")
    came_a = lax.ppermute(send_a, "store", [(i, i ^ 1) for i in range(owners)])
    came_b = lax.ppermute(send_b, "dp", [(i, i ^ 2) for i in range(4)])
    return came_a, came_b


def by_owner(matrix):
    owners = lax.axis_size("store")
    return matrix.astype(jnp.bfloat16).reshape(owners, -1, D)


def reduce_packed(packed):
    return lax.psum_scatter(
        packed.reshape(-1, D), ("store", "dp"), scatter_dimension=0, tiled=True
    )


def all_copies(share):
    return lax.all_gather(share, "dp", axis=0, tiled=True).astype(jnp.float32)


def pack_early(inner, outer, squares):
    blocks = [inner[:, block * D : (block + 1) * D] for block in range(inner.shape[1] // D)]
    return jnp.concatenate([by_owner(piece) for piece in blocks + [outer] + list(squares)], axis=1)


def unpack_early(total, wide):
    part = D // lax.axis_size("store")
    inner_total = jnp.transpose(total[: wide * part].reshape(wide, part, D), (1, 0, 2))
    rest = total[wide * part :]
    return (
        inner_total.reshape(part, wide * D),
        rest[: wide * part],
        rest[wide * part :].reshape(-1, part, D),
    )


def pack_late(squares, features, inner_bias):
    owners = lax.axis_size("store")
    part = D // owners
    wide = inner_bias.shape[0] // D
    small = jnp.concatenate(
        [feature.astype(jnp.bfloat16).reshape(owners, part) for feature in features]
        + [inner_bias.astype(jnp.bfloat16).reshape(owners, wide * part)],
        axis=1,
    )
    small = jnp.pad(small, ((0, 0), (0, part * D - small.shape[1]))).reshape(owners, part, D)
    return jnp.concatenate([by_owner(square) for square in squares] + [small], axis=1)


def add_cores(packed):
    core = lax.axis_index("dp") % 2
    halves = packed.reshape(packed.shape[0], 2, -1, D)
    mine = lax.dynamic_index_in_dim(halves, core, axis=1, keepdims=False)
    other = lax.dynamic_index_in_dim(halves, 1 - core, axis=1, keepdims=False)
    other = lax.ppermute(other, "dp", PAIRS)
    return plus(mine, other).reshape(-1, D)


def unpack_late(total, count, features, wide):
    part = D // lax.axis_size("store")
    tail = total[count * part :].reshape(-1)
    table = tail[: features * part].reshape(features, part)
    return (
        total[: count * part].reshape(count, part, D),
        table,
        tail[features * part :][: wide * part],
    )


def cross_probs_of(folded, rows):
    scores = lax.dot_general(folded, rows, (((1,), (1,)), ((), ())), preferred_element_type=jnp.float32)
    token = lax.broadcasted_iota(jnp.int32, scores.shape, 0) % CROSS_TOKENS
    owner = lax.broadcasted_iota(jnp.int32, scores.shape, 1) // K
    scores = jnp.where(token == owner, scores, -1e30)
    raised = jnp.exp(scores - jnp.max(scores, axis=1, keepdims=True))
    return raised * (1.0 / jnp.sum(raised, axis=1, keepdims=True))


def cross_tiles(ref):
    tokens = ref.shape[1]
    for first in range(0, tokens, CROSS_TOKENS):
        yield pl.ds(first, CROSS_TOKENS), pl.ds(first * K, CROSS_TOKENS * K)


def cross_forward_kernel(folded_ref, rows_ref, summary_ref):
    for some, slots in cross_tiles(folded_ref):
        rows = rows_ref[slots, :]
        probs = cross_probs_of(folded_ref[:, some, :].reshape(H * CROSS_TOKENS, D), rows)
        summary = jnp.dot(probs.astype(jnp.bfloat16), rows, preferred_element_type=jnp.float32)
        summary_ref[:, some, :] = summary.astype(jnp.bfloat16).reshape(H, CROSS_TOKENS, D)


def cross_backward_kernel(folded_ref, grad_ref, rows_ref, row_grad_ref, folded_grad_ref):
    for some, slots in cross_tiles(folded_ref):
        rows = rows_ref[slots, :]
        folded = folded_ref[:, some, :].reshape(H * CROSS_TOKENS, D)
        grad = grad_ref[:, some, :].reshape(H * CROSS_TOKENS, D)
        probs = cross_probs_of(folded, rows)
        prob_grad = lax.dot_general(
            grad, rows, (((1,), (1,)), ((), ())), preferred_element_type=jnp.float32
        )
        total = jnp.sum(probs * prob_grad, axis=1, keepdims=True)
        score_low = (probs * (prob_grad - total)).astype(jnp.bfloat16)
        turned = (((0,), (0,)), ((), ()))
        row_grad = lax.dot_general(
            probs.astype(jnp.bfloat16), grad, turned, preferred_element_type=jnp.float32
        )
        row_grad += lax.dot_general(score_low, folded, turned, preferred_element_type=jnp.float32)
        row_grad_ref[slots, :] = row_grad.astype(jnp.bfloat16)
        folded_grad = jnp.dot(score_low, rows, preferred_element_type=jnp.float32)
        folded_grad_ref[:, some, :] = folded_grad.astype(jnp.bfloat16).reshape(H, CROSS_TOKENS, D)


CROSS_TOKENS = 16
CROSS_STEP = 64


def cross_specs():
    heads = pl.BlockSpec((H, CROSS_STEP, D), lambda i: (0, i, 0))
    rows = pl.BlockSpec((CROSS_STEP * K, D), lambda i: (i, 0))
    return heads, rows


def cross_forward(folded, fetched):
    heads, rows = cross_specs()
    tokens = folded.shape[1]
    return pl.pallas_call(
        cross_forward_kernel,
        out_shape=jax.ShapeDtypeStruct((H, tokens, D), jnp.bfloat16),
        grid=(tokens // CROSS_STEP,),
        in_specs=[heads, rows],
        out_specs=heads,
        cost_estimate=pl.CostEstimate(flops=0, transcendentals=0, bytes_accessed=55_000_000),
        name="cross_forward",
    )(folded, fetched)


def cross_backward(folded, grad, fetched):
    heads, rows = cross_specs()
    tokens = folded.shape[1]
    return pl.pallas_call(
        cross_backward_kernel,
        out_shape=[
            jax.ShapeDtypeStruct((tokens * K, D), jnp.bfloat16),
            jax.ShapeDtypeStruct((H, tokens, D), jnp.bfloat16),
        ],
        grid=(tokens // CROSS_STEP,),
        in_specs=[heads, heads, rows],
        out_specs=[rows, heads],
        cost_estimate=pl.CostEstimate(flops=0, transcendentals=0, bytes_accessed=100_000_000),
        name="cross_backward",
    )(folded, grad, fetched)


def body(
    tokens,
    datastore,
    indices,
    lengths,
    proj_weight,
    out_weight,
    proj_bias,
    norm_gain,
    norm_bias,
    inner_weight,
    inner_bias,
    outer_weight,
    outer_bias,
    cotangent,
):
    seq_len = tokens.shape[0]
    score_scale = HD ** (-0.5)
    owners = lax.axis_size("store")
    rows_here = datastore.shape[0]
    capacity = 2 * seq_len * K // owners
    position = jnp.arange(seq_len)
    length = lengths[0]
    allowed = (position[None, :] <= position[:, None]) & (position[None, :] < length)
    valid = (position < length)[:, None]
    dense = is_dense(owners, rows_here)
    if dense:
        plan = plan_store(indices, rows_here)
        fetched, plan = fetch_dense(datastore, indices, plan)
    else:
        target, request = route_slots(indices, rows_here, owners, capacity)
        returned, _ = fetch_rows(request, datastore)
        fetched = returned.reshape(owners * capacity, D)[target].reshape(seq_len, K, D)
    self_bias = jnp.concatenate([proj_bias[:, 0], jnp.zeros((D,), jnp.float32), proj_bias[:, 1]])
    self_proj = proj_weight[:, 0:3, :].reshape(D, 3 * D)
    joined = (product(tokens, self_proj) + self_bias).astype(jnp.bfloat16)
    queries = joined[:, :D].reshape(seq_len, H, HD)
    self_keys = joined[:, D : 2 * D].reshape(seq_len, H, HD)
    values = joined[:, 2 * D :].reshape(seq_len, H, HD)
    scores = self_scores(queries, self_keys, allowed, score_scale)
    self_lse = log_total(scores)
    self_probs = jnp.exp(scores - self_lse).astype(jnp.bfloat16)
    self_mixed = (
        jnp.einsum("hqk,khe->qhe", self_probs, values, preferred_element_type=jnp.float32)
        .reshape(seq_len, D)
        .astype(jnp.bfloat16)
    )
    first_pre = tokens.astype(jnp.float32) + (
        product(self_mixed, out_weight[:, 0, :]) + proj_bias[:, 2]
    )
    first_out, first_normed, first_inverse = norm_forward(
        first_pre, norm_gain[:, 0], norm_bias[:, 0]
    )
    first_low = first_out.astype(jnp.bfloat16)
    cross_query = (
        (product(first_low, proj_weight[:, 3, :]) + proj_bias[:, 3])
        .astype(jnp.bfloat16)
        .reshape(seq_len, H, HD)
    )
    key_heads = proj_weight[:, 4, :].reshape(D, H, HD)
    folded = (
        jnp.einsum("the,dhe->thd", cross_query, key_heads, preferred_element_type=jnp.float32)
        * score_scale
    ).astype(jnp.bfloat16)
    if dense:
        folded_heads = jnp.transpose(folded, (1, 0, 2))
        summary = jnp.transpose(cross_forward(folded_heads, fetched), (1, 0, 2))
    else:
        cross_scores = jnp.einsum("thd,tkd->thk", folded, fetched, preferred_element_type=jnp.float32)
        cross_lse = log_total(cross_scores)
        cross_full = jnp.exp(cross_scores - cross_lse)
        cross_probs = cross_full.astype(jnp.bfloat16)
        summary = jnp.einsum(
            "thk,tkd->thd", cross_probs, fetched, preferred_element_type=jnp.float32
        ).astype(jnp.bfloat16)
    value_heads = proj_weight[:, 5, :].reshape(D, H, HD)
    cross_mixed = (
        jnp.einsum(
            "thd,dhe->the", summary, value_heads, preferred_element_type=jnp.float32
        ).reshape(seq_len, D)
        + proj_bias[:, 4]
    ).astype(jnp.bfloat16)
    second_pre = first_out + (product(cross_mixed, out_weight[:, 1, :]) + proj_bias[:, 5])
    second_out, second_normed, second_inverse = norm_forward(
        second_pre, norm_gain[:, 1], norm_bias[:, 1]
    )
    second_low = second_out.astype(jnp.bfloat16)
    inner_pre = product(second_low, inner_weight) + inner_bias
    activated = jax.nn.gelu(inner_pre, approximate=False).astype(jnp.bfloat16)
    third_pre = second_out + (product(activated, outer_weight) + outer_bias)
    third_out, third_normed, third_inverse = norm_forward(
        third_pre, norm_gain[:, 2], norm_bias[:, 2]
    )
    output = jnp.where(valid, third_out, 0.0).astype(jnp.bfloat16)
    upstream = jnp.where(valid, cotangent.astype(jnp.float32), 0.0)
    third_grad, gain_three, shift_three = norm_backward(
        upstream, third_normed, third_inverse, norm_gain[:, 2]
    )
    outer_low = third_grad.astype(jnp.bfloat16)
    grad_outer_weight = contract_rows(activated, outer_low)
    grad_outer_bias = column_sum(outer_low)
    act_grad = product_back(outer_low, outer_weight)
    slope = jax.vjp(lambda activation_in: jax.nn.gelu(activation_in, approximate=False), inner_pre)[
        1
    ](act_grad)[0]
    inner_low = slope.astype(jnp.bfloat16)
    grad_inner_weight = contract_rows(second_low, inner_low)
    grad_inner_bias = column_sum(inner_low)
    second_up = third_grad + product_back(inner_low, inner_weight)
    second_grad, gain_two, shift_two = norm_backward(
        second_up, second_normed, second_inverse, norm_gain[:, 1]
    )
    cross_out_low = second_grad.astype(jnp.bfloat16)
    grad_cross_out = contract_rows(cross_mixed, cross_out_low)
    bias_five = column_sum(cross_out_low)
    mixed_low = product_back(cross_out_low, out_weight[:, 1, :]).astype(jnp.bfloat16)
    bias_four = column_sum(mixed_low)
    mixed_heads = mixed_low.reshape(seq_len, H, HD)
    grad_value_heads = jnp.einsum(
        "thd,the->dhe", summary, mixed_heads, preferred_element_type=jnp.float32
    )
    if dense:
        packed_early = pack_early(grad_inner_weight, grad_outer_weight, (grad_cross_out,))
        mixed_heads, packed_early = lax.optimization_barrier((mixed_heads, packed_early))
        share_early = reduce_packed(packed_early)
    summary_low = jnp.einsum(
        "the,dhe->thd", mixed_heads, value_heads, preferred_element_type=jnp.float32
    ).astype(jnp.bfloat16)
    if dense:
        own_grad, folded_low = cross_backward(
            folded_heads, jnp.transpose(summary_low, (1, 0, 2)), fetched
        )
        folded_low = jnp.transpose(folded_low, (1, 0, 2))
        other_grad = lax.ppermute(own_grad, "dp", PAIRS)
    else:
        returned_again, asked_back = fetch_again(request, datastore)
        fetched_back = returned_again.reshape(owners * capacity, D)[target].reshape(seq_len, K, D)
        prob_grad = jnp.einsum(
            "thd,tkd->thk", summary_low, fetched_back, preferred_element_type=jnp.float32
        )
        score_low = (
            cross_full * (prob_grad - jnp.sum(cross_full * prob_grad, axis=-1, keepdims=True))
        ).astype(jnp.bfloat16)
        row_grad = (
            jnp.einsum("thk,thd->tkd", cross_probs, summary_low, preferred_element_type=jnp.float32)
            + jnp.einsum("thk,thd->tkd", score_low, folded, preferred_element_type=jnp.float32)
        ).astype(jnp.bfloat16)
        folded_low = jnp.einsum(
            "thk,tkd->thd", score_low, fetched_back, preferred_element_type=jnp.float32
        ).astype(jnp.bfloat16)
    grad_key_heads = (
        jnp.einsum("thd,the->dhe", folded_low, cross_query, preferred_element_type=jnp.float32)
        * score_scale
    )
    query_low = (
        (
            jnp.einsum("thd,dhe->the", folded_low, key_heads, preferred_element_type=jnp.float32)
            * score_scale
        )
        .astype(jnp.bfloat16)
        .reshape(seq_len, D)
    )
    if dense:
        query_low, other_grad = lax.optimization_barrier((query_low, other_grad))
        send_a, send_b, keep = add_store(plan, own_grad, other_grad, rows_here)
        query_low, mixed_heads, send_a, send_b, keep = lax.optimization_barrier(
            (query_low, mixed_heads, send_a, send_b, keep)
        )
        grad_value_heads = jnp.einsum(
            "thd,the->dhe", summary, mixed_heads, preferred_element_type=jnp.float32
        )
        came_a, came_b = swap_store(send_a, send_b)
    bias_three = column_sum(query_low)
    grad_cross_query = contract_rows(first_low, query_low)
    if not dense:
        grad_buffer = (
            jnp.zeros((owners * capacity, D), jnp.bfloat16)
            .at[target]
            .set(row_grad.reshape(-1, D))
            .reshape(owners, capacity, D)
        )
        arrived = lax.all_to_all(grad_buffer, "store", split_axis=0, concat_axis=0, tiled=True)
        partial_store = (
            jnp.zeros((rows_here, D), jnp.float32)
            .at[asked_back.reshape(-1)]
            .add(arrived.reshape(-1, D).astype(jnp.float32))
        )
        grad_store = lax.psum(partial_store.astype(jnp.bfloat16), "dp").astype(jnp.float32)
    first_up = second_grad + product_back(query_low, proj_weight[:, 3, :])
    first_grad, gain_one, shift_one = norm_backward(
        first_up, first_normed, first_inverse, norm_gain[:, 0]
    )
    self_out_low = first_grad.astype(jnp.bfloat16)
    grad_self_out = contract_rows(self_mixed, self_out_low)
    bias_two = column_sum(self_out_low)
    self_mixed_low = (
        product_back(self_out_low, out_weight[:, 0, :]).astype(jnp.bfloat16).reshape(seq_len, H, HD)
    )
    value_grad = jnp.einsum(
        "hqk,qhe->khe", self_probs, self_mixed_low, preferred_element_type=jnp.float32
    )
    attend_grad = jnp.einsum(
        "qhe,khe->hqk", self_mixed_low, values, preferred_element_type=jnp.float32
    )
    self_full = jnp.exp(self_scores(queries, self_keys, allowed, score_scale) - self_lse)
    self_score_low = (
        self_full * (attend_grad - jnp.sum(self_full * attend_grad, axis=-1, keepdims=True))
    ).astype(jnp.bfloat16)
    query_grad = (
        jnp.einsum("hqk,khe->qhe", self_score_low, self_keys, preferred_element_type=jnp.float32)
        * score_scale
    )
    key_grad = (
        jnp.einsum("hqk,qhe->khe", self_score_low, queries, preferred_element_type=jnp.float32)
        * score_scale
    )
    joined_low = jnp.concatenate(
        [
            query_grad.reshape(seq_len, D),
            key_grad.reshape(seq_len, D),
            value_grad.reshape(seq_len, D),
        ],
        axis=1,
    ).astype(jnp.bfloat16)
    grad_self_proj = contract_rows(tokens, joined_low).reshape(D, 3, D)
    bias_zero = column_sum(joined_low[:, :D])
    bias_one = column_sum(joined_low[:, 2 * D :])
    grad_tokens = (first_grad + product_back(joined_low, self_proj)).astype(jnp.bfloat16)
    if dense:
        packed_late = pack_late(
            (
                grad_self_proj[:, 0],
                grad_self_proj[:, 1],
                grad_self_proj[:, 2],
                grad_cross_query,
                grad_key_heads.reshape(D, D),
                grad_value_heads.reshape(D, D),
                grad_self_out,
            ),
            (bias_zero, bias_one, bias_two, bias_three, bias_four, bias_five)
            + (gain_one, gain_two, gain_three)
            + (shift_one, shift_two, shift_three)
            + (grad_outer_bias,),
            grad_inner_bias,
        )
        wide = grad_inner_bias.shape[0] // D
        early_totals = unpack_early(all_copies(share_early), wide)
        keep, came_a, came_b, output, grad_tokens, early_totals = lax.optimization_barrier(
            (keep, came_a, came_b, output, grad_tokens, early_totals)
        )
        inner_total, outer_total, early = early_totals
        grad_store, total_late = reduce_rows(keep, came_a, came_b, add_cores(packed_late))
        grad_store = grad_store.astype(jnp.float32)
        late, table, bias_inner = unpack_late(total_late.astype(jnp.float32), 7, 13, wide)
        return (
            output,
            grad_tokens,
            grad_store,
            jnp.stack([late[0], late[1], late[2], late[3], late[4], late[5]], axis=1),
            jnp.stack([late[6], early[0]], axis=1),
            jnp.transpose(table[0:6]),
            jnp.transpose(table[6:9]),
            jnp.transpose(table[9:12]),
            inner_total,
            bias_inner,
            outer_total,
            table[12],
        )
    grad_proj = jnp.stack(
        [
            grad_self_proj[:, 0],
            grad_self_proj[:, 1],
            grad_self_proj[:, 2],
            grad_cross_query,
            grad_key_heads.reshape(D, D),
            grad_value_heads.reshape(D, D),
        ],
        axis=1,
    )
    grad_out = jnp.stack([grad_self_out, grad_cross_out], axis=1)
    grad_bias = jnp.stack([bias_zero, bias_one, bias_two, bias_three, bias_four, bias_five], axis=1)
    grad_gain = jnp.stack([gain_one, gain_two, gain_three], axis=1)
    grad_shift = jnp.stack([shift_one, shift_two, shift_three], axis=1)
    shares = (
        lax.psum_scatter(
            grad_proj.astype(jnp.bfloat16), "store", scatter_dimension=0, tiled=True
        ).astype(jnp.float32),
        lax.psum_scatter(
            grad_out.astype(jnp.bfloat16), "store", scatter_dimension=0, tiled=True
        ).astype(jnp.float32),
        lax.psum_scatter(
            grad_bias.astype(jnp.bfloat16), "store", scatter_dimension=0, tiled=True
        ).astype(jnp.float32),
        lax.psum_scatter(
            grad_gain.astype(jnp.bfloat16), "store", scatter_dimension=0, tiled=True
        ).astype(jnp.float32),
        lax.psum_scatter(
            grad_shift.astype(jnp.bfloat16), "store", scatter_dimension=0, tiled=True
        ).astype(jnp.float32),
        lax.psum_scatter(
            grad_inner_weight.astype(jnp.bfloat16), "store", scatter_dimension=0, tiled=True
        ).astype(jnp.float32),
        lax.psum_scatter(
            grad_inner_bias.astype(jnp.bfloat16), "store", scatter_dimension=0, tiled=True
        ).astype(jnp.float32),
        lax.psum_scatter(
            grad_outer_weight.astype(jnp.bfloat16), "store", scatter_dimension=0, tiled=True
        ).astype(jnp.float32),
        lax.psum_scatter(
            grad_outer_bias.astype(jnp.bfloat16), "store", scatter_dimension=0, tiled=True
        ).astype(jnp.float32),
    )
    totals = (
        lax.psum(shares[0].astype(jnp.bfloat16), "dp").astype(jnp.float32),
        lax.psum(shares[1].astype(jnp.bfloat16), "dp").astype(jnp.float32),
        lax.psum(shares[2].astype(jnp.bfloat16), "dp").astype(jnp.float32),
        lax.psum(shares[3].astype(jnp.bfloat16), "dp").astype(jnp.float32),
        lax.psum(shares[4].astype(jnp.bfloat16), "dp").astype(jnp.float32),
        lax.psum(shares[5].astype(jnp.bfloat16), "dp").astype(jnp.float32),
        lax.psum(shares[6].astype(jnp.bfloat16), "dp").astype(jnp.float32),
        lax.psum(shares[7].astype(jnp.bfloat16), "dp").astype(jnp.float32),
        lax.psum(shares[8].astype(jnp.bfloat16), "dp").astype(jnp.float32),
    )
    return (
        output,
        grad_tokens,
        grad_store,
        totals[0],
        totals[1],
        totals[2],
        totals[3],
        totals[4],
        totals[5],
        totals[6],
        totals[7],
        totals[8],
    )


def solution(mesh):
    in_specs = (
        P(("dp", "store"), None),
        P("store", None),
        P(("dp", "store"), None),
        P(("dp", "store")),
        P(),
        P(),
        P(),
        P(),
        P(),
        P(),
        P(),
        P(),
        P(),
        P(("dp", "store"), None),
    )
    out_specs = (
        P(("dp", "store"), None),
        P(("dp", "store"), None),
        P("store", None),
        P("store", None, None),
        P("store", None, None),
        P("store", None),
        P("store", None),
        P("store", None),
        P("store", None),
        P("store"),
        P("store", None),
        P("store"),
    )

    return jax.shard_map(body, mesh=mesh, in_specs=in_specs, out_specs=out_specs, check_vma=False)
```
